32 devices in a mesh: dp: 4 (over x, core), fsdp: 8 (over z, y).
Axes of the slice: x: 2, y: 2, z: 4, core: 2. Of those that a mesh axis runs over, the one named last changes fastest.
Arguments:
- tokens: bfloat16 [32, 512, 768], P(('dp', 'fsdp')), may hold values from -6 to 6
- out_grad: bfloat16 [32, 512, 768], P(('dp', 'fsdp')), may hold values from -6 to 6
- segment_ids: int32 [32, 512], P(('dp', 'fsdp')), may hold values from 0 to 3, never falling along the last dimension, each value on 1 to 256 neighbouring positions
- labels: int32 [32], P(('dp', 'fsdp')), may hold values from 0 to 2
- query_weight: bfloat16 [768, 768], P('fsdp'), may hold values from -0.3125 to 0.3125
- query_bias: bfloat16 [768], P('fsdp'), may hold values from -3 to 3
- key_weight: bfloat16 [768, 768], P('fsdp'), may hold values from -0.21875 to 0.21875
- value_weight: bfloat16 [768, 768], P('fsdp'), may hold values from -0.21875 to 0.21875
- value_bias: bfloat16 [768], P('fsdp'), may hold values from -3 to 3
- output_weight: bfloat16 [768, 768], P('fsdp'), may hold values from -0.625 to 0.625
- output_bias: bfloat16 [768], P('fsdp'), may hold values from -3 to 3
- first_norm_gain: bfloat16 [768], P('fsdp'), may hold values from 0.5 to 1.5
- first_norm_shift: bfloat16 [768], P('fsdp'), may hold values from -3 to 3
- inner_weight: bfloat16 [768, 3072], P('fsdp'), may hold values from -0.21875 to 0.21875
- inner_bias: bfloat16 [3072], P('fsdp'), may hold values from -3 to 3
- outer_weight: bfloat16 [3072, 768], P('fsdp'), may hold values from -0.109375 to 0.109375
- outer_bias: bfloat16 [768], P('fsdp'), may hold values from -3 to 3
- second_norm_gain: bfloat16 [768], P('fsdp'), may hold values from 0.5 to 1.5
- second_norm_shift: bfloat16 [768], P('fsdp'), may hold values from -3 to 3
- pooler_weight: bfloat16 [768, 768], P('fsdp'), may hold values from -0.21875 to 0.21875
- pooler_bias: bfloat16 [768], P('fsdp'), may hold values from -3 to 3
- class_weight: bfloat16 [768, 3], P('fsdp'), may hold values from -0.625 to 0.625
- class_bias: bfloat16 [3], replicated, may hold values from -1 to 1
Outputs:
- hidden_state: bfloat16 [32, 512, 768], P(('dp', 'fsdp'))
- tokens_grad: float32 [32, 512, 768], P(('dp', 'fsdp'))
- ramp_loss: float32 [32], P(('dp', 'fsdp'))
- query_weight_grad: float32 [768, 768], P('fsdp')
- query_bias_grad: float32 [768], P('fsdp')
- key_weight_grad: float32 [768, 768], P('fsdp')
- value_weight_grad: float32 [768, 768], P('fsdp')
- value_bias_grad: float32 [768], P('fsdp')
- output_weight_grad: float32 [768, 768], P('fsdp')
- output_bias_grad: float32 [768], P('fsdp')
- first_norm_gain_grad: float32 [768], P('fsdp')
- first_norm_shift_grad: float32 [768], P('fsdp')
- inner_weight_grad: float32 [768, 3072], P('fsdp')
- inner_bias_grad: float32 [3072], P('fsdp')
- outer_weight_grad: float32 [3072, 768], P('fsdp')
- outer_bias_grad: float32 [768], P('fsdp')
- second_norm_gain_grad: float32 [768], P('fsdp')
- second_norm_shift_grad: float32 [768], P('fsdp')
- pooler_weight_grad: float32 [768, 768], P('fsdp')
- pooler_bias_grad: float32 [768], P('fsdp')
- class_weight_grad: float32 [768, 3], P('fsdp')
- class_bias_grad: float32 [3], replicated
The draws below stay inside these ranges and needn't reach their ends.
Inputs may be any that keep to these rules, and one draw needn't show every extreme that they name: `segment_ids`: in each row the ids start at 0 and never fall; each of the 4 ids covers 1 to 256 consecutive positions, and one covers exactly 256.
All inputs are finite; a program needn't handle non-finite values.
Results may differ from the reference program's by a relative error of at most 0.018.
Values may be sent and summed in bfloat16 or wider, within the bound.
No kernel may reach another device: no remote copies, remote signals or barrier semaphores. Data moves between devices by JAX's collectives and lax.ppermute only.
A program may use at most 192 MiB of HBM per device.

```python
import math
import jax
import jax.numpy as jnp
import numpy as np
from jax import lax

D = 768
FF = 3072
HEADS = 12
HEAD_DIM = 64
CLASSES = 3
SEQ = 512
SEGS = 4
ROWS = 32


def plant(values, stream_key, least, largest):
    place = [jax.random.randint(jax.random.fold_in(stream_key, axis), (), 0, length) for axis, length in enumerate(values.shape)]
    main_axis = values.shape.index(max(values.shape))
    beside = place[:main_axis] + [(place[main_axis] + 1) % values.shape[main_axis]] + place[main_axis + 1:]
    return values.at[tuple(place)].set(least).at[tuple(beside)].set(largest)


def with_spikes(entries, rng, source, target, parts, factor):
    owner, partner = [(jnp.arange(entries.shape[axis_at]) // (entries.shape[axis_at] // parts)).reshape([-1 if axis == axis_at else 1 for axis in range(entries.ndim)]) for axis_at in (source, target)]
    chosen = jax.random.permutation(rng, parts)[partner]
    strong = (owner == chosen) | (owner == (partner + parts // 2) % parts)
    return jnp.where(strong, factor * entries, entries)


def block_scale(key, shape, split, smallest, largest):
    def one(dim, shards_of):
        heights = jax.random.uniform(jax.random.fold_in(jax.random.fold_in(key, 6), dim), (shards_of,), jnp.float32, smallest / len(split), largest / len(split))
        return jnp.repeat(jnp.exp(heights), shape[dim] // shards_of).reshape((-1,) + (1,) * (len(shape) - dim - 1))

    loudness = one(*split[0])
    for cut in split[1:]:
        loudness = loudness * one(*cut)
    return loudness


def length_profile(count, total, bound, slope):
    portions = [(1 << 20) // math.isqrt(standing ** slope) + 1 for standing in range(2, count + 1)]
    spare, holding = total - bound - (count - 1), [1] * (count - 1)
    while spare > 0:
        free = [i for i in range(count - 1) if holding[i] < bound]
        mass, remaining = sum([portions[i] for i in free]), spare
        for i in free:
            more = min(bound - holding[i], max(1, remaining * portions[i] // mass), spare)
            holding[i] = holding[i] + more
            spare = spare - more
    return np.array([bound] + holding)


def ragged(rng, number_of, total, bound, lean):
    if number_of == 2:
        one = jax.random.randint(rng, (), max(1, total - bound), min(bound, total - 1) + 1)
        return jnp.stack([one, total - one])
    tallies = jnp.asarray(length_profile(number_of, total, bound, lean), jnp.int32)
    pairs = (number_of - 1) // 2
    giver, taker = tallies[1:1 + 2 * pairs:2], tallies[2:2 + 2 * pairs:2]
    margin = jnp.minimum(giver - 1, bound - taker)
    shifted = jax.random.randint(jax.random.fold_in(rng, 1), (pairs,), 0, 1 << 20) % (margin + 1)
    tallies = tallies.at[1:1 + 2 * pairs:2].set(giver - shifted).at[2:2 + 2 * pairs:2].set(taker + shifted)
    return tallies[jax.random.permutation(jax.random.fold_in(rng, 2), number_of)]


def scatter_about(stream_key, extent, spread, reach, pieces=(), held_as=jnp.bfloat16):
    loudness = block_scale(stream_key, extent, pieces, -0.22, 0.18) if pieces else 1.0
    drawn = jax.random.normal(stream_key, extent, jnp.float32) * spread * loudness
    return jnp.minimum(jnp.maximum(drawn, -reach), reach).astype(held_as)


def bell_draw_with(rng, extent, scale, limit, shards, heavy, dtype=jnp.bfloat16):
    array = scale * jax.random.normal(rng, extent, jnp.float32)
    if shards:
        array = array * block_scale(rng, extent, shards, -0.22, 0.18)
    return jnp.clip(with_spikes(array, jax.random.fold_in(rng, 3), *heavy), -limit, limit).astype(dtype)


def setup_inputs(seed: int = 0) -> dict:
    key_list = jax.random.split(jax.random.key(seed), 24)
    tokens = bell_draw_with(key_list[0], (ROWS, SEQ, D), 1.0, 6.0, ((0, 32),), (0, 2, 32, 2.75))
    out_grad = scatter_about(key_list[1], (ROWS, SEQ, D), 1.0, 6.0, ((0, 32),))
    segment_ids = jax.vmap(lambda own: jnp.searchsorted(jnp.cumsum(ragged(own, SEGS, SEQ, SEQ // 2, 0)), jnp.arange(SEQ), side="right"))(jax.random.split(key_list[2], ROWS)).reshape((ROWS, SEQ)).astype(jnp.int32)
    labels = plant(jax.random.randint(key_list[3], (ROWS,), 0, CLASSES), jax.random.fold_in(key_list[3], 1), 0, CLASSES - 1).astype(jnp.int32)
    query_weight = scatter_about(key_list[4], (D, D), (D // 2) ** -0.5, 0.3125, ((0, 8),))
    query_bias = scatter_about(key_list[5], (D,), 0.5, 3.0, ((0, 8),))
    key_weight = scatter_about(key_list[6], (D, D), D ** -0.5, 0.21875, ((0, 8),))
    value_weight = scatter_about(key_list[7], (D, D), D ** -0.5, 0.21875, ((0, 8),))
    value_bias = scatter_about(key_list[8], (D,), 0.5, 3.0, ((0, 8),))
    output_weight = scatter_about(key_list[9], (D, D), (D // 8) ** -0.5, 0.625, ((0, 8),))
    output_bias = scatter_about(key_list[10], (D,), 0.5, 3.0, ((0, 8),))
    first_norm_gain = jnp.clip(1.0 + 0.1 * jax.random.normal(key_list[11], (D,), jnp.float32), 0.5, 1.5).astype(jnp.bfloat16)
    first_norm_shift = scatter_about(key_list[12], (D,), 0.5, 3.0, ((0, 8),))
    inner_weight = scatter_about(key_list[13], (D, FF), D ** -0.5, 0.21875, ((0, 8),))
    inner_bias = scatter_about(key_list[14], (FF,), 0.5, 3.0, ((0, 8),))
    outer_weight = scatter_about(key_list[15], (FF, D), FF ** -0.5, 0.109375, ((0, 8),))
    outer_bias = scatter_about(key_list[16], (D,), 0.5, 3.0, ((0, 8),))
    second_norm_gain = jnp.clip(1.0 + 0.1 * jax.random.normal(key_list[17], (D,), jnp.float32), 0.5, 1.5).astype(jnp.bfloat16)
    second_norm_shift = scatter_about(key_list[18], (D,), 0.5, 3.0, ((0, 8),))
    pooler_weight = scatter_about(key_list[19], (D, D), D ** -0.5, 0.21875, ((0, 8),))
    pooler_bias = scatter_about(key_list[20], (D,), 0.5, 3.0, ((0, 8),))
    class_weight = scatter_about(key_list[21], (D, CLASSES), (D // 8) ** -0.5, 0.625, ((0, 8),))
    class_bias = jnp.clip(jax.random.uniform(key_list[22], (CLASSES,), jnp.float32, -1.0, 1.0), -1.0, 1.0).astype(jnp.bfloat16)
    return dict(tokens=tokens, out_grad=out_grad, segment_ids=segment_ids, labels=labels, query_weight=query_weight, query_bias=query_bias, key_weight=key_weight, value_weight=value_weight, value_bias=value_bias, output_weight=output_weight, output_bias=output_bias, first_norm_gain=first_norm_gain, first_norm_shift=first_norm_shift, inner_weight=inner_weight, inner_bias=inner_bias, outer_weight=outer_weight, outer_bias=outer_bias, second_norm_gain=second_norm_gain, second_norm_shift=second_norm_shift, pooler_weight=pooler_weight, pooler_bias=pooler_bias, class_weight=class_weight, class_bias=class_bias)


EPS = 1e-06
NEG = -1000000000.0

@jax.custom_vjp
def low(v):
    return lax.optimization_barrier(v.astype(jnp.bfloat16)).astype(jnp.float32)

@jax.custom_vjp
def low_back(v):
    return v

def low_keep(v):
    return (low(v), None)

def low_pass(kept, grad):
    return (grad,)

def back_keep(v):
    return (v, None)

def back_low(kept, grad):
    return (low(grad),)
low.defvjp(low_keep, low_pass)
low_back.defvjp(back_keep, back_low)

def product(left_side, right_side):
    return jnp.dot(left_side, right_side, precision=lax.Precision.HIGHEST)

def layer_norm(inputs, gain_row, shift_row):
    row_mean = lax.optimization_barrier(jnp.mean(inputs, axis=-1, keepdims=True))
    centered = inputs - row_mean
    variance = lax.optimization_barrier(jnp.mean(centered * centered, axis=-1, keepdims=True))
    return centered * lax.rsqrt(variance + EPS) * gain_row + shift_row

def attend(queries, key_block, values, segment_row):
    same_doc = segment_row[:, None] == segment_row[None, :]
    query_heads = queries.reshape(SEQ, HEADS, HEAD_DIM)
    key_heads = key_block.reshape(SEQ, HEADS, HEAD_DIM)
    value_heads = values.reshape(SEQ, HEADS, HEAD_DIM)
    scores = jnp.einsum('qhd,khd->hqk', query_heads, key_heads, precision=lax.Precision.HIGHEST) * HEAD_DIM ** (-0.5)
    scores = low_back(scores)
    scores = jnp.where(same_doc[None], scores, NEG)
    row_max = lax.optimization_barrier(jnp.max(scores, axis=-1, keepdims=True))
    exponent = jnp.exp(scores - row_max)
    weights_soft = low(exponent / lax.optimization_barrier(jnp.sum(exponent, axis=-1, keepdims=True)))
    context = jnp.einsum('hqk,khd->qhd', weights_soft, value_heads, precision=lax.Precision.HIGHEST)
    return context.reshape(SEQ, D)

def layer_forward(params, tokens_in, segment_group, onehot):
    query_matrix, query_offset, keys_matrix, value_matrix, value_offset, output_matrix, output_offset, first_gain, first_shift, inner_matrix, inner_offset, outer_matrix, outer_offset, second_gain, second_shift, pooler_matrix, pooler_offset, class_matrix, class_offset = params
    row_count = tokens_in.shape[0]
    flat_tokens = tokens_in.reshape(row_count * SEQ, D)
    queries = low_back(low(product(flat_tokens, query_matrix) + query_offset))
    key_block = low_back(low(product(flat_tokens, keys_matrix)))
    values = low_back(low(product(flat_tokens, value_matrix) + value_offset))

    def one_row(item):
        return jax.checkpoint(attend)(item[0], item[1], item[2], item[3])
    context = lax.map(one_row, (queries.reshape(row_count, SEQ, D), key_block.reshape(row_count, SEQ, D), values.reshape(row_count, SEQ, D), segment_group))
    context = low_back(low(context.reshape(row_count * SEQ, D)))
    attended = low_back(product(context, output_matrix) + output_offset)
    first_out = layer_norm(flat_tokens + attended, first_gain, first_shift)
    inner_pre = low_back(product(low(first_out), inner_matrix) + inner_offset)
    activated = low_back(low(jax.nn.gelu(inner_pre, approximate=False)))
    outer_out = low_back(product(activated, outer_matrix) + outer_offset)
    second_out = layer_norm(first_out + outer_out, second_gain, second_shift)
    hidden = second_out.reshape(row_count, SEQ, D)
    class_rows = low(hidden[:, 0, :])
    pooled_pre = low_back(product(class_rows, pooler_matrix) + pooler_offset)
    pooled = low(jnp.tanh(pooled_pre))
    logits = low_back(product(pooled, class_matrix) + class_offset)
    row_max = lax.optimization_barrier(jnp.max(logits, axis=-1, keepdims=True))
    log_total = row_max[:, 0] + jnp.log(lax.optimization_barrier(jnp.sum(jnp.exp(logits - row_max), axis=-1)))
    return (hidden, log_total - lax.optimization_barrier(jnp.sum(logits * onehot, axis=-1)))

def reference(tokens, out_grad, segment_ids, labels, query_weight, query_bias, key_weight, value_weight, value_bias, output_weight, output_bias, first_norm_gain, first_norm_shift, inner_weight, inner_bias, outer_weight, outer_bias, second_norm_gain, second_norm_shift, pooler_weight, pooler_bias, class_weight, class_bias):
    params = jax.tree.map(lambda param_array: param_array.astype(jnp.float32), (query_weight, query_bias, key_weight, value_weight, value_bias, output_weight, output_bias, first_norm_gain, first_norm_shift, inner_weight, inner_bias, outer_weight, outer_bias, second_norm_gain, second_norm_shift, pooler_weight, pooler_bias, class_weight, class_bias))
    group_rows = math.gcd(ROWS, 8)
    group_count = ROWS // group_rows

    def regroup(param_array):
        return param_array.reshape((group_count, group_rows) + param_array.shape[1:])

    def group_step(totals, item):
        token_group, grad_group, segment_group, label_group = item
        onehot = (label_group[:, None] == jnp.arange(CLASSES)[None, :]).astype(jnp.float32)

        def run_layer(param_tree, tokens_in):
            return layer_forward(param_tree, tokens_in, segment_group, onehot)
        (hidden, losses), pullback = jax.vjp(run_layer, params, token_group.astype(jnp.float32))
        param_grads, token_grads = pullback((grad_group.astype(jnp.float32), jnp.ones_like(losses)))
        return (jax.tree.map(jnp.add, totals, param_grads), (hidden.astype(jnp.bfloat16), token_grads, losses))
    zeros_tree = jax.tree.map(jnp.zeros_like, params)
    param_grads, (hidden_all, grads_all, losses_all) = lax.scan(group_step, zeros_tree, (regroup(tokens), regroup(out_grad), regroup(segment_ids), regroup(labels)))
    hidden_state = hidden_all.reshape(ROWS, SEQ, D)
    tokens_grad = grads_all.reshape(ROWS, SEQ, D)
    ramp_loss = losses_all.reshape(ROWS)
    return (hidden_state, tokens_grad, ramp_loss, param_grads[0], param_grads[1], param_grads[2], param_grads[3], param_grads[4], param_grads[5], param_grads[6], param_grads[7], param_grads[8], param_grads[9], param_grads[10], param_grads[11], param_grads[12], param_grads[13], param_grads[14], param_grads[15], param_grads[16], param_grads[17], param_grads[18])
```

```python
import functools

import jax
import jax.numpy as jnp
from jax import lax
from jax.experimental import pallas as pl
from jax.experimental.pallas import tpu as pltpu
from jax.sharding import PartitionSpec as P

HEAD_DIM = 64
CLASSES = 3
EPS = 1e-06
NEG = -1000000000.0
SCALE = HEAD_DIM**-0.5
LOW = jnp.bfloat16
F32 = jnp.float32
MESH_AXES = ("dp", "fsdp")
MIB = 1 << 20

QUERY_B, VALUE_B, OUTPUT_B, GAIN1, SHIFT1, OUTER_B, GAIN2, SHIFT2, POOLER_B, INNER_B, CLASS_W = (
    0, 1, 2, 3, 4, 5, 6, 7, 8, 9, 13,
)
TABLE = 16


def dot(a, b, dims=((1,), (0,))):
    return lax.dot_general(a, b, (dims, ((), ())), preferred_element_type=F32)


def dot_nt(a, b):
    return dot(a, b, ((1,), (1,)))


def full(shape):
    zeros = (0,) * len(shape)
    return pl.BlockSpec(shape, lambda *_: zeros)


def call(kernel, outs, in_specs, out_specs, args, *, grid=(1,), scratch=(), prefetch=0, flops=0, moved=0, trans=0, vmem=48):
    return pl.pallas_call(
        kernel,
        out_shape=outs,
        grid_spec=pltpu.PrefetchScalarGridSpec(
            num_scalar_prefetch=prefetch,
            grid=grid,
            in_specs=in_specs,
            out_specs=out_specs,
            scratch_shapes=scratch,
        ),
        compiler_params=pltpu.CompilerParams(
            dimension_semantics=("arbitrary",) * len(grid), vmem_limit_bytes=vmem * MIB
        ),
        cost_estimate=pl.CostEstimate(flops=flops, bytes_accessed=moved, transcendentals=trans),
    )(*args)


def shape(*dims, dtype=LOW):
    return jax.ShapeDtypeStruct(dims, dtype)


def lane_masks(rows):
    lanes = lax.broadcasted_iota(jnp.int32, (rows, 128), 1)
    return lanes < HEAD_DIM


def attention_kernel(tok, wq, wk, wv, table, seg_row, seg_col, q_o, k_o, v_o, ctx_o, lse_o, bias):
    step = pl.program_id(0)
    seq = tok.shape[0]

    @pl.when(step == 0)
    def _():
        bias[...] = jnp.where(seg_col[...] == seg_row[...], 0.0, NEG)

    x = tok[...]
    q = (dot(x, wq[...]) + table[QUERY_B : QUERY_B + 1, :]).astype(LOW)
    k = dot(x, wk[...]).astype(LOW)
    v = (dot(x, wv[...]) + table[VALUE_B : VALUE_B + 1, :]).astype(LOW)
    q_o[...] = q
    k_o[...] = k
    v_o[...] = v
    first = lane_masks(seq)
    zero = jnp.zeros((seq, 128), LOW)
    for pair in range(q.shape[1] // 128):
        cols = slice(pair * 128, pair * 128 + 128)
        q2, k2, v2t = q[:, cols], k[:, cols], v[:, cols].T
        parts = []
        for half in range(2):
            qm = jnp.where(first, q2, zero) if half == 0 else jnp.where(first, zero, q2)
            s = dot_nt(k2, qm) * SCALE + bias[...]
            top = jnp.max(s, axis=0, keepdims=True)
            e = jnp.exp(s - top)
            total = jnp.sum(e, axis=0, keepdims=True)
            out = dot(v2t[half * HEAD_DIM : (half + 1) * HEAD_DIM], e.astype(LOW)) / total
            parts.append(out)
            row = pair * 2 + half
            lse_o[0, row : row + 1, :] = top + jnp.log(total)
        ctx_o[:, cols] = jnp.concatenate(parts, axis=0).astype(LOW).T


def attention(tokens, wq, wk, wv, table, segments):
    seq, width = tokens.shape
    blk = 256
    steps = width // blk
    cols = pl.BlockSpec((seq, blk), lambda i: (0, i))
    wcols = pl.BlockSpec((width, blk), lambda i: (0, i))
    return call(
        attention_kernel,
        (shape(seq, width),) * 4 + (shape(steps, 8, seq, dtype=F32),),
        [full((seq, width)), wcols, wcols, wcols, pl.BlockSpec((TABLE, blk), lambda i: (0, i)), full((1, seq)), full((seq, 1))],
        (cols,) * 4 + (pl.BlockSpec((1, 8, seq), lambda i: (i, 0, 0)),),
        (tokens, wq, wk, wv, table, segments.reshape(1, seq), segments.reshape(seq, 1)),
        grid=(steps,),
        scratch=[pltpu.VMEM((seq, seq), F32)],
        flops=2 * seq * width * (3 * width + 2 * seq),
        moved=8 * seq * width + 6 * width * width,
        trans=seq * seq * width // HEAD_DIM,
    )


def rows_norm(v):
    mean = jnp.mean(v, axis=-1, keepdims=True)
    centered = v - mean
    variance = jnp.mean(centered * centered, axis=-1, keepdims=True)
    scale = lax.rsqrt(variance + EPS)
    return centered * scale, scale


def attended_kernel(ctx, wo, tok, table, n1_o, r1_o, low_o):
    v = dot(ctx[...], wo[...]) + table[OUTPUT_B : OUTPUT_B + 1, :] + tok[...].astype(F32)
    n, r = rows_norm(v)
    n1_o[...] = n
    r1_o[...] = r
    low_o[...] = (n * table[GAIN1 : GAIN1 + 1, :] + table[SHIFT1 : SHIFT1 + 1, :]).astype(LOW)


def attended(ctx, wo, tokens, table):
    seq, width = tokens.shape
    blk = 128
    rows = pl.BlockSpec((blk, width), lambda i: (i, 0))
    return call(
        attended_kernel,
        (shape(seq, width, dtype=F32), shape(seq, 1, dtype=F32), shape(seq, width)),
        [rows, full((width, width)), rows, full((TABLE, width))],
        (rows, pl.BlockSpec((blk, 1), lambda i: (i, 0)), rows),
        (ctx, wo, tokens, table),
        grid=(seq // blk,),
        flops=2 * seq * width * width,
        moved=2 * width * width + 10 * seq * width,
    )


ERFC_POLY = (
    0.2820605933666229,
    0.28293782472610474,
    0.237934872508049,
    0.22901807725429535,
    -0.10879392176866531,
    0.44148358702659607,
    -0.6950507164001465,
    0.44817423820495605,
    -0.13161660730838776,
    0.013852047733962536,
)


def gelu_parts(v):
    u = jnp.abs(v) * (0.5**0.5)
    t = 1.0 / (1.0 + 0.5 * u)
    poly = jnp.full_like(t, ERFC_POLY[-1])
    for coefficient in ERFC_POLY[-2::-1]:
        poly = poly * t + coefficient
    bell = jnp.exp(v * v * -0.5)
    tail = (0.5 * t) * poly * bell
    below = jnp.where(v < 0, tail, 1.0 - tail)
    return v * below, below + v * (bell * 0.3989422804014327)


def inner_kernel(low, wi, bi, act_o, slope_o):
    v = dot(low[...], wi[...]) + bi[...]
    act, slope = gelu_parts(v)
    act_o[...] = act.astype(LOW)
    slope_o[...] = slope.astype(LOW)


def inner(low, wi, bi):
    seq, width = low.shape
    ff = wi.shape[1]
    blk = 512
    cols = pl.BlockSpec((seq, blk), lambda i: (0, i))
    return call(
        inner_kernel,
        (shape(seq, ff), shape(seq, ff)),
        [full((seq, width)), pl.BlockSpec((width, blk), lambda i: (0, i)), pl.BlockSpec((1, blk), lambda i: (0, i))],
        (cols, cols),
        (low, wi, bi),
        grid=(ff // blk,),
        flops=2 * seq * width * ff,
        moved=2 * width * ff + 4 * seq * ff,
        trans=2 * seq * ff,
    )


def outer_kernel(labels, bias3, act, w, n1, table, out_grad, wp, hid_o, sg_o, bg_o, sums_o, head_o, loss_o, acc, n2_s, r2_s):
    step = pl.program_id(0)
    seq, width = n1.shape

    @pl.when(step == 0)
    def _():
        acc[...] = jnp.zeros_like(acc)

    acc[...] += dot(act[...], w[...])

    @pl.when(step == pl.num_programs(0) - 1)
    def _():
        def row(at):
            return table[at : at + 1, :]

        gain2, shift2 = row(GAIN2), row(SHIFT2)
        blk = 64
        for at in range(0, seq, blk):
            rows = slice(at, at + blk)
            v = acc[rows, :] + row(OUTER_B) + (n1[rows, :] * row(GAIN1) + row(SHIFT1))
            n, r = rows_norm(v)
            n2_s[rows, :] = n
            r2_s[rows, :] = r
            hid_o[rows, :] = (n * gain2 + shift2).astype(LOW)
        class_rows = hid_o[0:8, :]
        pooled_pre = dot(class_rows, wp[...])[0:1, :] + row(POOLER_B)
        bent = jnp.tanh(pooled_pre)
        pooled = bent.astype(LOW).astype(F32)
        logits = [
            jnp.sum(pooled * row(CLASS_W + j), axis=-1, keepdims=True) + bias3[j] for j in range(CLASSES)
        ]
        top = functools.reduce(jnp.maximum, logits)
        exps = [jnp.exp(v - top) for v in logits]
        total = functools.reduce(jnp.add, exps)
        label = labels[0]
        hot = [jnp.where(label == j, 1.0, 0.0) for j in range(CLASSES)]
        picked = functools.reduce(jnp.add, [a * b for a, b in zip(logits, hot)])
        loss_o[...] = jnp.broadcast_to(top + jnp.log(total) - picked, loss_o.shape)
        slopes = [(e / total - o).astype(LOW).astype(F32) for e, o in zip(exps, hot)]
        pooled_grad = functools.reduce(
            jnp.add, [g * row(CLASS_W + j) for j, g in enumerate(slopes)]
        )
        pre_grad = (pooled_grad * (1.0 - bent * bent)).astype(LOW)
        row_grad = dot_nt(jnp.broadcast_to(pre_grad, (8, width)), wp[...])[0:1, :]
        head_o[...] = jnp.zeros_like(head_o)
        lanes = lax.broadcasted_iota(jnp.int32, (1, width), 1)
        head_o[0:1, :] = class_rows[0:1, :].astype(F32)
        head_o[1:2, :] = pre_grad.astype(F32)
        head_o[2:3, :] = pooled
        head_o[3:4, :] = functools.reduce(
            jnp.add, [jnp.where(lanes == j, g, 0.0) for j, g in enumerate(slopes)]
        )
        gain_sum = jnp.zeros((1, width), F32)
        shift_sum = jnp.zeros((1, width), F32)
        bias_sum = jnp.zeros((1, width), F32)
        for at in range(0, seq, blk):
            rows = slice(at, at + blk)
            fg = out_grad[rows, :].astype(F32)
            if at == 0:
                lead = lax.broadcasted_iota(jnp.int32, (blk, width), 0) == 0
                fg = fg + jnp.where(lead, jnp.broadcast_to(row_grad, (blk, width)), 0.0)
            n = n2_s[rows, :]
            g = fg * gain2
            gm = jnp.mean(g, axis=-1, keepdims=True)
            gn = jnp.mean(g * n, axis=-1, keepdims=True)
            sg = r2_s[rows, :] * (g - gm - n * gn)
            low = sg.astype(LOW)
            sg_o[rows, :] = sg
            bg_o[rows, :] = low
            gain_sum += jnp.sum(fg * n, axis=0, keepdims=True)
            shift_sum += jnp.sum(fg, axis=0, keepdims=True)
            bias_sum += jnp.sum(low.astype(F32), axis=0, keepdims=True)
        sums_o[...] = jnp.zeros_like(sums_o)
        sums_o[0:1, :] = gain_sum
        sums_o[1:2, :] = shift_sum
        sums_o[2:3, :] = bias_sum


def outer(act, w, n1, table, out_grad, wp, labels, bias3):
    seq, width = n1.shape
    ff = act.shape[1]
    blk = 512
    whole = full((seq, width))
    return call(
        outer_kernel,
        (
            shape(seq, width),
            shape(seq, width, dtype=F32),
            shape(seq, width),
            shape(8, width, dtype=F32),
            shape(8, width, dtype=F32),
            shape(8, 128, dtype=F32),
        ),
        [
            pl.BlockSpec((seq, blk), lambda i, *_: (0, i)),
            pl.BlockSpec((blk, width), lambda i, *_: (i, 0)),
            whole,
            full((TABLE, width)),
            whole,
            full((width, width)),
        ],
        (whole, whole, whole, full((8, width)), full((8, width)), full((8, 128))),
        (labels, bias3, act, w, n1, table, out_grad, wp),
        grid=(ff // blk,),
        scratch=[pltpu.VMEM((seq, width), F32), pltpu.VMEM((seq, width), F32), pltpu.VMEM((seq, 1), F32)],
        prefetch=2,
        flops=2 * seq * width * ff,
        moved=2 * width * ff + 2 * seq * ff + 14 * seq * width,
    )


def inner_back_kernel(bg, w_out, w_in, slope, sg, n1, r1, table, ig_o, ib_o, res_o, ag_o, sums_o, acc):
    step = pl.program_id(0)
    seq, width = n1.shape
    ig = (dot_nt(bg[...], w_out[...]) * slope[...].astype(F32)).astype(LOW)
    ig_o[...] = ig
    ib_o[...] = jnp.sum(ig.astype(F32), axis=0, keepdims=True)

    @pl.when(step == 0)
    def _():
        acc[...] = jnp.zeros_like(acc)

    acc[...] += dot_nt(ig, w_in[...])

    @pl.when(step == pl.num_programs(0) - 1)
    def _():
        gain1 = table[GAIN1 : GAIN1 + 1, :]
        gain_sum = jnp.zeros((1, width), F32)
        shift_sum = jnp.zeros((1, width), F32)
        bias_sum = jnp.zeros((1, width), F32)
        blk = 64
        for at in range(0, seq, blk):
            rows = slice(at, at + blk)
            fg = sg[rows, :] + acc[rows, :]
            n = n1[rows, :]
            g = fg * gain1
            gm = jnp.mean(g, axis=-1, keepdims=True)
            gn = jnp.mean(g * n, axis=-1, keepdims=True)
            res = r1[rows, :] * (g - gm - n * gn)
            low = res.astype(LOW)
            res_o[rows, :] = res
            ag_o[rows, :] = low
            gain_sum += jnp.sum(fg * n, axis=0, keepdims=True)
            shift_sum += jnp.sum(fg, axis=0, keepdims=True)
            bias_sum += jnp.sum(low.astype(F32), axis=0, keepdims=True)
        sums_o[...] = jnp.zeros_like(sums_o)
        sums_o[0:1, :] = gain_sum
        sums_o[1:2, :] = shift_sum
        sums_o[2:3, :] = bias_sum


def inner_back(bg, w_out, w_in, slope, sg, n1, r1, table):
    seq, width = n1.shape
    ff = slope.shape[1]
    blk = 512
    whole = full((seq, width))
    cols = pl.BlockSpec((seq, blk), lambda i: (0, i))
    return call(
        inner_back_kernel,
        (
            shape(seq, ff),
            shape(1, ff, dtype=F32),
            shape(seq, width, dtype=F32),
            shape(seq, width),
            shape(8, width, dtype=F32),
        ),
        [
            whole,
            pl.BlockSpec((blk, width), lambda i: (i, 0)),
            pl.BlockSpec((width, blk), lambda i: (0, i)),
            cols,
            whole,
            whole,
            full((seq, 1)),
            full((TABLE, width)),
        ],
        (cols, pl.BlockSpec((1, blk), lambda i: (0, i)), whole, whole, full((8, width))),
        (bg, w_out, w_in, slope, sg, n1, r1, table),
        grid=(ff // blk,),
        scratch=[pltpu.VMEM((seq, width), F32)],
        flops=4 * seq * width * ff,
        moved=4 * width * ff + 4 * seq * ff + 16 * seq * width,
    )


def attention_back_kernel(q, k, v, lse, ag, wo, seg_row, seg_col, dq_o, dk_o, dv_o, sums_o, bias):
    seq = ag.shape[0]

    @pl.when(pl.program_id(0) == 0)
    def _():
        bias[...] = jnp.where(seg_col[...] == seg_row[...], 0.0, NEG)

    grad = dot_nt(ag[...], wo[...]).astype(LOW)
    first = lane_masks(seq)
    zero = jnp.zeros((seq, 128), LOW)
    sums_o[...] = jnp.zeros_like(sums_o)
    for pair in range(q.shape[1] // 128):
        cols = slice(pair * 128, pair * 128 + 128)
        q2, k2, v2, g2 = q[:, cols], k[:, cols], v[:, cols], grad[:, cols]
        k2t = k2.T
        dqs, dks, dvs = [], [], []
        for half in range(2):
            def own(a):
                return jnp.where(first, a, zero) if half == 0 else jnp.where(first, zero, a)

            row = pair * 2 + half
            s = dot_nt(k2, own(q2)) * SCALE + bias[...]
            p = jnp.exp(s - lse[0, row : row + 1, :])
            dp = dot_nt(v2, own(g2))
            weighted = p * dp
            level = jnp.sum(weighted, axis=0, keepdims=True)
            ds = (weighted - p * level).astype(LOW)
            dvs.append(dot(p.astype(LOW), g2))
            dks.append(dot(ds, q2))
            dqs.append(dot(k2t[half * HEAD_DIM : (half + 1) * HEAD_DIM], ds))
        dq = (jnp.concatenate(dqs, axis=0) * SCALE).astype(LOW).T
        dk = (jnp.where(first, dks[0], dks[1]) * SCALE).astype(LOW)
        dv = jnp.where(first, dvs[0], dvs[1]).astype(LOW)
        dq_o[:, cols] = dq
        dk_o[:, cols] = dk
        dv_o[:, cols] = dv
        sums_o[0:1, cols] = jnp.sum(dq.astype(F32), axis=0, keepdims=True)
        sums_o[1:2, cols] = jnp.sum(dv.astype(F32), axis=0, keepdims=True)


def attention_back(q, k, v, lse, ag, wo, segments):
    seq, width = ag.shape
    blk = 256
    steps = width // blk
    cols = pl.BlockSpec((seq, blk), lambda i: (0, i))
    return call(
        attention_back_kernel,
        (shape(seq, width),) * 3 + (shape(8, width, dtype=F32),),
        [
            cols,
            cols,
            cols,
            pl.BlockSpec((1, 8, seq), lambda i: (i, 0, 0)),
            full((seq, width)),
            pl.BlockSpec((blk, width), lambda i: (i, 0)),
            full((1, seq)),
            full((seq, 1)),
        ],
        (cols,) * 3 + (pl.BlockSpec((8, blk), lambda i: (0, i)),),
        (q, k, v, lse, ag, wo, segments.reshape(1, seq), segments.reshape(seq, 1)),
        grid=(steps,),
        scratch=[pltpu.VMEM((seq, seq), F32)],
        flops=2 * seq * width * (width + 5 * seq),
        moved=16 * seq * width + 2 * width * width,
        trans=seq * seq * width // HEAD_DIM,
    )


def tokens_back_kernel(res, dq, dk, dv, wq, wk, wv, out):
    out[...] = res[...] + dot_nt(dq[...], wq[...]) + dot_nt(dk[...], wk[...]) + dot_nt(dv[...], wv[...])


def tokens_back(res, dq, dk, dv, wq, wk, wv):
    seq, width = res.shape
    blk = 128
    rows = pl.BlockSpec((blk, width), lambda i: (i, 0))
    weight = full((width, width))
    return call(
        tokens_back_kernel,
        shape(seq, width, dtype=F32),
        [rows] * 4 + [weight] * 3,
        rows,
        (res, dq, dk, dv, wq, wk, wv),
        grid=(seq // blk,),
        flops=6 * seq * width * width,
        moved=14 * seq * width + 6 * width * width,
    )


def grads(where, lefts, which, rights, other, add=None):
    seq = lefts[0].shape[0]
    parts = lefts[0].shape[1] // 16
    widths = tuple((w, r.shape[1] // 2) for w, r in zip(which, rights))
    total = sum(w for _, w in widths)
    half = (lambda i, where: (0, 1 - where[3])) if other else (lambda i, where: (0, where[3]))
    right_specs = [pl.BlockSpec((seq, w), half) for _, w in widths]
    piece = (4, parts, total)
    specs = [full(a.shape) for a in lefts] + right_specs
    args = [where, *lefts, *rights]
    if add is not None:
        specs += [full(piece)] * 4
        args += list(add)

    def kernel(where_ref, *refs):
        n, m = len(lefts), len(rights)
        left_refs, right_refs = refs[:n], refs[n : n + m]
        rest = refs[n + m :]
        grad_body(where_ref, left_refs, right_refs, rest, widths, parts, add is not None)

    return call(
        kernel,
        (shape(*piece),) * 4,
        specs,
        (full(piece),) * 4,
        args,
        scratch=[pltpu.VMEM((a.shape[1], seq), LOW) for a in lefts],
        prefetch=1,
        flops=2 * seq * 16 * parts * total,
        moved=2 * 16 * parts * total + 2 * seq * 16 * parts,
    )


def grad_body(where, lefts, rights, rest, widths, parts, with_add):
    adds = rest[:4] if with_add else None
    outs = rest[4:8] if with_add else rest[:4]
    turned = rest[8:] if with_add else rest[4:]
    x, y = where[0], where[1]
    for left, store in zip(lefts, turned):
        for start in range(0, left.shape[1], 256):
            store[start : start + 256, :] = left[:, start : start + 256].T
    for place in range(4):
        hh = jnp.bitwise_xor(x, place // 2)
        yy = jnp.bitwise_xor(y, place % 2)
        column = 0
        for (which, width), right in zip(widths, rights):
            rows = [
                turned[which][pl.ds(pl.multiple_of(((z * 2 + yy) * 2 + hh) * parts, 16), parts), :]
                for z in range(4)
            ]
            got = dot(jnp.concatenate(rows, axis=0), right[...]).reshape(4, parts, width)
            cols = slice(column, column + width)
            if with_add:
                got = got + adds[place][:, :, cols].astype(F32)
            outs[place][:, :, cols] = got.astype(LOW)
            column += width


def weights_kernel(spans, where, *refs):
    pieces, outs, sem = refs[:8], refs[8:-1], refs[-1]
    copies = []
    for place in range(8):
        hh = jnp.bitwise_xor(where[0], place // 4)
        yy = jnp.bitwise_xor(where[1], place // 2 % 2)
        cc = jnp.bitwise_xor(where[3], place % 2)
        for (start, width), out in zip(spans, outs):
            to = out.at[:, yy, hh, :, pl.ds(pl.multiple_of(cc * width, 128), width)]
            copies.append(pltpu.make_async_copy(pieces[place].at[:, :, start : start + width], to, sem.at[len(copies)]))
    for copy in copies:
        copy.start()
    for copy in copies:
        copy.wait()


def place_weights(where, pieces, widths):
    parts = pieces[0].shape[1]
    spans, start = [], 0
    for width in widths:
        spans.append((start, width // 2))
        start += width // 2
    anywhere = pl.BlockSpec(memory_space=pl.ANY)
    outs = call(
        functools.partial(weights_kernel, tuple(spans)),
        tuple(shape(4, 2, 2, parts, w) for w in widths),
        [anywhere] * 8,
        (anywhere,) * len(widths),
        (where, *pieces),
        scratch=[pltpu.SemaphoreType.DMA((8 * len(widths),))],
        prefetch=1,
        moved=4 * 16 * parts * sum(widths),
        vmem=4,
    )
    return [o.reshape(16 * parts, w) for o, w in zip(outs, widths)]


def shards_kernel(spans, where, *refs):
    pieces, outs = refs[:4], refs[4:]
    for place in range(4):
        hh = jnp.bitwise_xor(where[0], place // 2)
        for core in range(2):
            @pl.when(jnp.bitwise_xor(where[3], place % 2) == core)
            def _():
                for (start, width), out in zip(spans, outs):
                    out[hh, :, core * width : (core + 1) * width] = pieces[place][
                        :, start : start + width
                    ].astype(F32)


def place_shards(where, pieces, widths):
    parts = pieces[0].shape[0]
    spans, start = [], 0
    for width in widths:
        spans.append((start, width // 2))
        start += width // 2
    outs = call(
        functools.partial(shards_kernel, tuple(spans)),
        tuple(shape(2, parts, w, dtype=F32) for w in widths),
        [full(pieces[0].shape)] * 4,
        tuple(full((2, parts, w)) for w in widths),
        (where, *pieces),
        prefetch=1,
        moved=12 * parts * sum(widths),
        vmem=16,
    )
    return [o.reshape(2 * parts, w) for o, w in zip(outs, widths)]


def device(x, core, z, y):
    return (x * 2 + core) * 8 + z * 2 + y


ALL = [(x, core, z, y) for x in range(2) for core in range(2) for z in range(4) for y in range(2)]
CORE_SWAP = [(device(*a), device(a[0], 1 - a[1], a[2], a[3])) for a in ALL]
X_SWAP = [(device(*a), device(1 - a[0], a[1], a[2], a[3])) for a in ALL]
Y_SWAP = [(device(*a), device(a[0], a[1], a[2], 1 - a[3])) for a in ALL]
Z_SWAPS = [[(device(*a), device(a[0], a[1], a[2] ^ d, a[3])) for a in ALL] for d in (1, 2)]
Z_GROUPS = [
    [device(x, core, z, y) for z in range(4)] for x in range(2) for core in range(2) for y in range(2)
]


def swap(a, pairs):
    return lax.ppermute(a, MESH_AXES, pairs)


def z_exchange(a):
    four, rows, columns = a.shape
    got = lax.all_to_all(
        a.reshape(four * rows, columns), MESH_AXES, 0, 0, axis_index_groups=Z_GROUPS, tiled=True
    )
    return got.reshape(a.shape)


def gather_weights(place, where, shards, over_y_last):
    x, core = place
    cut = []
    for shard in shards:
        rows, width = shard.shape
        cut.append(lax.dynamic_slice(shard, (x * (rows // 2), core * (width // 2)), (rows // 2, width // 2)))
    own = jnp.concatenate(cut, axis=1) if len(cut) > 1 else cut[0]
    near = z_exchange(jnp.broadcast_to(own[None], (4, *own.shape)))
    by_x = swap(near, X_SWAP)
    by_y = swap(near, Y_SWAP)
    both = swap(by_x, Y_SWAP) if over_y_last else swap(by_y, X_SWAP)
    pieces = []
    for piece in (near, by_y, by_x, both):
        pieces += [piece, swap(piece, CORE_SWAP)]
    return place_weights(where, pieces, [s.shape[1] for s in shards])


def reduce_shards(where, same, by_y, by_x, both, over_y_first, widths):
    if over_y_first:
        got = swap(both, Y_SWAP)
        by_x = (by_x.astype(F32) + got.astype(F32)).astype(LOW)
    else:
        got = swap(both, X_SWAP)
        by_y = (by_y.astype(F32) + got.astype(F32)).astype(LOW)
    from_x, from_y = swap(by_x, X_SWAP), swap(by_y, Y_SWAP)
    total = (same.astype(F32) + from_x.astype(F32) + from_y.astype(F32)).astype(LOW)
    own = jnp.sum(z_exchange(total).astype(F32), axis=0).astype(LOW)
    across = swap(own, X_SWAP)
    pieces = (own, swap(own, CORE_SWAP), across, swap(across, CORE_SWAP))
    return place_shards(where, pieces, widths)


def on_device(
    by_links,
    tokens,
    out_grad,
    segment_ids,
    labels,
    query_weight,
    query_bias,
    key_weight,
    value_weight,
    value_bias,
    output_weight,
    output_bias,
    first_norm_gain,
    first_norm_shift,
    inner_weight,
    inner_bias,
    outer_weight,
    outer_bias,
    second_norm_gain,
    second_norm_shift,
    pooler_weight,
    pooler_bias,
    class_weight,
    class_bias,
):
    _, seq, width = tokens.shape
    tokens = tokens.reshape(seq, width)
    out_grad = out_grad.reshape(seq, width)
    dp, fsdp = lax.axis_index("dp"), lax.axis_index("fsdp")
    where = jnp.stack([dp // 2, fsdp % 2, fsdp // 2, dp % 2]).astype(jnp.int32)
    local = query_bias.shape[0]
    shards = width // local
    ff = inner_weight.shape[1]

    small = jnp.concatenate(
        [
            jnp.stack(
                [
                    query_bias,
                    value_bias,
                    output_bias,
                    first_norm_gain,
                    first_norm_shift,
                    outer_bias,
                    second_norm_gain,
                    second_norm_shift,
                    pooler_bias,
                ]
            ),
            inner_bias.reshape(ff // width, local),
            class_weight.T,
        ]
    )

    def everywhere(a, axis, count):
        if not by_links:
            return lax.all_gather(a, axis)
        rows, columns = a.shape
        got = lax.all_to_all(
            jnp.broadcast_to(a[None], (count, rows, columns)).reshape(count * rows, columns), axis, 0, 0, tiled=True
        )
        return got.reshape(count, rows, columns)

    got = everywhere(small, "fsdp", shards).astype(F32)
    table = jnp.transpose(got, (1, 0, 2)).reshape(TABLE, width)
    inner_row = got[:, INNER_B:CLASS_W, :].reshape(1, ff)

    if by_links:
        place = (where[0], where[3])
        wq, wk, wv = gather_weights(place, where, [query_weight, key_weight, value_weight], False)
        wo, wp = gather_weights(place, where, [output_weight, pooler_weight], False)
        (wi,) = gather_weights(place, where, [inner_weight], True)
        (wf,) = gather_weights(place, where, [outer_weight], False)
    else:
        wq, wk, wv, wo, wp, wi, wf = (
            lax.all_gather(w, "fsdp", axis=0, tiled=True)
            for w in (
                query_weight,
                key_weight,
                value_weight,
                output_weight,
                pooler_weight,
                inner_weight,
                outer_weight,
            )
        )

    q, k, v, context, lse = attention(tokens, wq, wk, wv, table, segment_ids)
    n1, r1, first_low = attended(context, wo, tokens, table)
    activated, slope = inner(first_low, wi, inner_row)
    hidden, second_grad, branch_grad, sums2, head, loss = outer(
        activated, wf, n1, table, out_grad, wp, labels, class_bias.astype(F32)
    )
    if by_links:
        other = grads(where, [activated], [0], [branch_grad], True)
        other = [swap(a, CORE_SWAP) for a in other]
    inner_grad, inner_sums, residual_grad, attended_grad, sums1 = inner_back(
        branch_grad, wf, wi, slope, second_grad, n1, r1, table
    )
    if by_links:
        mine = grads(where, [activated], [0], [branch_grad], False, other)
        (outer_grad,) = reduce_shards(where, *mine, True, [width])
        lefts, rights = [first_low, context], [inner_grad, attended_grad]
        other = grads(where, lefts, [0, 1], rights, True)
        other = [swap(a, CORE_SWAP) for a in other]
    dq, dk, dv, sums0 = attention_back(q, k, v, lse, attended_grad, wo, segment_ids)
    if by_links:
        mine = grads(where, lefts, [0, 1], rights, False, other)
        inner_weight_grad, output_grad = reduce_shards(where, *mine, False, [ff, width])
        rights = [dq, dk, dv]
        other = grads(where, [tokens], [0, 0, 0], rights, True)
        other = [swap(a, CORE_SWAP) for a in other]
        mine = grads(where, [tokens], [0, 0, 0], rights, False, other)
        query_grad, key_grad, value_grad = reduce_shards(where, *mine, True, [width] * 3)
    else:
        def reduced(left, right):
            local_grad = lax.dot_general(left, right, (((0,), (0,)), ((), ())), preferred_element_type=F32)
            shard = lax.psum_scatter(local_grad, "fsdp", scatter_dimension=0, tiled=True)
            return lax.psum(shard.astype(LOW), "dp").astype(F32)

        outer_grad = reduced(activated, branch_grad)
        inner_weight_grad = reduced(first_low, inner_grad)
        output_grad = reduced(context, attended_grad)
        query_grad, key_grad, value_grad = (reduced(tokens, d) for d in (dq, dk, dv))
    tokens_grad = tokens_back(residual_grad, dq, dk, dv, wq, wk, wv)

    sums = jnp.concatenate([sums2[:3], sums1[:3], sums0[:2], inner_sums.reshape(ff // width, width)])
    if by_links:
        for pairs in (CORE_SWAP, X_SWAP, Y_SWAP, *Z_SWAPS):
            sums = sums + swap(sums, pairs)
    else:
        sums = lax.psum(sums, MESH_AXES)
    vectors = lax.dynamic_slice(sums, (0, fsdp * local), (8, local))
    inner_bias_grad = lax.dynamic_slice(sums[8:].reshape(ff), (fsdp * (ff // shards),), (ff // shards,))

    heads = everywhere(head.astype(LOW), "fsdp", shards).reshape(shards * 8, width)
    heads = everywhere(heads, "dp", lax.axis_size("dp")).reshape(-1, 8, width)
    class_rows, pre_grads, pooled = heads[:, 0], heads[:, 1], heads[:, 2]
    logit_grads = heads[:, 3, :CLASSES]

    def own_columns(a):
        return lax.dynamic_slice(a, (0, fsdp * local), (a.shape[0], local))

    def over_rows(a, b):
        return lax.dot_general(a, b, (((0,), (0,)), ((), ())), preferred_element_type=F32)

    pooler_grad = over_rows(own_columns(class_rows), pre_grads)
    pooler_bias_grad = jnp.sum(own_columns(pre_grads).astype(F32), axis=0)
    class_grad = over_rows(own_columns(pooled), logit_grads)
    class_bias_grad = jnp.sum(logit_grads.astype(F32), axis=0)

    return (
        hidden[None],
        tokens_grad[None],
        loss[0, :1],
        query_grad,
        vectors[6],
        key_grad,
        value_grad,
        vectors[7],
        output_grad,
        vectors[5],
        vectors[3],
        vectors[4],
        inner_weight_grad,
        inner_bias_grad,
        outer_grad,
        vectors[2],
        vectors[0],
        vectors[1],
        pooler_grad,
        pooler_bias_grad,
        class_grad,
        class_bias_grad,
    )


def solution(mesh):
    sizes = dict(mesh.shape)
    by_links = sizes == {"dp": 4, "fsdp": 8}
    rows = P(MESH_AXES, None, None)
    ids = P(MESH_AXES, None)
    row = P(MESH_AXES)
    matrix = P("fsdp", None)
    vector = P("fsdp")
    return jax.shard_map(
        functools.partial(on_device, by_links),
        mesh=mesh,
        in_specs=(
            rows, rows, ids, row,
            matrix, vector, matrix, matrix, vector, matrix, vector, vector, vector,
            matrix, vector, matrix, vector, vector, vector, matrix, vector, matrix, P(),
        ),
        out_specs=(
            rows, rows, row,
            matrix, vector, matrix, matrix, vector, matrix, vector, vector, vector,
            matrix, vector, matrix, vector, vector, vector, matrix, vector, matrix, P(),
        ),
        check_vma=False,
    )
```

```python
import functools
import math

import jax
import jax.numpy as jnp
from jax import lax
from jax.experimental import pallas as pl
from jax.experimental.pallas import tpu as pltpu
from jax.sharding import PartitionSpec as P

HEAD_DIM = 64
CLASSES = 3
EPS = 1e-06
NEG = -1000000000.0
SCALE = HEAD_DIM**-0.5
LOW = jnp.bfloat16
F32 = jnp.float32
MESH_AXES = ("dp", "fsdp")
MIB = 1 << 20

QUERY_B, VALUE_B, OUTPUT_B, GAIN1, SHIFT1, OUTER_B, GAIN2, SHIFT2, POOLER_B, INNER_B, CLASS_W = (
    0, 1, 2, 3, 4, 5, 6, 7, 8, 9, 13,
)
TABLE = 16


def dot(a, b, dims=((1,), (0,))):
    return lax.dot_general(a, b, (dims, ((), ())), preferred_element_type=F32)


def dot_nt(a, b):
    return dot(a, b, ((1,), (1,)))


def full(shape):
    zeros = (0,) * len(shape)
    return pl.BlockSpec(shape, lambda *_: zeros, pipeline_mode=pl.Buffered(1))


def after(a, *others):
    return lax.optimization_barrier((a, *others))[0]


def call(kernel, outs, in_specs, out_specs, args, *, grid=(1,), scratch=(), prefetch=0, flops=0, moved=0, trans=0, vmem=20, name=None):
    return pl.pallas_call(
        kernel,
        name=name,
        out_shape=outs,
        grid_spec=pltpu.PrefetchScalarGridSpec(
            num_scalar_prefetch=prefetch,
            grid=grid,
            in_specs=in_specs,
            out_specs=out_specs,
            scratch_shapes=scratch,
        ),
        compiler_params=pltpu.CompilerParams(
            dimension_semantics=("arbitrary",) * len(grid), vmem_limit_bytes=vmem * MIB
        ),
        cost_estimate=pl.CostEstimate(flops=flops // 16, bytes_accessed=moved // 16, transcendentals=trans // 16),
    )(*args)


def shape(*dims, dtype=LOW):
    return jax.ShapeDtypeStruct(dims, dtype)


def lane_masks(rows):
    lanes = lax.broadcasted_iota(jnp.int32, (rows, 128), 1)
    return lanes < HEAD_DIM


def attention_kernel(tok, wq, wk, wv, table, seg_row, seg_col, q_o, k_o, v_o, ctx_o, lse_o, bias):
    step = pl.program_id(0)
    seq = tok.shape[0]

    @pl.when(step == 0)
    def _():
        bias[...] = jnp.where(seg_col[...] == seg_row[...], 0.0, NEG)

    x = tok[...]
    q = (dot(x, wq[...]) + table[QUERY_B : QUERY_B + 1, :]).astype(LOW)
    k = dot(x, wk[...]).astype(LOW)
    v = (dot(x, wv[...]) + table[VALUE_B : VALUE_B + 1, :]).astype(LOW)
    q_o[...] = q
    k_o[...] = k
    v_o[...] = v
    first = lane_masks(seq)
    zero = jnp.zeros((seq, 128), LOW)
    for pair in range(q.shape[1] // 128):
        cols = slice(pair * 128, pair * 128 + 128)
        q2, k2, v2t = q[:, cols], k[:, cols], v[:, cols].T
        parts = []
        for half in range(2):
            qm = jnp.where(first, q2, zero) if half == 0 else jnp.where(first, zero, q2)
            s = dot_nt(k2, qm) * SCALE + bias[...]
            top = jnp.max(s, axis=0, keepdims=True)
            e = jnp.exp(s - top)
            total = jnp.sum(e, axis=0, keepdims=True)
            out = dot(v2t[half * HEAD_DIM : (half + 1) * HEAD_DIM], e.astype(LOW)) / total
            parts.append(out)
            row = pair * 2 + half
            lse_o[0, row : row + 1, :] = top + jnp.log(total)
        ctx_o[:, cols] = jnp.concatenate(parts, axis=0).astype(LOW).T


def attention(tokens, wq, wk, wv, table, segments):
    seq, width = tokens.shape
    blk = 256
    steps = width // blk
    cols = pl.BlockSpec((seq, blk), lambda i: (0, i))
    wcols = pl.BlockSpec((width, blk), lambda i: (0, i))
    return call(
        attention_kernel,
        (shape(seq, width),) * 4 + (shape(steps, 8, seq, dtype=F32),),
        [full((seq, width)), wcols, wcols, wcols, pl.BlockSpec((TABLE, blk), lambda i: (0, i)), full((1, seq)), full((seq, 1))],
        (cols,) * 4 + (pl.BlockSpec((1, 8, seq), lambda i: (i, 0, 0)),),
        (tokens, wq, wk, wv, table, segments.reshape(1, seq), segments.reshape(seq, 1)),
        grid=(steps,),
        scratch=[pltpu.VMEM((seq, seq), F32)],
        flops=2 * seq * width * (3 * width + 2 * seq),
        moved=8 * seq * width + 6 * width * width,
        trans=seq * seq * width // HEAD_DIM,
        name="attention",
    )


def rows_norm(v):
    mean = jnp.mean(v, axis=-1, keepdims=True)
    centered = v - mean
    variance = jnp.mean(centered * centered, axis=-1, keepdims=True)
    scale = lax.rsqrt(variance + EPS)
    return centered * scale, scale


def attended_kernel(ctx, wo, tok, table, n1_o, r1_o, low_o):
    v = dot(ctx[...], wo[...]) + table[OUTPUT_B : OUTPUT_B + 1, :] + tok[...].astype(F32)
    n, r = rows_norm(v)
    n1_o[...] = n
    r1_o[...] = r
    low_o[...] = (n * table[GAIN1 : GAIN1 + 1, :] + table[SHIFT1 : SHIFT1 + 1, :]).astype(LOW)


def attended(ctx, wo, tokens, table):
    seq, width = tokens.shape
    blk = 128
    rows = pl.BlockSpec((blk, width), lambda i: (i, 0))
    return call(
        attended_kernel,
        (shape(seq, width, dtype=F32), shape(seq, 1, dtype=F32), shape(seq, width)),
        [rows, full((width, width)), rows, full((TABLE, width))],
        (rows, pl.BlockSpec((blk, 1), lambda i: (i, 0)), rows),
        (ctx, wo, tokens, table),
        grid=(seq // blk,),
        flops=2 * seq * width * width,
        moved=2 * width * width + 10 * seq * width,
        name="attended",
    )


ERFC_POLY = (
    0.2820605933666229,
    0.28293782472610474,
    0.237934872508049,
    0.22901807725429535,
    -0.10879392176866531,
    0.44148358702659607,
    -0.6950507164001465,
    0.44817423820495605,
    -0.13161660730838776,
    0.013852047733962536,
)


def gelu_parts(v):
    u = jnp.abs(v) * (0.5**0.5)
    t = 1.0 / (1.0 + 0.5 * u)
    poly = jnp.full_like(t, ERFC_POLY[-1])
    for coefficient in ERFC_POLY[-2::-1]:
        poly = poly * t + coefficient
    bell = jnp.exp(v * v * -0.5)
    tail = (0.5 * t) * poly * bell
    below = jnp.where(v < 0, tail, 1.0 - tail)
    return v * below, below + v * (bell * 0.3989422804014327)


def inner_kernel(low, wi, bi, act_o, slope_o):
    v = dot(low[...], wi[...]) + bi[...]
    act, slope = gelu_parts(v)
    act_o[...] = act.astype(LOW)
    slope_o[...] = slope.astype(LOW)


def inner(low, wi, bi):
    seq, width = low.shape
    ff = wi.shape[1]
    blk = 512
    cols = pl.BlockSpec((seq, blk), lambda i: (0, i))
    return call(
        inner_kernel,
        (shape(seq, ff), shape(seq, ff)),
        [full((seq, width)), pl.BlockSpec((width, blk), lambda i: (0, i)), pl.BlockSpec((1, blk), lambda i: (0, i))],
        (cols, cols),
        (low, wi, bi),
        grid=(ff // blk,),
        flops=2 * seq * width * ff,
        moved=2 * width * ff + 4 * seq * ff,
        trans=2 * seq * ff,
        name="inner",
    )


def outer_kernel(labels, bias3, act, w, n1, table, out_grad, wp, hid_o, sg_o, bg_o, sums_o, head_o, loss_o, acc, n2_s, r2_s):
    step = pl.program_id(0)
    seq, width = n1.shape

    @pl.when(step == 0)
    def _():
        acc[...] = jnp.zeros_like(acc)

    acc[...] += dot(act[...], w[...])

    @pl.when(step == pl.num_programs(0) - 1)
    def _():
        def row(at):
            return table[at : at + 1, :]

        gain2, shift2 = row(GAIN2), row(SHIFT2)
        blk = 64
        for at in range(0, seq, blk):
            rows = slice(at, at + blk)
            v = acc[rows, :] + row(OUTER_B) + (n1[rows, :] * row(GAIN1) + row(SHIFT1))
            n, r = rows_norm(v)
            n2_s[rows, :] = n
            r2_s[rows, :] = r
            hid_o[rows, :] = (n * gain2 + shift2).astype(LOW)
        class_rows = hid_o[0:8, :]
        pooled_pre = dot(class_rows, wp[...])[0:1, :] + row(POOLER_B)
        bent = jnp.tanh(pooled_pre)
        pooled = bent.astype(LOW).astype(F32)
        logits = [
            jnp.sum(pooled * row(CLASS_W + j), axis=-1, keepdims=True) + bias3[j] for j in range(CLASSES)
        ]
        top = functools.reduce(jnp.maximum, logits)
        exps = [jnp.exp(v - top) for v in logits]
        total = functools.reduce(jnp.add, exps)
        label = labels[0]
        hot = [jnp.where(label == j, 1.0, 0.0) for j in range(CLASSES)]
        picked = functools.reduce(jnp.add, [a * b for a, b in zip(logits, hot)])
        loss_o[...] = jnp.broadcast_to(top + jnp.log(total) - picked, loss_o.shape)
        slopes = [(e / total - o).astype(LOW).astype(F32) for e, o in zip(exps, hot)]
        pooled_grad = functools.reduce(
            jnp.add, [g * row(CLASS_W + j) for j, g in enumerate(slopes)]
        )
        pre_grad = (pooled_grad * (1.0 - bent * bent)).astype(LOW)
        row_grad = dot_nt(jnp.broadcast_to(pre_grad, (8, width)), wp[...])[0:1, :]
        head_o[...] = jnp.zeros_like(head_o)
        lanes = lax.broadcasted_iota(jnp.int32, (1, width), 1)
        head_o[0:1, :] = class_rows[0:1, :].astype(F32)
        head_o[1:2, :] = pre_grad.astype(F32)
        head_o[2:3, :] = pooled
        head_o[3:4, :] = functools.reduce(
            jnp.add, [jnp.where(lanes == j, g, 0.0) for j, g in enumerate(slopes)]
        )
        gain_sum = jnp.zeros((1, width), F32)
        shift_sum = jnp.zeros((1, width), F32)
        bias_sum = jnp.zeros((1, width), F32)
        for at in range(0, seq, blk):
            rows = slice(at, at + blk)
            fg = out_grad[rows, :].astype(F32)
            if at == 0:
                lead = lax.broadcasted_iota(jnp.int32, (blk, width), 0) == 0
                fg = fg + jnp.where(lead, jnp.broadcast_to(row_grad, (blk, width)), 0.0)
            n = n2_s[rows, :]
            g = fg * gain2
            gm = jnp.mean(g, axis=-1, keepdims=True)
            gn = jnp.mean(g * n, axis=-1, keepdims=True)
            sg = r2_s[rows, :] * (g - gm - n * gn)
            low = sg.astype(LOW)
            sg_o[rows, :] = sg
            bg_o[rows, :] = low
            gain_sum += jnp.sum(fg * n, axis=0, keepdims=True)
            shift_sum += jnp.sum(fg, axis=0, keepdims=True)
            bias_sum += jnp.sum(low.astype(F32), axis=0, keepdims=True)
        sums_o[...] = jnp.zeros_like(sums_o)
        sums_o[0:1, :] = gain_sum
        sums_o[1:2, :] = shift_sum
        sums_o[2:3, :] = bias_sum


def outer(act, w, n1, table, out_grad, wp, labels, bias3):
    seq, width = n1.shape
    ff = act.shape[1]
    blk = 512
    whole = full((seq, width))
    return call(
        outer_kernel,
        (
            shape(seq, width),
            shape(seq, width, dtype=F32),
            shape(seq, width),
            shape(8, width, dtype=F32),
            shape(8, width, dtype=F32),
            shape(8, 128, dtype=F32),
        ),
        [
            pl.BlockSpec((seq, blk), lambda i, *_: (0, i)),
            pl.BlockSpec((blk, width), lambda i, *_: (i, 0)),
            whole,
            full((TABLE, width)),
            whole,
            full((width, width)),
        ],
        (whole, whole, whole, full((8, width)), full((8, width)), full((8, 128))),
        (labels, bias3, act, w, n1, table, out_grad, wp),
        grid=(ff // blk,),
        scratch=[pltpu.VMEM((seq, width), F32), pltpu.VMEM((seq, width), F32), pltpu.VMEM((seq, 1), F32)],
        prefetch=2,
        flops=2 * seq * width * ff,
        moved=2 * width * ff + 2 * seq * ff + 14 * seq * width,
        name="outer",
    )


def inner_grad_kernel(bg, w_out, slope, ig_o):
    ig_o[...] = (dot_nt(bg[...], w_out[...]) * slope[...].astype(F32)).astype(LOW)


def inner_grads(bg, w_out, slope):
    seq, width = bg.shape
    ff = slope.shape[1]
    blk = 512
    cols = pl.BlockSpec((seq, blk), lambda i: (0, i))
    return call(
        inner_grad_kernel,
        shape(seq, ff),
        [full((seq, width)), pl.BlockSpec((blk, width), lambda i: (i, 0)), cols],
        cols,
        (bg, w_out, slope),
        grid=(ff // blk,),
        flops=2 * seq * width * ff,
        moved=2 * width * ff + 4 * seq * ff,
        name="inner_grads",
    )


def inner_back_kernel(ig, w_in, sg, n1, r1, table, res_o, ag_o, sums_o, acc, ib):
    step = pl.program_id(0)
    seq, width = n1.shape
    blk = ig.shape[1]
    ib[:, pl.ds(pl.multiple_of(step * blk, blk), blk)] = jnp.sum(ig[...].astype(F32), axis=0, keepdims=True)

    @pl.when(step == 0)
    def _():
        acc[...] = jnp.zeros_like(acc)

    acc[...] += dot_nt(ig[...], w_in[...])

    @pl.when(step == pl.num_programs(0) - 1)
    def _():
        gain1 = table[GAIN1 : GAIN1 + 1, :]
        gain_sum = jnp.zeros((1, width), F32)
        shift_sum = jnp.zeros((1, width), F32)
        bias_sum = jnp.zeros((1, width), F32)
        blk = 64
        for at in range(0, seq, blk):
            rows = slice(at, at + blk)
            fg = sg[rows, :] + acc[rows, :]
            n = n1[rows, :]
            g = fg * gain1
            gm = jnp.mean(g, axis=-1, keepdims=True)
            gn = jnp.mean(g * n, axis=-1, keepdims=True)
            res = r1[rows, :] * (g - gm - n * gn)
            low = res.astype(LOW)
            res_o[rows, :] = res
            ag_o[rows, :] = low
            gain_sum += jnp.sum(fg * n, axis=0, keepdims=True)
            shift_sum += jnp.sum(fg, axis=0, keepdims=True)
            bias_sum += jnp.sum(low.astype(F32), axis=0, keepdims=True)
        sums_o[...] = jnp.zeros_like(sums_o)
        sums_o[0:1, :] = gain_sum
        sums_o[1:2, :] = shift_sum
        sums_o[2:3, :] = bias_sum
        for at in range(ib.shape[1] // width):
            sums_o[3 + at : 4 + at, :] = ib[:, at * width : (at + 1) * width]


def inner_back(ig, w_in, sg, n1, r1, table):
    seq, width = n1.shape
    ff = ig.shape[1]
    blk = 512
    whole = full((seq, width))
    return call(
        inner_back_kernel,
        (shape(seq, width, dtype=F32), shape(seq, width), shape(8, width, dtype=F32)),
        [
            pl.BlockSpec((seq, blk), lambda i: (0, i)),
            pl.BlockSpec((width, blk), lambda i: (0, i)),
            whole,
            whole,
            full((seq, 1)),
            full((TABLE, width)),
        ],
        (whole, whole, full((8, width))),
        (ig, w_in, sg, n1, r1, table),
        grid=(ff // blk,),
        scratch=[pltpu.VMEM((seq, width), F32), pltpu.VMEM((1, ff), F32)],
        flops=2 * seq * width * ff,
        moved=2 * width * ff + 2 * seq * ff + 16 * seq * width,
        name="inner_back",
    )


def attention_back_kernel(q, k, v, lse, ag, wo, seg_row, seg_col, dq_o, dk_o, dv_o, sums_o, bias):
    seq = ag.shape[0]

    @pl.when(pl.program_id(0) == 0)
    def _():
        bias[...] = jnp.where(seg_col[...] == seg_row[...], 0.0, NEG)

    grad = dot_nt(ag[...], wo[...]).astype(LOW)
    first = lane_masks(seq)
    zero = jnp.zeros((seq, 128), LOW)
    sums_o[...] = jnp.zeros_like(sums_o)
    for pair in range(q.shape[1] // 128):
        cols = slice(pair * 128, pair * 128 + 128)
        q2, k2, v2, g2 = q[:, cols], k[:, cols], v[:, cols], grad[:, cols]
        k2t = k2.T
        dqs, dks, dvs = [], [], []
        for half in range(2):
            def own(a):
                return jnp.where(first, a, zero) if half == 0 else jnp.where(first, zero, a)

            row = pair * 2 + half
            s = dot_nt(k2, own(q2)) * SCALE + bias[...]
            p = jnp.exp(s - lse[0, row : row + 1, :])
            dp = dot_nt(v2, own(g2))
            weighted = p * dp
            level = jnp.sum(weighted, axis=0, keepdims=True)
            ds = (weighted - p * level).astype(LOW)
            dvs.append(dot(p.astype(LOW), g2))
            dks.append(dot(ds, q2))
            dqs.append(dot(k2t[half * HEAD_DIM : (half + 1) * HEAD_DIM], ds))
        dq = (jnp.concatenate(dqs, axis=0) * SCALE).astype(LOW).T
        dk = (jnp.where(first, dks[0], dks[1]) * SCALE).astype(LOW)
        dv = jnp.where(first, dvs[0], dvs[1]).astype(LOW)
        dq_o[:, cols] = dq
        dk_o[:, cols] = dk
        dv_o[:, cols] = dv
        sums_o[0:1, cols] = jnp.sum(dq.astype(F32), axis=0, keepdims=True)
        sums_o[1:2, cols] = jnp.sum(dv.astype(F32), axis=0, keepdims=True)


def attention_back(q, k, v, lse, ag, wo, segments, begin, count):
    seq, width = ag.shape
    blk = 256
    begin, steps = begin // blk, count // blk
    cols = pl.BlockSpec((seq, blk), lambda i: (0, i + begin))
    out = pl.BlockSpec((seq, blk), lambda i: (0, i))
    return call(
        attention_back_kernel,
        (shape(seq, count),) * 3 + (shape(8, count, dtype=F32),),
        [
            cols,
            cols,
            cols,
            pl.BlockSpec((1, 8, seq), lambda i: (i + begin, 0, 0)),
            full((seq, width)),
            pl.BlockSpec((blk, width), lambda i: (i + begin, 0)),
            full((1, seq)),
            full((seq, 1)),
        ],
        (out,) * 3 + (pl.BlockSpec((8, blk), lambda i: (0, i)),),
        (q, k, v, lse, ag, wo, segments.reshape(1, seq), segments.reshape(seq, 1)),
        grid=(steps,),
        scratch=[pltpu.VMEM((seq, seq), F32)],
        flops=2 * seq * count * (width + 5 * seq),
        moved=16 * seq * count + 2 * width * count,
        trans=seq * seq * count // HEAD_DIM,
        name="attention_back",
    )


def tokens_back_kernel(res, dq, dk, dv, wq, wk, wv, out):
    out[...] = res[...] + dot_nt(dq[...], wq[...]) + dot_nt(dk[...], wk[...]) + dot_nt(dv[...], wv[...])


def tokens_back(res, dq, dk, dv, wq, wk, wv):
    seq, width = res.shape
    blk = 128
    rows = pl.BlockSpec((blk, width), lambda i: (i, 0))
    weight = full((width, width))
    return call(
        tokens_back_kernel,
        shape(seq, width, dtype=F32),
        [rows] * 4 + [weight] * 3,
        rows,
        (res, dq, dk, dv, wq, wk, wv),
        grid=(seq // blk,),
        flops=6 * seq * width * width,
        moved=14 * seq * width + 6 * width * width,
        name="tokens_back",
    )


def grads(name, where, lefts, which, rights, add=None, form=None):
    seq = lefts[0].shape[0]
    parts = lefts[0].shape[1] // 16
    widths = tuple((w, r.shape[1] // 2) for w, r in zip(which, rights))
    total = sum(w for _, w in widths)
    half = (lambda i, where: (0, 1 - where[3])) if add is None else (lambda i, where: (0, where[3]))
    specs = [full(a.shape) for a in lefts]
    specs += [pl.BlockSpec((seq, w), half, pipeline_mode=pl.Buffered(1)) for _, w in widths]
    args = [where, *lefts, *rights]
    if add is None:
        outs = ((4, 4, parts, total),)
    elif form == "z":
        outs = ((2, 4, parts, total),) * 2
    else:
        outs = ((4, parts, total),) * 4
    if add is not None:
        specs.append(full(add.shape))
        args.append(add)

    def kernel(where, *refs):
        left_refs, refs = refs[: len(lefts)], refs[len(lefts) :]
        right_refs, refs = refs[: len(rights)], refs[len(rights) :]
        add_ref = None if add is None else refs[0]
        out_refs, turned = refs[: len(outs)] if add is None else refs[1 : 1 + len(outs)], refs[-len(lefts) :]
        x, y, z0 = where[0], where[1], where[2]
        for left, store in zip(left_refs, turned):
            for start in range(0, left.shape[1], 256):
                store[start : start + 256, :] = left[:, start : start + 256].T
        for place in range(4):
            hh = jnp.bitwise_xor(x, place // 2)
            yy = jnp.bitwise_xor(y, place % 2)
            column = 0
            for (at, width), right in zip(widths, right_refs):
                rows = []
                for dz in range(4):
                    shard = jnp.bitwise_xor(z0, dz) * 2 + yy
                    rows.append(turned[at][pl.ds(pl.multiple_of((shard * 2 + hh) * parts, 16), parts), :])
                got = dot(jnp.concatenate(rows, axis=0), right[...]).reshape(4, parts, width)
                cols = slice(column, column + width)
                if add is not None:
                    got = got + add_ref[place, :, :, cols].astype(F32)
                got = got.astype(LOW)
                if add is None:
                    out_refs[0][place, :, :, cols] = got
                elif form == "z":
                    for dz in range(4):
                        out_refs[dz % 2][dz // 2, place, :, cols] = got[dz]
                else:
                    out_refs[place][:, :, cols] = got
                column += width

    got = call(
        kernel,
        tuple(shape(*o) for o in outs),
        specs,
        tuple(full(o) for o in outs),
        args,
        scratch=[pltpu.VMEM((a.shape[1], seq), LOW) for a in lefts],
        prefetch=1,
        flops=2 * seq * 16 * parts * total,
        moved=2 * 16 * parts * total + 2 * seq * 16 * parts,
        name=name,
    )
    return got[0] if add is None else got


def pack_kernel(where, wq, wk, wv, wo, wi, wf, wp, small, own_a, own_b, own_c):
    for out, weights in ((own_a, (wq, wk, wv)), (own_b, (wo, wi))):
        left = 0
        for ref in weights:
            out[: ref.shape[0], left : left + ref.shape[1]] = ref[...]
            left += ref.shape[1]
    at = wq.shape[0]
    own_a[at:, :] = jnp.zeros((8, own_a.shape[1]), LOW)
    for top in range(0, small.shape[0], 8):
        own_a[at:, top * 16 : top * 16 + small.shape[1]] = small[top : top + 8, :]
    rows = wf.shape[0]
    own_c[:rows, :] = wf[...]
    own_c[rows:, :] = wp[...]


def pack(where, wq, wk, wv, wo, wi, wf, wp, small):
    rows, width = wq.shape
    deep = wf.shape[0] // 2
    ff = wi.shape[1]
    outs = (shape(rows // 2 + 8, 3 * width // 2), shape(rows // 2, (width + ff) // 2), shape(deep + rows // 2, width // 2))
    weights = (wq, wk, wv, wo, wi, wf, wp)
    quarters = [
        pl.BlockSpec((w.shape[0] // 2, w.shape[1] // 2), lambda i, where: (where[0], where[3])) for w in weights
    ]
    return call(
        pack_kernel,
        outs,
        quarters + [full(small.shape)],
        tuple(full(o.shape) for o in outs),
        (where, *(pltpu.with_memory_space_constraint(w, pltpu.HBM) for w in weights), small),
        prefetch=1,
        moved=4 * sum(math.prod(o.shape) for o in outs),
        vmem=8,
        name="pack",
    )


def weights_kernel(spans, where, *refs):
    pieces, outs, sem = refs[:8], refs[8:-1], refs[-1]
    copies = []
    for place in range(8):
        hh = jnp.bitwise_xor(where[0], place // 4)
        yy = jnp.bitwise_xor(where[1], place // 2 % 2)
        cc = jnp.bitwise_xor(where[3], place % 2)
        for dz in range(4):
            zz = jnp.bitwise_xor(where[2], dz)
            for (top, rows, left, width), out in zip(spans, outs):
                to = out.at[zz, yy, hh, :, pl.ds(pl.multiple_of(cc * width, 128), width)]
                come = pieces[place].at[dz, top : top + rows, left : left + width]
                copies.append(pltpu.make_async_copy(come, to, sem.at[len(copies)]))
    for one in copies:
        one.start()
    for one in copies:
        one.wait()


def place_weights(where, pieces, spans):
    anywhere = pl.BlockSpec(memory_space=pl.ANY)
    outs = call(
        functools.partial(weights_kernel, tuple(spans)),
        tuple(shape(4, 2, 2, rows, 2 * width) for _, rows, _, width in spans),
        [anywhere] * 8,
        (anywhere,) * len(spans),
        (where, *(pltpu.with_memory_space_constraint(p, pltpu.VMEM) for p in pieces)),
        scratch=[pltpu.SemaphoreType.DMA((32 * len(spans),))],
        prefetch=1,
        moved=4 * 8 * pieces[0].size,
        vmem=4,
        name="place_weights",
    )
    return [o.reshape(16 * rows, 2 * width) for o, (_, rows, _, width) in zip(outs, spans)]


def shards_kernel(spans, where, *refs):
    pieces, outs = refs[:4], refs[4:]
    for place in range(4):
        hh = jnp.bitwise_xor(where[0], place // 2)
        for core in range(2):
            @pl.when(jnp.bitwise_xor(where[3], place % 2) == core)
            def _():
                for (start, width), out in zip(spans, outs):
                    out[hh, :, core * width : (core + 1) * width] = pieces[place][
                        :, start : start + width
                    ].astype(F32)


def place_shards(where, pieces, widths):
    parts = pieces[0].shape[0]
    spans, start = [], 0
    for width in widths:
        spans.append((start, width // 2))
        start += width // 2
    outs = call(
        functools.partial(shards_kernel, tuple(spans)),
        tuple(shape(2, parts, w, dtype=F32) for w in widths),
        [full(pieces[0].shape)] * 4,
        tuple(full((2, parts, w)) for w in widths),
        (where, *pieces),
        prefetch=1,
        moved=12 * parts * sum(widths),
        vmem=12,
        name="place_shards",
    )
    return [o.reshape(2 * parts, w) for o, w in zip(outs, widths)]


def device(x, core, z, y):
    return (x * 2 + core) * 8 + z * 2 + y


ALL = [(x, core, z, y) for x in range(2) for core in range(2) for z in range(4) for y in range(2)]
CORE_SWAP = [(device(*a), device(a[0], 1 - a[1], a[2], a[3])) for a in ALL]
X_SWAP = [(device(*a), device(1 - a[0], a[1], a[2], a[3])) for a in ALL]
Y_SWAP = [(device(*a), device(a[0], a[1], a[2], 1 - a[3])) for a in ALL]
Z_SWAPS = [[(device(*a), device(a[0], a[1], a[2] ^ d, a[3])) for a in ALL] for d in range(4)]
X_CORE_SWAP = [(device(*a), device(1 - a[0], 1 - a[1], a[2], a[3])) for a in ALL]
XY_SWAP = [(device(*a), device(1 - a[0], a[1], a[2], 1 - a[3])) for a in ALL]


def swap(a, pairs):
    return lax.ppermute(a, MESH_AXES, pairs)


def wide(*arrays):
    return functools.reduce(jnp.add, [a.astype(F32) for a in arrays])


def along_z(own):
    return [swap(own, Z_SWAPS[d]) for d in (1, 2, 3)]


def to_core(arrays):
    return [swap(a, CORE_SWAP) for a in arrays]


def together(*groups):
    leaves, tree = jax.tree.flatten(groups)
    return jax.tree.unflatten(tree, lax.optimization_barrier(tuple(leaves)))


def low(a):
    return a.astype(LOW)


def sums_by_z(parts):
    return [wide(*(p[d] for p in parts)) for d in range(4)]


def on_device(
    by_links,
    tokens,
    out_grad,
    segment_ids,
    labels,
    query_weight,
    query_bias,
    key_weight,
    value_weight,
    value_bias,
    output_weight,
    output_bias,
    first_norm_gain,
    first_norm_shift,
    inner_weight,
    inner_bias,
    outer_weight,
    outer_bias,
    second_norm_gain,
    second_norm_shift,
    pooler_weight,
    pooler_bias,
    class_weight,
    class_bias,
):
    _, seq, width = tokens.shape
    tokens = tokens.reshape(seq, width)
    out_grad = out_grad.reshape(seq, width)
    dp, fsdp = lax.axis_index("dp"), lax.axis_index("fsdp")
    where = jnp.stack([dp // 2, fsdp % 2, fsdp // 2, dp % 2]).astype(jnp.int32)
    local = query_bias.shape[0]
    shards = width // local
    ff = inner_weight.shape[1]

    small = jnp.concatenate(
        [
            jnp.stack(
                [
                    query_bias,
                    value_bias,
                    output_bias,
                    first_norm_gain,
                    first_norm_shift,
                    outer_bias,
                    second_norm_gain,
                    second_norm_shift,
                    pooler_bias,
                ]
            ),
            inner_bias.reshape(ff // width, local),
            class_weight.T,
        ]
    )

    def tables(got):
        table = jnp.transpose(got, (1, 0, 2)).reshape(TABLE, width)
        return table, got[:, INNER_B:CLASS_W, :].reshape(1, ff)

    bias3 = class_bias.astype(F32)
    if by_links:
        own_a, own_b, own_c = pack(
            where,
            query_weight,
            key_weight,
            value_weight,
            output_weight,
            inner_weight,
            outer_weight,
            pooler_weight,
            small,
        )
        parts, deep = local // 2, outer_weight.shape[0] // 2
        spans_a = [(0, parts, at * (width // 2), width // 2) for at in range(3)]
        spans_b = [(0, parts, 0, width // 2), (0, parts, width // 2, ff // 2)]
        spans_c = [(0, deep, 0, width // 2), (deep, parts, 0, width // 2)]

        def mixed(near, other):
            return [a for pair in zip(near, other) for a in pair]

        z_a = along_z(own_a)
        (z_a, own_a, own_b, own_c) = together(z_a, own_a, own_b, own_c)
        z_b = along_z(own_b)
        far_a = jnp.stack([own_a, *z_a])
        x_a, y_a = swap(far_a, X_SWAP), swap(far_a, Y_SWAP)
        (far_a, x_a, y_a, z_b, own_b, own_c) = together(far_a, x_a, y_a, z_b, own_b, own_c)
        z_c = along_z(own_c)
        far_b = jnp.stack([own_b, *z_b])
        xy_a = swap(x_a, Y_SWAP)
        x_b = swap(far_b, X_SWAP)
        (core_a,) = to_core([jnp.concatenate([far_a, y_a, x_a])])
        order = [((where[2] ^ d) * 2 + (where[1] ^ e)) for e in range(2) for d in range(4)]
        spread = (jnp.stack(order)[None, :] == jnp.arange(shards)[:, None]).astype(LOW)
        small = jnp.concatenate([far_a[:, parts:, :256], y_a[:, parts:, :256]])
        small = jnp.concatenate([small[:, :, :local], small[:, :, 128 : 128 + local]], axis=1)
        table, inner_row = tables(jnp.einsum("sp,pji->sji", spread, small, preferred_element_type=F32))
        (far_a, y_a, x_a, xy_a, far_b, x_b, z_c, core_a, own_c, table, inner_row) = together(
            far_a, y_a, x_a, xy_a, far_b, x_b, z_c, core_a, own_c, table, inner_row
        )
        y_b = swap(far_b, Y_SWAP)
        far_c = jnp.stack([own_c, *z_c])
        x_c = swap(far_c, X_SWAP)
        core_a = [core_a[:4], core_a[4:8], core_a[8:]] + to_core([xy_a])
        wq, wk, wv = place_weights(where, mixed((far_a, y_a, x_a, xy_a), core_a), spans_a)
        q, k, v, context, lse = attention(tokens, wq, wk, wv, table, segment_ids)
        (q, k, v, context, lse, far_b, x_b, y_b, far_c, x_c) = together(
            q, k, v, context, lse, far_b, x_b, y_b, far_c, x_c
        )
        xy_b = swap(y_b, X_SWAP)
        y_c = swap(far_c, Y_SWAP)
        core_b = to_core([far_b, y_b, x_b])
        (far_b, y_b, x_b, xy_b, core_b, far_c, x_c, y_c) = together(
            far_b, y_b, x_b, xy_b, core_b, far_c, x_c, y_c
        )
        xy_c = swap(x_c, Y_SWAP)
        core_b += to_core([xy_b])
        core_c = to_core([far_c, y_c, x_c])
        wo, wi = place_weights(where, mixed((far_b, y_b, x_b, xy_b), core_b), spans_b)
        n1, r1, first_low = attended(context, wo, tokens, table)
        activated, slope = inner(first_low, wi, inner_row)
        (far_c, y_c, x_c, xy_c, core_c, activated, slope) = together(
            far_c, y_c, x_c, xy_c, core_c, activated, slope
        )
        core_c += to_core([xy_c])
        wf, wp = place_weights(where, mixed((far_c, y_c, x_c, xy_c), core_c), spans_c)
    else:
        wq, wk, wv, wo, wp, wi, wf = (
            lax.all_gather(w, "fsdp", axis=0, tiled=True)
            for w in (
                query_weight,
                key_weight,
                value_weight,
                output_weight,
                pooler_weight,
                inner_weight,
                outer_weight,
            )
        )
        table, inner_row = tables(lax.all_gather(small, "fsdp").astype(F32))
        q, k, v, context, lse = attention(tokens, wq, wk, wv, table, segment_ids)
        n1, r1, first_low = attended(context, wo, tokens, table)
        activated, slope = inner(first_low, wi, inner_row)

    hidden, second_grad, branch_grad, sums2, head, loss = outer(
        activated, wf, n1, table, out_grad, wp, labels, bias3
    )
    def attention_step(attended_grad, begin, count):
        return attention_back(q, k, v, lse, attended_grad, wo, segment_ids, begin, count)

    cut = 512
    if by_links:

        def doubled(both, pairs):
            come = swap(both, pairs)
            return jnp.concatenate([both[:3] + come[:3], both[3:], come[3:]])

        def plane(parts):
            same, y, x, xy = parts
            return [same, swap(x, X_SWAP), swap(y, Y_SWAP), swap(xy, XY_SWAP)]

        other = grads("outer_grad_a", where, [activated], [0], [branch_grad])
        (other, branch_grad) = together(other, branch_grad)
        other = swap(other, CORE_SWAP)
        inner_grad = inner_grads(branch_grad, wf, slope)
        (other, inner_grad) = together(other, inner_grad)
        mine = grads("outer_grad_b", where, [activated], [0], [branch_grad], other, "place")
        (mine, inner_grad) = together(mine, inner_grad)
        same_f, y_f, x_f, xy_f = mine
        from_x, from_y = swap(x_f[:2], X_SWAP), swap(y_f[:2], Y_SWAP)
        residual_grad, attended_grad, sums1 = inner_back(inner_grad, wi, second_grad, n1, r1, table)
        (attended_grad, inner_grad) = together(attended_grad, inner_grad)
        lefts, rights = [first_low, context], [inner_grad, attended_grad]
        other = grads("inner_grad_a", where, lefts, [0, 1], rights)
        (other, attended_grad, from_x, from_y, x_f, y_f, xy_f) = together(
            other, attended_grad, from_x, from_y, x_f[2:], y_f[2:], xy_f
        )
        other = swap(other, CORE_SWAP)
        x_f, y_f, xy_f = swap(x_f, X_SWAP), swap(y_f, Y_SWAP), swap(xy_f, XY_SWAP)
        back_a = attention_step(attended_grad, 0, cut)
        (other, back_a, attended_grad) = together(other, back_a, attended_grad)
        mine = grads("inner_grad_b", where, lefts, [0, 1], rights, other, "place")
        (mine, attended_grad) = together(mine, attended_grad)
        back_b = attention_step(attended_grad, cut, width - cut)
        dq, dk, dv, sums0 = (jnp.concatenate([a, b], axis=1) for a, b in zip(back_a, back_b))
        rights = [dq, dk, dv]
        other = grads("query_grad_a", where, [tokens], [0, 0, 0], rights)
        (other, dq, dk, dv, sums0, x_f, y_f, xy_f, mine) = together(other, dq, dk, dv, sums0, x_f, y_f, xy_f, mine)
        rights = [dq, dk, dv]
        parts_i = plane(mine)
        other = swap(other, CORE_SWAP)
        totals_f = [wide(same_f[d], xy_f[d], from_x[d], from_y[d]) for d in range(2)]
        totals_f += [wide(same_f[2 + d], xy_f[2 + d], x_f[d], y_f[d]) for d in range(2)]
        mine = grads("query_grad_b", where, [tokens], [0, 0, 0], rights, other, "place")
        odd_f = swap(low(jnp.stack([totals_f[1], totals_f[3]])), Z_SWAPS[1])
        both = jnp.concatenate([jnp.stack([sums2, sums1, sums0]), head[None]])
        (mine, odd_f, even_f, dq, dk, dv, both) = together(mine, odd_f, [totals_f[0], totals_f[2]], dq, dk, dv, both)
        go_f = swap(low(wide(even_f[1], odd_f[1])), Z_SWAPS[2])
        both = doubled(both, Z_SWAPS[1])
        tokens_grad = tokens_back(residual_grad, dq, dk, dv, wq, wk, wv)
        (parts_i, mine, go_f, stay_f, tokens_grad, both) = together(
            parts_i, mine, go_f, wide(even_f[0], odd_f[0]), tokens_grad, both
        )
        parts_q = plane(mine)
        own_f = low(wide(stay_f, go_f))
        totals_i = sums_by_z(parts_i)
        odd_i = swap(low(jnp.stack([totals_i[1], totals_i[3]])), Z_SWAPS[1])
        both = doubled(both, Z_SWAPS[2])
        (odd_i, own_f, even_i, both) = together(odd_i, own_f, [totals_i[0], totals_i[2]], both)
        go_i = swap(low(wide(even_i[1], odd_i[1])), Z_SWAPS[2])
        stay_i = wide(even_i[0], odd_i[0])
        (parts_q, go_i, stay_i, own_f, both) = together(parts_q, go_i, stay_i, own_f, both)
        totals_q = sums_by_z(parts_q)
        z_q = [swap(low(totals_q[d]), Z_SWAPS[d]) for d in (1, 2, 3)]
        own_i = low(wide(stay_i, go_i))
        both = doubled(both, X_SWAP)
        (z_q, own_q, own_i, both, own_f) = together(z_q, totals_q[0], own_i, both, own_f)
        def shared(own):
            return [own, swap(own, CORE_SWAP), swap(own, X_SWAP), swap(own, X_CORE_SWAP)]

        all_f = shared(own_f)
        own_q = low(wide(own_q, *z_q))
        both = doubled(both, Y_SWAP)
        (all_f, own_q, both, own_i) = together(all_f, own_q, both, own_i)
        all_q, all_i = shared(own_q), shared(own_i)
        both = doubled(both, CORE_SWAP)
        (outer_grad,) = place_shards(where, all_f, [width])
        inner_weight_grad, output_grad = place_shards(where, all_i, [ff, width])
        query_grad, key_grad, value_grad = place_shards(where, all_q, [width] * 3)
        sums, heads = both[:3], both[3:]
    else:

        def reduced(left, right):
            local_grad = lax.dot_general(left, right, (((0,), (0,)), ((), ())), preferred_element_type=F32)
            shard = lax.psum_scatter(local_grad, "fsdp", scatter_dimension=0, tiled=True)
            return lax.psum(low(shard), "dp").astype(F32)

        inner_grad = inner_grads(branch_grad, wf, slope)
        residual_grad, attended_grad, sums1 = inner_back(inner_grad, wi, second_grad, n1, r1, table)
        dq, dk, dv, sums0 = attention_step(attended_grad, 0, width)
        outer_grad = reduced(activated, branch_grad)
        inner_weight_grad = reduced(first_low, inner_grad)
        output_grad = reduced(context, attended_grad)
        query_grad, key_grad, value_grad = (reduced(tokens, d) for d in (dq, dk, dv))
        tokens_grad = tokens_back(residual_grad, dq, dk, dv, wq, wk, wv)
        sums = lax.psum(jnp.stack([sums2, sums1, sums0]), MESH_AXES)
        heads = lax.all_gather(head, MESH_AXES)

    vectors = lax.dynamic_slice(sums, (0, 0, fsdp * local), (3, 8, local))
    inner_bias_grad = lax.dynamic_slice(
        sums[1, 3 : 3 + ff // width].reshape(ff), (fsdp * (ff // shards),), (ff // shards,)
    )
    class_rows, pre_grads, pooled = heads[:, 0], heads[:, 1], heads[:, 2]
    logit_grads = heads[:, 3, :CLASSES]

    def own_columns(a):
        return lax.dynamic_slice(a, (0, fsdp * local), (a.shape[0], local))

    def over_rows(a, b):
        return lax.dot_general(a, b, (((0,), (0,)), ((), ())), preferred_element_type=F32)

    pooler_grad = over_rows(own_columns(class_rows), pre_grads)
    pooler_bias_grad = jnp.sum(own_columns(pre_grads).astype(F32), axis=0)
    class_grad = over_rows(own_columns(pooled), logit_grads)
    class_bias_grad = jnp.sum(logit_grads.astype(F32), axis=0)

    return (
        hidden[None],
        tokens_grad[None],
        loss[0, :1],
        query_grad,
        vectors[2, 0],
        key_grad,
        value_grad,
        vectors[2, 1],
        output_grad,
        vectors[1, 2],
        vectors[1, 0],
        vectors[1, 1],
        inner_weight_grad,
        inner_bias_grad,
        outer_grad,
        vectors[0, 2],
        vectors[0, 0],
        vectors[0, 1],
        pooler_grad,
        pooler_bias_grad,
        class_grad,
        class_bias_grad,
    )


def solution(mesh):
    sizes = dict(mesh.shape)
    by_links = sizes == {"dp": 4, "fsdp": 8}
    rows = P(MESH_AXES, None, None)
    ids = P(MESH_AXES, None)
    row = P(MESH_AXES)
    matrix = P("fsdp", None)
    vector = P("fsdp")
    return jax.shard_map(
        functools.partial(on_device, by_links),
        mesh=mesh,
        in_specs=(
            rows, rows, ids, row,
            matrix, vector, matrix, matrix, vector, matrix, vector, vector, vector,
            matrix, vector, matrix, vector, vector, vector, matrix, vector, matrix, P(),
        ),
        out_specs=(
            rows, rows, row,
            matrix, vector, matrix, matrix, vector, matrix, vector, vector, vector,
            matrix, vector, matrix, vector, vector, vector, matrix, vector, matrix, P(),
        ),
        check_vma=False,
    )
```

```python
import functools
import math

import jax
import jax.numpy as jnp
from jax import lax
from jax.experimental import pallas as pl
from jax.experimental.pallas import tpu as pltpu
from jax.sharding import PartitionSpec as P

HEAD_DIM = 64
CLASSES = 3
EPS = 1e-06
NEG = -1000000000.0
SCALE = HEAD_DIM**-0.5
LOW = jnp.bfloat16
F32 = jnp.float32
MESH_AXES = ("dp", "fsdp")
MIB = 1 << 20

QUERY_B, VALUE_B, OUTPUT_B, GAIN1, SHIFT1, OUTER_B, GAIN2, SHIFT2, POOLER_B, INNER_B, CLASS_W = (
    0, 1, 2, 3, 4, 5, 6, 7, 8, 9, 13,
)
TABLE = 16
COLUMNS = 384


def dot(a, b, dims=((1,), (0,))):
    return lax.dot_general(a, b, (dims, ((), ())), preferred_element_type=F32)


def dot_nt(a, b):
    return dot(a, b, ((1,), (1,)))


def full(shape):
    zeros = (0,) * len(shape)
    return pl.BlockSpec(shape, lambda *_: zeros, pipeline_mode=pl.Buffered(1))


def after(a, *others):
    return lax.optimization_barrier((a, *others))[0]


def call(kernel, outs, in_specs, out_specs, args, *, grid=(1,), scratch=(), prefetch=0, flops=0, moved=0, trans=0, vmem=20, name=None):
    return pl.pallas_call(
        kernel,
        name=name,
        out_shape=outs,
        grid_spec=pltpu.PrefetchScalarGridSpec(
            num_scalar_prefetch=prefetch,
            grid=grid,
            in_specs=in_specs,
            out_specs=out_specs,
            scratch_shapes=scratch,
        ),
        compiler_params=pltpu.CompilerParams(
            dimension_semantics=("arbitrary",) * len(grid), vmem_limit_bytes=vmem * MIB
        ),
        cost_estimate=pl.CostEstimate(flops=flops // 16, bytes_accessed=moved // 16, transcendentals=trans // 16),
    )(*args)


def shape(*dims, dtype=LOW):
    return jax.ShapeDtypeStruct(dims, dtype)


def lane_masks(rows):
    lanes = lax.broadcasted_iota(jnp.int32, (rows, 128), 1)
    return lanes < HEAD_DIM


def attention_kernel(tok, wq, wk, wv, table, seg_row, seg_col, q_o, k_o, v_o, ctx_o, lse_o, bias):
    step = pl.program_id(0)
    seq = tok.shape[0]

    @pl.when(step == 0)
    def _():
        bias[...] = jnp.where(seg_col[...] == seg_row[...], 0.0, NEG)

    x = tok[...]
    q = (dot(x, wq[...]) + table[QUERY_B : QUERY_B + 1, :]).astype(LOW)
    k = dot(x, wk[...]).astype(LOW)
    v = (dot(x, wv[...]) + table[VALUE_B : VALUE_B + 1, :]).astype(LOW)
    q_o[...] = q
    k_o[...] = k
    v_o[...] = v
    first = lane_masks(seq)
    zero = jnp.zeros((seq, 128), LOW)
    for pair in range(q.shape[1] // 128):
        cols = slice(pair * 128, pair * 128 + 128)
        q2, k2, v2t = q[:, cols], k[:, cols], v[:, cols].T
        parts = []
        for half in range(2):
            qm = jnp.where(first, q2, zero) if half == 0 else jnp.where(first, zero, q2)
            s = dot_nt(k2, qm) * SCALE + bias[...]
            top = jnp.max(s, axis=0, keepdims=True)
            e = jnp.exp(s - top)
            total = jnp.sum(e, axis=0, keepdims=True)
            out = dot(v2t[half * HEAD_DIM : (half + 1) * HEAD_DIM], e.astype(LOW)) / total
            parts.append(out)
            row = pair * 2 + half
            lse_o[0, row : row + 1, :] = top + jnp.log(total)
        ctx_o[:, cols] = jnp.concatenate(parts, axis=0).astype(LOW).T


def attention(tokens, wq, wk, wv, table, segments):
    seq, width = tokens.shape
    blk = 256
    steps = width // blk
    cols = pl.BlockSpec((seq, blk), lambda i: (0, i))
    wcols = pl.BlockSpec((width, blk), lambda i: (0, i))
    return call(
        attention_kernel,
        (shape(seq, width),) * 4 + (shape(steps, 8, seq, dtype=F32),),
        [full((seq, width)), wcols, wcols, wcols, pl.BlockSpec((TABLE, blk), lambda i: (0, i)), full((1, seq)), full((seq, 1))],
        (cols,) * 4 + (pl.BlockSpec((1, 8, seq), lambda i: (i, 0, 0)),),
        (tokens, wq, wk, wv, table, segments.reshape(1, seq), segments.reshape(seq, 1)),
        grid=(steps,),
        scratch=[pltpu.VMEM((seq, seq), F32)],
        flops=2 * seq * width * (3 * width + 2 * seq),
        moved=8 * seq * width + 6 * width * width,
        trans=seq * seq * width // HEAD_DIM,
        name="attention",
    )


def rows_norm(v):
    mean = jnp.mean(v, axis=-1, keepdims=True)
    centered = v - mean
    variance = jnp.mean(centered * centered, axis=-1, keepdims=True)
    scale = lax.rsqrt(variance + EPS)
    return centered * scale, scale


def attended_kernel(ctx, wo, tok, table, n1_o, r1_o, low_o):
    v = dot(ctx[...], wo[...]) + table[OUTPUT_B : OUTPUT_B + 1, :] + tok[...].astype(F32)
    n, r = rows_norm(v)
    n1_o[...] = n
    r1_o[...] = r
    low_o[...] = (n * table[GAIN1 : GAIN1 + 1, :] + table[SHIFT1 : SHIFT1 + 1, :]).astype(LOW)


def attended(ctx, wo, tokens, table):
    seq, width = tokens.shape
    blk = 128
    rows = pl.BlockSpec((blk, width), lambda i: (i, 0))
    return call(
        attended_kernel,
        (shape(seq, width, dtype=F32), shape(seq, 1, dtype=F32), shape(seq, width)),
        [rows, full((width, width)), rows, full((TABLE, width))],
        (rows, pl.BlockSpec((blk, 1), lambda i: (i, 0)), rows),
        (ctx, wo, tokens, table),
        grid=(seq // blk,),
        flops=2 * seq * width * width,
        moved=2 * width * width + 10 * seq * width,
        name="attended",
    )


ERFC_POLY = (
    0.2820605933666229,
    0.28293782472610474,
    0.237934872508049,
    0.22901807725429535,
    -0.10879392176866531,
    0.44148358702659607,
    -0.6950507164001465,
    0.44817423820495605,
    -0.13161660730838776,
    0.013852047733962536,
)


def gelu_parts(v):
    u = jnp.abs(v) * (0.5**0.5)
    t = 1.0 / (1.0 + 0.5 * u)
    poly = jnp.full_like(t, ERFC_POLY[-1])
    for coefficient in ERFC_POLY[-2::-1]:
        poly = poly * t + coefficient
    bell = jnp.exp(v * v * -0.5)
    tail = (0.5 * t) * poly * bell
    below = jnp.where(v < 0, tail, 1.0 - tail)
    return v * below, below + v * (bell * 0.3989422804014327)


def inner_kernel(low, wi, bi, act_o, slope_o):
    v = dot(low[...], wi[...]) + bi[...]
    act, slope = gelu_parts(v)
    act_o[...] = act.astype(LOW)
    slope_o[...] = slope.astype(LOW)


def inner(low, wi, bi):
    seq, width = low.shape
    ff = wi.shape[1]
    blk = 512
    cols = pl.BlockSpec((seq, blk), lambda i: (0, i))
    return call(
        inner_kernel,
        (shape(seq, ff), shape(seq, ff)),
        [full((seq, width)), pl.BlockSpec((width, blk), lambda i: (0, i)), pl.BlockSpec((1, blk), lambda i: (0, i))],
        (cols, cols),
        (low, wi, bi),
        grid=(ff // blk,),
        flops=2 * seq * width * ff,
        moved=2 * width * ff + 4 * seq * ff,
        trans=2 * seq * ff,
        name="inner",
    )


def outer_kernel(labels, bias3, act, w, n1, table, out_grad, wp, hid_o, sg_o, bg_o, sums_o, head_o, loss_o, acc, n2_s, r2_s):
    step = pl.program_id(0)
    seq, width = n1.shape

    @pl.when(step == 0)
    def _():
        acc[...] = jnp.zeros_like(acc)

    acc[...] += dot(act[...], w[...])

    @pl.when(step == pl.num_programs(0) - 1)
    def _():
        def row(at):
            return table[at : at + 1, :]

        gain2, shift2 = row(GAIN2), row(SHIFT2)
        blk = 64
        for at in range(0, seq, blk):
            rows = slice(at, at + blk)
            v = acc[rows, :] + row(OUTER_B) + (n1[rows, :] * row(GAIN1) + row(SHIFT1))
            n, r = rows_norm(v)
            n2_s[rows, :] = n
            r2_s[rows, :] = r
            hid_o[rows, :] = (n * gain2 + shift2).astype(LOW)
        class_rows = hid_o[0:8, :]
        pooled_pre = dot(class_rows, wp[...])[0:1, :] + row(POOLER_B)
        bent = jnp.tanh(pooled_pre)
        pooled = bent.astype(LOW).astype(F32)
        logits = [
            jnp.sum(pooled * row(CLASS_W + j), axis=-1, keepdims=True) + bias3[j] for j in range(CLASSES)
        ]
        top = functools.reduce(jnp.maximum, logits)
        exps = [jnp.exp(v - top) for v in logits]
        total = functools.reduce(jnp.add, exps)
        label = labels[0]
        hot = [jnp.where(label == j, 1.0, 0.0) for j in range(CLASSES)]
        picked = functools.reduce(jnp.add, [a * b for a, b in zip(logits, hot)])
        loss_o[...] = jnp.broadcast_to(top + jnp.log(total) - picked, loss_o.shape)
        slopes = [(e / total - o).astype(LOW).astype(F32) for e, o in zip(exps, hot)]
        pooled_grad = functools.reduce(
            jnp.add, [g * row(CLASS_W + j) for j, g in enumerate(slopes)]
        )
        pre_grad = (pooled_grad * (1.0 - bent * bent)).astype(LOW)
        row_grad = dot_nt(jnp.broadcast_to(pre_grad, (8, width)), wp[...])[0:1, :]
        head_o[...] = jnp.zeros_like(head_o)
        lanes = lax.broadcasted_iota(jnp.int32, (1, width), 1)
        head_o[0:1, :] = class_rows[0:1, :].astype(F32)
        head_o[1:2, :] = pre_grad.astype(F32)
        head_o[2:3, :] = pooled
        head_o[3:4, :] = functools.reduce(
            jnp.add, [jnp.where(lanes == j, g, 0.0) for j, g in enumerate(slopes)]
        )
        gain_sum = jnp.zeros((1, width), F32)
        shift_sum = jnp.zeros((1, width), F32)
        bias_sum = jnp.zeros((1, width), F32)
        for at in range(0, seq, blk):
            rows = slice(at, at + blk)
            fg = out_grad[rows, :].astype(F32)
            if at == 0:
                lead = lax.broadcasted_iota(jnp.int32, (blk, width), 0) == 0
                fg = fg + jnp.where(lead, jnp.broadcast_to(row_grad, (blk, width)), 0.0)
            n = n2_s[rows, :]
            g = fg * gain2
            gm = jnp.mean(g, axis=-1, keepdims=True)
            gn = jnp.mean(g * n, axis=-1, keepdims=True)
            sg = r2_s[rows, :] * (g - gm - n * gn)
            low = sg.astype(LOW)
            sg_o[rows, :] = sg
            bg_o[rows, :] = low
            gain_sum += jnp.sum(fg * n, axis=0, keepdims=True)
            shift_sum += jnp.sum(fg, axis=0, keepdims=True)
            bias_sum += jnp.sum(low.astype(F32), axis=0, keepdims=True)
        sums_o[...] = jnp.zeros_like(sums_o)
        sums_o[0:1, :] = gain_sum
        sums_o[1:2, :] = shift_sum
        sums_o[2:3, :] = bias_sum


def outer(act, w, n1, table, out_grad, wp, labels, bias3):
    seq, width = n1.shape
    ff = act.shape[1]
    blk = 512
    whole = full((seq, width))
    return call(
        outer_kernel,
        (
            shape(seq, width),
            shape(seq, width, dtype=F32),
            shape(seq, width),
            shape(8, width, dtype=F32),
            shape(8, width, dtype=F32),
            shape(8, 128, dtype=F32),
        ),
        [
            pl.BlockSpec((seq, blk), lambda i, *_: (0, i)),
            pl.BlockSpec((blk, width), lambda i, *_: (i, 0)),
            whole,
            full((TABLE, width)),
            whole,
            full((width, width)),
        ],
        (whole, whole, whole, full((8, width)), full((8, width)), full((8, 128))),
        (labels, bias3, act, w, n1, table, out_grad, wp),
        grid=(ff // blk,),
        scratch=[pltpu.VMEM((seq, width), F32), pltpu.VMEM((seq, width), F32), pltpu.VMEM((seq, 1), F32)],
        prefetch=2,
        flops=2 * seq * width * ff,
        moved=2 * width * ff + 2 * seq * ff + 14 * seq * width,
        name="outer",
    )


def inner_grad_kernel(bg, w_out, slope, ig_o):
    ig_o[...] = (dot_nt(bg[...], w_out[...]) * slope[...].astype(F32)).astype(LOW)


def inner_grads(bg, w_out, slope):
    seq, width = bg.shape
    ff = slope.shape[1]
    blk = 512
    cols = pl.BlockSpec((seq, blk), lambda i: (0, i))
    return call(
        inner_grad_kernel,
        shape(seq, ff),
        [full((seq, width)), pl.BlockSpec((blk, width), lambda i: (i, 0)), cols],
        cols,
        (bg, w_out, slope),
        grid=(ff // blk,),
        flops=2 * seq * width * ff,
        moved=2 * width * ff + 4 * seq * ff,
        name="inner_grads",
    )


def inner_back_kernel(ig, w_in, sg, n1, r1, table, res_o, ag_o, sums_o, acc, ib):
    step = pl.program_id(0)
    seq, width = n1.shape
    blk = ig.shape[1]
    ib[:, pl.ds(pl.multiple_of(step * blk, blk), blk)] = jnp.sum(ig[...].astype(F32), axis=0, keepdims=True)

    @pl.when(step == 0)
    def _():
        acc[...] = jnp.zeros_like(acc)

    acc[...] += dot_nt(ig[...], w_in[...])

    @pl.when(step == pl.num_programs(0) - 1)
    def _():
        gain1 = table[GAIN1 : GAIN1 + 1, :]
        gain_sum = jnp.zeros((1, width), F32)
        shift_sum = jnp.zeros((1, width), F32)
        bias_sum = jnp.zeros((1, width), F32)
        blk = 64
        for at in range(0, seq, blk):
            rows = slice(at, at + blk)
            fg = sg[rows, :] + acc[rows, :]
            n = n1[rows, :]
            g = fg * gain1
            gm = jnp.mean(g, axis=-1, keepdims=True)
            gn = jnp.mean(g * n, axis=-1, keepdims=True)
            res = r1[rows, :] * (g - gm - n * gn)
            low = res.astype(LOW)
            res_o[rows, :] = res
            ag_o[rows, :] = low
            gain_sum += jnp.sum(fg * n, axis=0, keepdims=True)
            shift_sum += jnp.sum(fg, axis=0, keepdims=True)
            bias_sum += jnp.sum(low.astype(F32), axis=0, keepdims=True)
        sums_o[...] = jnp.zeros_like(sums_o)
        sums_o[0:1, :] = gain_sum
        sums_o[1:2, :] = shift_sum
        sums_o[2:3, :] = bias_sum
        for at in range(ib.shape[1] // width):
            sums_o[3 + at : 4 + at, :] = ib[:, at * width : (at + 1) * width]


def inner_back(ig, w_in, sg, n1, r1, table):
    seq, width = n1.shape
    ff = ig.shape[1]
    blk = 512
    whole = full((seq, width))
    return call(
        inner_back_kernel,
        (shape(seq, width, dtype=F32), shape(seq, width), shape(8, width, dtype=F32)),
        [
            pl.BlockSpec((seq, blk), lambda i: (0, i)),
            pl.BlockSpec((width, blk), lambda i: (0, i)),
            whole,
            whole,
            full((seq, 1)),
            full((TABLE, width)),
        ],
        (whole, whole, full((8, width))),
        (ig, w_in, sg, n1, r1, table),
        grid=(ff // blk,),
        scratch=[pltpu.VMEM((seq, width), F32), pltpu.VMEM((1, ff), F32)],
        flops=2 * seq * width * ff,
        moved=2 * width * ff + 2 * seq * ff + 16 * seq * width,
        name="inner_back",
    )


def attention_back_kernel(q, k, v, lse, ag, wo, seg_row, seg_col, dq_o, dk_o, dv_o, sums_o, bias):
    seq = ag.shape[0]

    @pl.when(pl.program_id(0) == 0)
    def _():
        bias[...] = jnp.where(seg_col[...] == seg_row[...], 0.0, NEG)

    grad = dot_nt(ag[...], wo[...]).astype(LOW)
    first = lane_masks(seq)
    zero = jnp.zeros((seq, 128), LOW)
    sums_o[...] = jnp.zeros_like(sums_o)
    for pair in range(q.shape[1] // 128):
        cols = slice(pair * 128, pair * 128 + 128)
        q2, k2, v2, g2 = q[:, cols], k[:, cols], v[:, cols], grad[:, cols]
        k2t = k2.T
        dqs, dks, dvs = [], [], []
        for half in range(2):
            def own(a):
                return jnp.where(first, a, zero) if half == 0 else jnp.where(first, zero, a)

            row = pair * 2 + half
            s = dot_nt(k2, own(q2)) * SCALE + bias[...]
            p = jnp.exp(s - lse[0, row : row + 1, :])
            dp = dot_nt(v2, own(g2))
            weighted = p * dp
            level = jnp.sum(weighted, axis=0, keepdims=True)
            ds = (weighted - p * level).astype(LOW)
            dvs.append(dot(p.astype(LOW), g2))
            dks.append(dot(ds, q2))
            dqs.append(dot(k2t[half * HEAD_DIM : (half + 1) * HEAD_DIM], ds))
        dq = (jnp.concatenate(dqs, axis=0) * SCALE).astype(LOW).T
        dk = (jnp.where(first, dks[0], dks[1]) * SCALE).astype(LOW)
        dv = jnp.where(first, dvs[0], dvs[1]).astype(LOW)
        dq_o[:, cols] = dq
        dk_o[:, cols] = dk
        dv_o[:, cols] = dv
        sums_o[0:1, cols] = jnp.sum(dq.astype(F32), axis=0, keepdims=True)
        sums_o[1:2, cols] = jnp.sum(dv.astype(F32), axis=0, keepdims=True)


def attention_back(q, k, v, lse, ag, wo, segments, begin, count):
    seq, width = ag.shape
    blk = 256
    begin, steps = begin // blk, count // blk
    cols = pl.BlockSpec((seq, blk), lambda i: (0, i + begin))
    out = pl.BlockSpec((seq, blk), lambda i: (0, i))
    return call(
        attention_back_kernel,
        (shape(seq, count),) * 3 + (shape(8, count, dtype=F32),),
        [
            cols,
            cols,
            cols,
            pl.BlockSpec((1, 8, seq), lambda i: (i + begin, 0, 0)),
            full((seq, width)),
            pl.BlockSpec((blk, width), lambda i: (i + begin, 0)),
            full((1, seq)),
            full((seq, 1)),
        ],
        (out,) * 3 + (pl.BlockSpec((8, blk), lambda i: (0, i)),),
        (q, k, v, lse, ag, wo, segments.reshape(1, seq), segments.reshape(seq, 1)),
        grid=(steps,),
        scratch=[pltpu.VMEM((seq, seq), F32)],
        flops=2 * seq * count * (width + 5 * seq),
        moved=16 * seq * count + 2 * width * count,
        trans=seq * seq * count // HEAD_DIM,
        name="attention_back",
    )


def tokens_back_kernel(res, dq, dk, dv, wq, wk, wv, out):
    out[...] = res[...] + dot_nt(dq[...], wq[...]) + dot_nt(dk[...], wk[...]) + dot_nt(dv[...], wv[...])


def tokens_back(res, dq, dk, dv, wq, wk, wv):
    seq, width = res.shape
    blk = 128
    rows = pl.BlockSpec((blk, width), lambda i: (i, 0))
    weight = full((width, width))
    return call(
        tokens_back_kernel,
        shape(seq, width, dtype=F32),
        [rows] * 4 + [weight] * 3,
        rows,
        (res, dq, dk, dv, wq, wk, wv),
        grid=(seq // blk,),
        flops=6 * seq * width * width,
        moved=14 * seq * width + 6 * width * width,
        name="tokens_back",
    )


def grads(name, where, lefts, which, rights, add=None):
    seq = lefts[0].shape[0]
    parts = lefts[0].shape[1] // 16
    widths = tuple((w, r.shape[1] // 2) for w, r in zip(which, rights))
    total = sum(w for _, w in widths)
    half = (lambda i, where: (0, 1 - where[3])) if add is None else (lambda i, where: (0, where[3]))
    specs = [full(a.shape) for a in lefts]
    specs += [pl.BlockSpec((seq, w), half, pipeline_mode=pl.Buffered(1)) for _, w in widths]
    args = [where, *lefts, *rights]
    piece = (4, parts * total // COLUMNS, COLUMNS)
    outs = ((4, *piece),) if add is None else (piece,) * 4
    if add is not None:
        specs.append(full(add.shape))
        args.append(add)

    def kernel(where, *refs):
        left_refs, refs = refs[: len(lefts)], refs[len(lefts) :]
        right_refs, refs = refs[: len(rights)], refs[len(rights) :]
        add_ref = None if add is None else refs[0]
        out_refs, turned = refs[: len(outs)] if add is None else refs[1 : 1 + len(outs)], refs[-len(lefts) :]
        x, y, z0 = where[0], where[1], where[2]
        for left, store in zip(left_refs, turned):
            for start in range(0, left.shape[1], 256):
                store[start : start + 256, :] = left[:, start : start + 256].T
        for place in range(4):
            hh = jnp.bitwise_xor(x, place // 2)
            yy = jnp.bitwise_xor(y, place % 2)
            top = 0
            for (at, width), right in zip(widths, right_refs):
                rows = []
                for dz in range(4):
                    shard = jnp.bitwise_xor(z0, dz) * 2 + yy
                    rows.append(turned[at][pl.ds(pl.multiple_of((shard * 2 + hh) * parts, 16), parts), :])
                got = dot(jnp.concatenate(rows, axis=0), right[...]).reshape(4, parts, width)
                for column in range(0, width, COLUMNS):
                    one = got[:, :, column : column + COLUMNS]
                    if add is None:
                        out_refs[0][place, :, top : top + parts, :] = one.astype(LOW)
                    else:
                        one = one + add_ref[place, :, top : top + parts, :].astype(F32)
                        out_refs[place][:, top : top + parts, :] = one.astype(LOW)
                    top += parts

    got = call(
        kernel,
        tuple(shape(*o) for o in outs),
        specs,
        tuple(full(o) for o in outs),
        args,
        scratch=[pltpu.VMEM((a.shape[1], seq), LOW) for a in lefts],
        prefetch=1,
        flops=2 * seq * 16 * parts * total,
        moved=2 * 16 * parts * total + 2 * seq * 16 * parts,
        name=name,
    )
    return got[0] if add is None else got


def pack_kernel(where, wq, wk, wv, wo, wi, wf, wp, small, own_a, own_b, own_c):
    for out, weights in ((own_a, (wq, wk, wv)), (own_b, (wo, wi))):
        left = 0
        for ref in weights:
            out[: ref.shape[0], left : left + ref.shape[1]] = ref[...]
            left += ref.shape[1]
    at = wq.shape[0]
    own_a[at:, :] = jnp.zeros((8, own_a.shape[1]), LOW)
    for top in range(0, small.shape[0], 8):
        own_a[at:, top * 16 : top * 16 + small.shape[1]] = small[top : top + 8, :]
    rows = wf.shape[0]
    own_c[:rows, :] = wf[...]
    own_c[rows:, :] = wp[...]


def pack(where, wq, wk, wv, wo, wi, wf, wp, small):
    rows, width = wq.shape
    deep = wf.shape[0] // 2
    ff = wi.shape[1]
    outs = (shape(rows // 2 + 8, 3 * width // 2), shape(rows // 2, (width + ff) // 2), shape(deep + rows // 2, width // 2))
    weights = (wq, wk, wv, wo, wi, wf, wp)
    quarters = [
        pl.BlockSpec((w.shape[0] // 2, w.shape[1] // 2), lambda i, where: (where[0], where[3])) for w in weights
    ]
    return call(
        pack_kernel,
        outs,
        quarters + [full(small.shape)],
        tuple(full(o.shape) for o in outs),
        (where, *(pltpu.with_memory_space_constraint(w, pltpu.HBM) for w in weights), small),
        prefetch=1,
        moved=4 * sum(math.prod(o.shape) for o in outs),
        vmem=8,
        name="pack",
    )


def weights_kernel(spans, where, *refs):
    pieces, outs, sem = refs[:8], refs[8:-1], refs[-1]
    copies = []
    for place in range(8):
        hh = jnp.bitwise_xor(where[0], place // 4)
        yy = jnp.bitwise_xor(where[1], place // 2 % 2)
        cc = jnp.bitwise_xor(where[3], place % 2)
        for dz in range(4):
            zz = jnp.bitwise_xor(where[2], dz)
            for (top, rows, left, width), out in zip(spans, outs):
                to = out.at[zz, yy, hh, :, pl.ds(pl.multiple_of(cc * width, 128), width)]
                come = pieces[place].at[dz, top : top + rows, left : left + width]
                copies.append(pltpu.make_async_copy(come, to, sem.at[len(copies)]))
    for one in copies:
        one.start()
    for one in copies:
        one.wait()


def place_weights(where, pieces, spans):
    anywhere = pl.BlockSpec(memory_space=pl.ANY)
    outs = call(
        functools.partial(weights_kernel, tuple(spans)),
        tuple(shape(4, 2, 2, rows, 2 * width) for _, rows, _, width in spans),
        [anywhere] * 8,
        (anywhere,) * len(spans),
        (where, *(pltpu.with_memory_space_constraint(p, pltpu.VMEM) for p in pieces)),
        scratch=[pltpu.SemaphoreType.DMA((32 * len(spans),))],
        prefetch=1,
        moved=4 * 8 * pieces[0].size,
        vmem=4,
        name="place_weights",
    )
    return [o.reshape(16 * rows, 2 * width) for o, (_, rows, _, width) in zip(outs, spans)]


def shards_kernel(spans, where, *refs):
    pieces, outs = refs[:4], refs[4:]
    for place in range(4):
        hh = jnp.bitwise_xor(where[0], place // 2)
        for core in range(2):

            @pl.when(jnp.bitwise_xor(where[3], place % 2) == core)
            def _():
                for (top, rows, blocks), out in zip(spans, outs):
                    for block in range(blocks):
                        left = (core * blocks + block) * COLUMNS
                        out[hh, :, left : left + COLUMNS] = pieces[place][
                            top + block * rows : top + (block + 1) * rows, :
                        ].astype(F32)


def place_shards(where, pieces, spans):
    sizes = [(2, rows, 2 * blocks * COLUMNS) for _, rows, blocks in spans]
    outs = call(
        functools.partial(shards_kernel, tuple(spans)),
        tuple(shape(*size, dtype=F32) for size in sizes),
        [full(pieces[0].shape)] * 4,
        tuple(full(size) for size in sizes),
        (where, *pieces),
        prefetch=1,
        moved=24 * pieces[0].size,
        vmem=12,
        name="place_shards",
    )
    return [o.reshape(2 * size[1], size[2]) for o, size in zip(outs, sizes)]


def device(x, core, z, y):
    return (x * 2 + core) * 8 + z * 2 + y


ALL = [(x, core, z, y) for x in range(2) for core in range(2) for z in range(4) for y in range(2)]
CORE_SWAP = [(device(*a), device(a[0], 1 - a[1], a[2], a[3])) for a in ALL]
X_SWAP = [(device(*a), device(1 - a[0], a[1], a[2], a[3])) for a in ALL]
Y_SWAP = [(device(*a), device(a[0], a[1], a[2], 1 - a[3])) for a in ALL]
Z_SWAPS = [[(device(*a), device(a[0], a[1], a[2] ^ d, a[3])) for a in ALL] for d in range(4)]
X_CORE_SWAP = [(device(*a), device(1 - a[0], 1 - a[1], a[2], a[3])) for a in ALL]
XY_SWAP = [(device(*a), device(1 - a[0], a[1], a[2], 1 - a[3])) for a in ALL]


def swap(a, pairs):
    return lax.ppermute(a, MESH_AXES, pairs)


def wide(*arrays):
    return functools.reduce(jnp.add, [a.astype(F32) for a in arrays])


def along_z(own):
    return [swap(own, Z_SWAPS[d]) for d in (1, 2, 3)]


def to_core(arrays):
    return [swap(a, CORE_SWAP) for a in arrays]


def together(*groups):
    leaves, tree = jax.tree.flatten(groups)
    return jax.tree.unflatten(tree, lax.optimization_barrier(tuple(leaves)))


def low(a):
    return a.astype(LOW)


def sums_by_z(parts):
    return [wide(*(p[d] for p in parts)) for d in range(4)]


def on_device(
    by_links,
    tokens,
    out_grad,
    segment_ids,
    labels,
    query_weight,
    query_bias,
    key_weight,
    value_weight,
    value_bias,
    output_weight,
    output_bias,
    first_norm_gain,
    first_norm_shift,
    inner_weight,
    inner_bias,
    outer_weight,
    outer_bias,
    second_norm_gain,
    second_norm_shift,
    pooler_weight,
    pooler_bias,
    class_weight,
    class_bias,
):
    _, seq, width = tokens.shape
    tokens = tokens.reshape(seq, width)
    out_grad = out_grad.reshape(seq, width)
    dp, fsdp = lax.axis_index("dp"), lax.axis_index("fsdp")
    where = jnp.stack([dp // 2, fsdp % 2, fsdp // 2, dp % 2]).astype(jnp.int32)
    local = query_bias.shape[0]
    shards = width // local
    ff = inner_weight.shape[1]

    small = jnp.concatenate(
        [
            jnp.stack(
                [
                    query_bias,
                    value_bias,
                    output_bias,
                    first_norm_gain,
                    first_norm_shift,
                    outer_bias,
                    second_norm_gain,
                    second_norm_shift,
                    pooler_bias,
                ]
            ),
            inner_bias.reshape(ff // width, local),
            class_weight.T,
        ]
    )

    def tables(got):
        table = jnp.transpose(got, (1, 0, 2)).reshape(TABLE, width)
        return table, got[:, INNER_B:CLASS_W, :].reshape(1, ff)

    bias3 = class_bias.astype(F32)
    if by_links:
        own_a, own_b, own_c = pack(
            where,
            query_weight,
            key_weight,
            value_weight,
            output_weight,
            inner_weight,
            outer_weight,
            pooler_weight,
            small,
        )
        parts, deep = local // 2, outer_weight.shape[0] // 2
        spans_a = [(0, parts, at * (width // 2), width // 2) for at in range(3)]
        spans_b = [(0, parts, 0, width // 2), (0, parts, width // 2, ff // 2)]
        spans_c = [(0, deep, 0, width // 2), (deep, parts, 0, width // 2)]

        def mixed(near, other):
            return [a for pair in zip(near, other) for a in pair]

        z_a = along_z(own_a)
        (z_a, own_a, own_b, own_c) = together(z_a, own_a, own_b, own_c)
        z_b = along_z(own_b)
        far_a = jnp.stack([own_a, *z_a])
        x_a, y_a = swap(far_a, X_SWAP), swap(far_a, Y_SWAP)
        (far_a, x_a, y_a, z_b, own_b, own_c) = together(far_a, x_a, y_a, z_b, own_b, own_c)
        z_c = along_z(own_c)
        far_b = jnp.stack([own_b, *z_b])
        xy_a = swap(x_a, Y_SWAP)
        x_b = swap(far_b, X_SWAP)
        (core_a,) = to_core([jnp.concatenate([far_a, y_a, x_a])])
        order = [((where[2] ^ d) * 2 + (where[1] ^ e)) for e in range(2) for d in range(4)]
        spread = (jnp.stack(order)[None, :] == jnp.arange(shards)[:, None]).astype(LOW)
        small = jnp.concatenate([far_a[:, parts:, :256], y_a[:, parts:, :256]])
        small = jnp.concatenate([small[:, :, :local], small[:, :, 128 : 128 + local]], axis=1)
        table, inner_row = tables(jnp.einsum("sp,pji->sji", spread, small, preferred_element_type=F32))
        (far_a, y_a, x_a, xy_a, far_b, x_b, z_c, core_a, own_c, table, inner_row) = together(
            far_a, y_a, x_a, xy_a, far_b, x_b, z_c, core_a, own_c, table, inner_row
        )
        y_b = swap(far_b, Y_SWAP)
        far_c = jnp.stack([own_c, *z_c])
        x_c = swap(far_c, X_SWAP)
        core_a = [core_a[:4], core_a[4:8], core_a[8:]] + to_core([xy_a])
        wq, wk, wv = place_weights(where, mixed((far_a, y_a, x_a, xy_a), core_a), spans_a)
        q, k, v, context, lse = attention(tokens, wq, wk, wv, table, segment_ids)
        (q, k, v, context, lse, far_b, x_b, y_b, far_c, x_c) = together(
            q, k, v, context, lse, far_b, x_b, y_b, far_c, x_c
        )
        xy_b = swap(y_b, X_SWAP)
        y_c = swap(far_c, Y_SWAP)
        core_b = to_core([far_b, y_b, x_b])
        (far_b, y_b, x_b, xy_b, core_b, far_c, x_c, y_c) = together(
            far_b, y_b, x_b, xy_b, core_b, far_c, x_c, y_c
        )
        xy_c = swap(x_c, Y_SWAP)
        core_b += to_core([xy_b])
        core_c = to_core([far_c, y_c, x_c])
        wo, wi = place_weights(where, mixed((far_b, y_b, x_b, xy_b), core_b), spans_b)
        n1, r1, first_low = attended(context, wo, tokens, table)
        activated, slope = inner(first_low, wi, inner_row)
        (far_c, y_c, x_c, xy_c, core_c, activated, slope) = together(
            far_c, y_c, x_c, xy_c, core_c, activated, slope
        )
        core_c += to_core([xy_c])
        wf, wp = place_weights(where, mixed((far_c, y_c, x_c, xy_c), core_c), spans_c)
    else:
        wq, wk, wv, wo, wp, wi, wf = (
            lax.all_gather(w, "fsdp", axis=0, tiled=True)
            for w in (
                query_weight,
                key_weight,
                value_weight,
                output_weight,
                pooler_weight,
                inner_weight,
                outer_weight,
            )
        )
        table, inner_row = tables(lax.all_gather(small, "fsdp").astype(F32))
        q, k, v, context, lse = attention(tokens, wq, wk, wv, table, segment_ids)
        n1, r1, first_low = attended(context, wo, tokens, table)
        activated, slope = inner(first_low, wi, inner_row)

    hidden, second_grad, branch_grad, sums2, head, loss = outer(
        activated, wf, n1, table, out_grad, wp, labels, bias3
    )
    def attention_step(attended_grad, begin, count):
        return attention_back(q, k, v, lse, attended_grad, wo, segment_ids, begin, count)

    cut = 512
    if by_links:

        def gathered(heads, pairs):
            return jnp.concatenate([heads, swap(heads, pairs)])

        heads = low(head)[None]

        def plane(parts):
            same, y, x, xy = parts
            return [same, swap(x, X_SWAP), swap(y, Y_SWAP), swap(xy, XY_SWAP)]

        other = grads("outer_grad_a", where, [activated], [0], [branch_grad])
        (other, branch_grad) = together(other, branch_grad)
        other, heads = swap(other, CORE_SWAP), gathered(heads, Z_SWAPS[1])
        inner_grad = inner_grads(branch_grad, wf, slope)
        (other, inner_grad, heads) = together(other, inner_grad, heads)
        mine = grads("outer_grad_b", where, [activated], [0], [branch_grad], other)
        (mine, inner_grad, heads) = together(mine, inner_grad, heads)
        same_f, y_f, x_f, xy_f = mine
        from_x, from_y = swap(x_f[:2], X_SWAP), swap(y_f[:2], Y_SWAP)
        heads = gathered(gathered(heads, Z_SWAPS[2]), Y_SWAP)
        residual_grad, attended_grad, sums1 = inner_back(inner_grad, wi, second_grad, n1, r1, table)
        (attended_grad, inner_grad) = together(attended_grad, inner_grad)
        lefts, rights = [context, first_low], [attended_grad, inner_grad]
        other = grads("inner_grad_a", where, lefts, [0, 1], rights)
        (other, attended_grad, from_x, from_y, x_f, y_f, xy_f, heads) = together(
            other, attended_grad, from_x, from_y, x_f[2:], y_f[2:], xy_f, heads
        )
        other = swap(other, CORE_SWAP)
        x_f, y_f, xy_f = swap(x_f, X_SWAP), swap(y_f, Y_SWAP), swap(xy_f, XY_SWAP)
        heads = gathered(heads, X_SWAP)
        back_a = attention_step(attended_grad, 0, cut)
        (other, back_a, attended_grad, heads) = together(other, back_a, attended_grad, heads)
        mine = grads("inner_grad_b", where, lefts, [0, 1], rights, other)
        (mine, attended_grad, heads) = together(mine, attended_grad, heads)
        heads = gathered(heads, CORE_SWAP)
        back_b = attention_step(attended_grad, cut, width - cut)
        dq, dk, dv, sums0 = (jnp.concatenate([a, b], axis=1) for a, b in zip(back_a, back_b))
        rights = [dq, dk, dv]
        other = grads("query_grad_a", where, [tokens], [0, 0, 0], rights)
        sums = jnp.stack([sums2, sums1, sums0])
        (other, dq, dk, dv, sums, x_f, y_f, xy_f, mine, heads) = together(
            other, dq, dk, dv, sums, x_f, y_f, xy_f, mine, heads
        )
        rights = [dq, dk, dv]
        parts_i = plane(mine)
        other = swap(other, CORE_SWAP)
        totals_f = [wide(same_f[d], xy_f[d], from_x[d], from_y[d]) for d in range(2)]
        totals_f += [wide(same_f[2 + d], xy_f[2 + d], x_f[d], y_f[d]) for d in range(2)]
        odd_f = swap(low(jnp.stack([totals_f[1], totals_f[3]])), Z_SWAPS[1])
        mine = grads("query_grad_b", where, [tokens], [0, 0, 0], rights, other)
        (mine, odd_f, even_f, dq, dk, dv, sums, heads) = together(
            mine, odd_f, [totals_f[0], totals_f[2]], dq, dk, dv, sums, heads
        )
        go_f = swap(low(wide(even_f[1], odd_f[1])), Z_SWAPS[2])
        sums = sums + swap(sums, Z_SWAPS[1])
        tokens_grad = tokens_back(residual_grad, dq, dk, dv, wq, wk, wv)
        (parts_i, mine, go_f, stay_f, tokens_grad, heads, sums) = together(
            parts_i, mine, go_f, wide(even_f[0], odd_f[0]), tokens_grad, heads, sums
        )
        parts_q = plane(mine)
        totals_i = sums_by_z(parts_i)
        odd_i = swap(low(jnp.stack([totals_i[1], totals_i[3]])), Z_SWAPS[1])
        own_f = low(wide(stay_f, go_f))
        sums = sums + swap(sums, Z_SWAPS[2])
        (odd_i, even_i, own_f, sums, heads) = together(odd_i, [totals_i[0], totals_i[2]], own_f, sums, heads)
        go_i = swap(low(wide(even_i[1], odd_i[1])), Z_SWAPS[2])
        sums = sums + swap(sums, X_SWAP)
        (parts_q, go_i, stay_i, own_f, sums, heads) = together(
            parts_q, go_i, wide(even_i[0], odd_i[0]), own_f, sums, heads
        )
        totals_q = sums_by_z(parts_q)
        z_q = [swap(low(totals_q[d]), Z_SWAPS[d]) for d in (1, 2, 3)]
        own = jnp.concatenate([own_f, low(wide(stay_i, go_i))])
        across = swap(own, X_SWAP)
        sums = sums + swap(sums, Y_SWAP)
        (z_q, own_q, own, across, sums, heads) = together(z_q, totals_q[0], own, across, sums, heads)
        sums = sums + swap(sums, CORE_SWAP)
        core = swap(jnp.stack([own, across]), CORE_SWAP)
        own_q = low(wide(own_q, *z_q))
        all_q = [own_q, swap(own_q, CORE_SWAP), swap(own_q, X_SWAP), swap(own_q, X_CORE_SWAP)]
        outer_grad, output_grad, inner_weight_grad = place_shards(
            where,
            [own, core[0], across, core[1]],
            [(0, deep, 1), (deep, parts, 1), (deep + parts, parts, ff // width)],
        )
        query_grad, key_grad, value_grad = place_shards(where, all_q, [(at * parts, parts, 1) for at in range(3)])
    else:

        def reduced(left, right):
            local_grad = lax.dot_general(left, right, (((0,), (0,)), ((), ())), preferred_element_type=F32)
            shard = lax.psum_scatter(local_grad, "fsdp", scatter_dimension=0, tiled=True)
            return lax.psum(low(shard), "dp").astype(F32)

        inner_grad = inner_grads(branch_grad, wf, slope)
        residual_grad, attended_grad, sums1 = inner_back(inner_grad, wi, second_grad, n1, r1, table)
        dq, dk, dv, sums0 = attention_step(attended_grad, 0, width)
        outer_grad = reduced(activated, branch_grad)
        inner_weight_grad = reduced(first_low, inner_grad)
        output_grad = reduced(context, attended_grad)
        query_grad, key_grad, value_grad = (reduced(tokens, d) for d in (dq, dk, dv))
        tokens_grad = tokens_back(residual_grad, dq, dk, dv, wq, wk, wv)
        sums = lax.psum(jnp.stack([sums2, sums1, sums0]), MESH_AXES)
        heads = lax.all_gather(head, MESH_AXES)

    vectors = lax.dynamic_slice(sums, (0, 0, fsdp * local), (3, 8, local))
    inner_bias_grad = lax.dynamic_slice(
        sums[1, 3 : 3 + ff // width].reshape(ff), (fsdp * (ff // shards),), (ff // shards,)
    )
    class_rows, pre_grads, pooled = heads[:, 0], heads[:, 1], heads[:, 2]
    logit_grads = heads[:, 3, :CLASSES]

    def own_columns(a):
        return lax.dynamic_slice(a, (0, fsdp * local), (a.shape[0], local))

    def over_rows(a, b):
        return lax.dot_general(a, b, (((0,), (0,)), ((), ())), preferred_element_type=F32)

    pooler_grad = over_rows(own_columns(class_rows), pre_grads)
    pooler_bias_grad = jnp.sum(own_columns(pre_grads).astype(F32), axis=0)
    class_grad = over_rows(own_columns(pooled), logit_grads)
    class_bias_grad = jnp.sum(logit_grads.astype(F32), axis=0)

    return (
        hidden[None],
        tokens_grad[None],
        loss[0, :1],
        query_grad,
        vectors[2, 0],
        key_grad,
        value_grad,
        vectors[2, 1],
        output_grad,
        vectors[1, 2],
        vectors[1, 0],
        vectors[1, 1],
        inner_weight_grad,
        inner_bias_grad,
        outer_grad,
        vectors[0, 2],
        vectors[0, 0],
        vectors[0, 1],
        pooler_grad,
        pooler_bias_grad,
        class_grad,
        class_bias_grad,
    )


def solution(mesh):
    sizes = dict(mesh.shape)
    by_links = sizes == {"dp": 4, "fsdp": 8}
    rows = P(MESH_AXES, None, None)
    ids = P(MESH_AXES, None)
    row = P(MESH_AXES)
    matrix = P("fsdp", None)
    vector = P("fsdp")
    return jax.shard_map(
        functools.partial(on_device, by_links),
        mesh=mesh,
        in_specs=(
            rows, rows, ids, row,
            matrix, vector, matrix, matrix, vector, matrix, vector, vector, vector,
            matrix, vector, matrix, vector, vector, vector, matrix, vector, matrix, P(),
        ),
        out_specs=(
            rows, rows, row,
            matrix, vector, matrix, matrix, vector, matrix, vector, vector, vector,
            matrix, vector, matrix, vector, vector, vector, matrix, vector, matrix, P(),
        ),
        check_vma=False,
    )
```

```python
import functools
import math

import jax
import jax.numpy as jnp
from jax import lax
from jax.experimental import pallas as pl
from jax.experimental.pallas import tpu as pltpu
from jax.sharding import PartitionSpec as P

HEAD_DIM = 64
CLASSES = 3
EPS = 1e-06
NEG = -1000000000.0
SCALE = HEAD_DIM**-0.5
LOW = jnp.bfloat16
F32 = jnp.float32
MESH_AXES = ("dp", "fsdp")
MIB = 1 << 20

QUERY_B, VALUE_B, OUTPUT_B, GAIN1, SHIFT1, OUTER_B, GAIN2, SHIFT2, POOLER_B, INNER_B, CLASS_W = (
    0, 1, 2, 3, 4, 5, 6, 7, 8, 9, 13,
)
TABLE = 16
COLUMNS = 384


def dot(a, b, dims=((1,), (0,))):
    return lax.dot_general(a, b, (dims, ((), ())), preferred_element_type=F32)


def dot_nt(a, b):
    return dot(a, b, ((1,), (1,)))


def full(shape):
    zeros = (0,) * len(shape)
    return pl.BlockSpec(shape, lambda *_: zeros, pipeline_mode=pl.Buffered(1))


def after(a, *others):
    return lax.optimization_barrier((a, *others))[0]


def call(kernel, outs, in_specs, out_specs, args, *, grid=(1,), scratch=(), prefetch=0, flops=0, moved=0, trans=0, vmem=20, name=None):
    return pl.pallas_call(
        kernel,
        name=name,
        out_shape=outs,
        grid_spec=pltpu.PrefetchScalarGridSpec(
            num_scalar_prefetch=prefetch,
            grid=grid,
            in_specs=in_specs,
            out_specs=out_specs,
            scratch_shapes=scratch,
        ),
        compiler_params=pltpu.CompilerParams(
            dimension_semantics=("arbitrary",) * len(grid), vmem_limit_bytes=vmem * MIB
        ),
        cost_estimate=pl.CostEstimate(flops=flops // 16, bytes_accessed=moved // 16, transcendentals=trans // 16),
    )(*args)


def shape(*dims, dtype=LOW):
    return jax.ShapeDtypeStruct(dims, dtype)


def lane_masks(rows):
    lanes = lax.broadcasted_iota(jnp.int32, (rows, 128), 1)
    return lanes < HEAD_DIM


def attention_kernel(tok, wq, wk, wv, table, seg_row, seg_col, q_o, k_o, v_o, ctx_o, lse_o, bias):
    step = pl.program_id(0)
    seq = tok.shape[0]

    @pl.when(step == 0)
    def _():
        bias[...] = jnp.where(seg_col[...] == seg_row[...], 0.0, NEG)

    x = tok[...]
    q = (dot(x, wq[...]) + table[QUERY_B : QUERY_B + 1, :]).astype(LOW)
    k = dot(x, wk[...]).astype(LOW)
    v = (dot(x, wv[...]) + table[VALUE_B : VALUE_B + 1, :]).astype(LOW)
    q_o[...] = q
    k_o[...] = k
    v_o[...] = v
    first = lane_masks(seq)
    zero = jnp.zeros((seq, 128), LOW)
    for pair in range(q.shape[1] // 128):
        cols = slice(pair * 128, pair * 128 + 128)
        q2, k2, v2t = q[:, cols], k[:, cols], v[:, cols].T
        parts = []
        for half in range(2):
            qm = jnp.where(first, q2, zero) if half == 0 else jnp.where(first, zero, q2)
            s = dot_nt(k2, qm) * SCALE + bias[...]
            top = jnp.max(s, axis=0, keepdims=True)
            e = jnp.exp(s - top)
            total = jnp.sum(e, axis=0, keepdims=True)
            out = dot(v2t[half * HEAD_DIM : (half + 1) * HEAD_DIM], e.astype(LOW)) / total
            parts.append(out)
            row = pair * 2 + half
            lse_o[0, row : row + 1, :] = top + jnp.log(total)
        ctx_o[:, cols] = jnp.concatenate(parts, axis=0).astype(LOW).T


def attention(tokens, wq, wk, wv, table, segments):
    seq, width = tokens.shape
    blk = 256
    steps = width // blk
    cols = pl.BlockSpec((seq, blk), lambda i: (0, i))
    wcols = pl.BlockSpec((width, blk), lambda i: (0, i))
    return call(
        attention_kernel,
        (shape(seq, width),) * 4 + (shape(steps, 8, seq, dtype=F32),),
        [full((seq, width)), wcols, wcols, wcols, pl.BlockSpec((TABLE, blk), lambda i: (0, i)), full((1, seq)), full((seq, 1))],
        (cols,) * 4 + (pl.BlockSpec((1, 8, seq), lambda i: (i, 0, 0)),),
        (tokens, wq, wk, wv, table, segments.reshape(1, seq), segments.reshape(seq, 1)),
        grid=(steps,),
        scratch=[pltpu.VMEM((seq, seq), F32)],
        flops=2 * seq * width * (3 * width + 2 * seq),
        moved=8 * seq * width + 6 * width * width,
        trans=seq * seq * width // HEAD_DIM,
        name="attention",
    )


def rows_norm(v):
    mean = jnp.mean(v, axis=-1, keepdims=True)
    centered = v - mean
    variance = jnp.mean(centered * centered, axis=-1, keepdims=True)
    scale = lax.rsqrt(variance + EPS)
    return centered * scale, scale


def attended_kernel(ctx, wo, tok, table, n1_o, r1_o, low_o):
    v = dot(ctx[...], wo[...]) + table[OUTPUT_B : OUTPUT_B + 1, :] + tok[...].astype(F32)
    n, r = rows_norm(v)
    n1_o[...] = n
    r1_o[...] = r
    low_o[...] = (n * table[GAIN1 : GAIN1 + 1, :] + table[SHIFT1 : SHIFT1 + 1, :]).astype(LOW)


def attended(ctx, wo, tokens, table):
    seq, width = tokens.shape
    blk = 128
    rows = pl.BlockSpec((blk, width), lambda i: (i, 0))
    return call(
        attended_kernel,
        (shape(seq, width, dtype=F32), shape(seq, 1, dtype=F32), shape(seq, width)),
        [rows, full((width, width)), rows, full((TABLE, width))],
        (rows, pl.BlockSpec((blk, 1), lambda i: (i, 0)), rows),
        (ctx, wo, tokens, table),
        grid=(seq // blk,),
        flops=2 * seq * width * width,
        moved=2 * width * width + 10 * seq * width,
        name="attended",
    )


ERFC_POLY = (
    0.14103029668331146,
    0.14146891236305237,
    0.1189674362540245,
    0.11450903862714767,
    -0.05439696088433266,
    0.22074179351329803,
    -0.34752535820007324,
    0.22408711910247803,
    -0.06580830365419388,
    0.006926023866981268,
)


def gelu_parts(v):
    t = 1.0 / (1.0 + (0.5 * 0.5**0.5) * jnp.abs(v))
    poly = ERFC_POLY[-1] * t + ERFC_POLY[-2]
    for coefficient in ERFC_POLY[-3::-1]:
        poly = poly * t + coefficient
    bell = jnp.exp2(v * v * (-0.5 * math.log2(math.e)))
    tail = t * poly * bell
    below = jnp.where(v < 0, tail, 1.0 - tail)
    return v * below, below + v * (bell * (2 * math.pi) ** -0.5)


def inner_kernel(low, wi, bi, act_o, slope_o):
    v = dot(low[...], wi[...]) + bi[...]
    act, slope = gelu_parts(v)
    act_o[...] = act.astype(LOW)
    slope_o[...] = slope.astype(LOW)


def inner(low, wi, bi):
    seq, width = low.shape
    ff = wi.shape[1]
    blk = 512
    cols = pl.BlockSpec((seq, blk), lambda i: (0, i))
    return call(
        inner_kernel,
        (shape(seq, ff), shape(seq, ff)),
        [full((seq, width)), pl.BlockSpec((width, blk), lambda i: (0, i)), pl.BlockSpec((1, blk), lambda i: (0, i))],
        (cols, cols),
        (low, wi, bi),
        grid=(ff // blk,),
        flops=2 * seq * width * ff,
        moved=2 * width * ff + 4 * seq * ff,
        trans=2 * seq * ff,
        name="inner",
    )


def outer_kernel(labels, bias3, act, w, n1, table, out_grad, wp, hid_o, sg_o, bg_o, sums_o, head_o, loss_o, acc, n2_s, r2_s):
    step = pl.program_id(0)
    seq, width = n1.shape

    @pl.when(step == 0)
    def _():
        acc[...] = jnp.zeros_like(acc)

    acc[...] += dot(act[...], w[...])

    @pl.when(step == pl.num_programs(0) - 1)
    def _():
        def row(at):
            return table[at : at + 1, :]

        gain2, shift2 = row(GAIN2), row(SHIFT2)
        blk = 64
        for at in range(0, seq, blk):
            rows = slice(at, at + blk)
            v = acc[rows, :] + row(OUTER_B) + (n1[rows, :] * row(GAIN1) + row(SHIFT1))
            n, r = rows_norm(v)
            n2_s[rows, :] = n
            r2_s[rows, :] = r
            hid_o[rows, :] = (n * gain2 + shift2).astype(LOW)
        class_rows = hid_o[0:8, :]
        pooled_pre = dot(class_rows, wp[...])[0:1, :] + row(POOLER_B)
        bent = jnp.tanh(pooled_pre)
        pooled = bent.astype(LOW).astype(F32)
        logits = [
            jnp.sum(pooled * row(CLASS_W + j), axis=-1, keepdims=True) + bias3[j] for j in range(CLASSES)
        ]
        top = functools.reduce(jnp.maximum, logits)
        exps = [jnp.exp(v - top) for v in logits]
        total = functools.reduce(jnp.add, exps)
        label = labels[0]
        hot = [jnp.where(label == j, 1.0, 0.0) for j in range(CLASSES)]
        picked = functools.reduce(jnp.add, [a * b for a, b in zip(logits, hot)])
        loss_o[...] = jnp.broadcast_to(top + jnp.log(total) - picked, loss_o.shape)
        slopes = [(e / total - o).astype(LOW).astype(F32) for e, o in zip(exps, hot)]
        pooled_grad = functools.reduce(
            jnp.add, [g * row(CLASS_W + j) for j, g in enumerate(slopes)]
        )
        pre_grad = (pooled_grad * (1.0 - bent * bent)).astype(LOW)
        row_grad = dot_nt(jnp.broadcast_to(pre_grad, (8, width)), wp[...])[0:1, :]
        head_o[...] = jnp.zeros_like(head_o)
        lanes = lax.broadcasted_iota(jnp.int32, (1, width), 1)
        head_o[0:1, :] = class_rows[0:1, :].astype(F32)
        head_o[1:2, :] = pre_grad.astype(F32)
        head_o[2:3, :] = pooled
        head_o[3:4, :] = functools.reduce(
            jnp.add, [jnp.where(lanes == j, g, 0.0) for j, g in enumerate(slopes)]
        )
        gain_sum = jnp.zeros((1, width), F32)
        shift_sum = jnp.zeros((1, width), F32)
        bias_sum = jnp.zeros((1, width), F32)
        for at in range(0, seq, blk):
            rows = slice(at, at + blk)
            fg = out_grad[rows, :].astype(F32)
            if at == 0:
                lead = lax.broadcasted_iota(jnp.int32, (blk, width), 0) == 0
                fg = fg + jnp.where(lead, jnp.broadcast_to(row_grad, (blk, width)), 0.0)
            n = n2_s[rows, :]
            g = fg * gain2
            gm = jnp.mean(g, axis=-1, keepdims=True)
            gn = jnp.mean(g * n, axis=-1, keepdims=True)
            sg = r2_s[rows, :] * (g - gm - n * gn)
            low = sg.astype(LOW)
            sg_o[rows, :] = sg
            bg_o[rows, :] = low
            gain_sum += jnp.sum(fg * n, axis=0, keepdims=True)
            shift_sum += jnp.sum(fg, axis=0, keepdims=True)
            bias_sum += jnp.sum(low.astype(F32), axis=0, keepdims=True)
        sums_o[...] = jnp.zeros_like(sums_o)
        sums_o[0:1, :] = gain_sum
        sums_o[1:2, :] = shift_sum
        sums_o[2:3, :] = bias_sum


def outer(act, w, n1, table, out_grad, wp, labels, bias3):
    seq, width = n1.shape
    ff = act.shape[1]
    blk = 1536
    whole = full((seq, width))
    return call(
        outer_kernel,
        (
            shape(seq, width),
            shape(seq, width, dtype=F32),
            shape(seq, width),
            shape(8, width, dtype=F32),
            shape(8, width, dtype=F32),
            shape(8, 128, dtype=F32),
        ),
        [
            pl.BlockSpec((seq, blk), lambda i, *_: (0, i)),
            pl.BlockSpec((blk, width), lambda i, *_: (i, 0)),
            whole,
            full((TABLE, width)),
            whole,
            full((width, width)),
        ],
        (whole, whole, whole, full((8, width)), full((8, width)), full((8, 128))),
        (labels, bias3, act, w, n1, table, out_grad, wp),
        grid=(ff // blk,),
        scratch=[pltpu.VMEM((seq, width), F32), pltpu.VMEM((seq, width), F32), pltpu.VMEM((seq, 1), F32)],
        prefetch=2,
        flops=2 * seq * width * ff,
        moved=2 * width * ff + 2 * seq * ff + 14 * seq * width,
        name="outer",
    )


def inner_grad_kernel(bg, w_out, slope, ig_o):
    ig_o[...] = (dot_nt(bg[...], w_out[...]) * slope[...].astype(F32)).astype(LOW)


def inner_grads(bg, w_out, slope):
    seq, width = bg.shape
    ff = slope.shape[1]
    blk = 1024
    cols = pl.BlockSpec((seq, blk), lambda i: (0, i))
    return call(
        inner_grad_kernel,
        shape(seq, ff),
        [full((seq, width)), pl.BlockSpec((blk, width), lambda i: (i, 0)), cols],
        cols,
        (bg, w_out, slope),
        grid=(ff // blk,),
        flops=2 * seq * width * ff,
        moved=2 * width * ff + 4 * seq * ff,
        name="inner_grads",
    )


def inner_back_kernel(ig, w_in, sg, n1, r1, table, res_o, ag_o, sums_o, acc, ib):
    step = pl.program_id(0)
    seq, width = n1.shape
    blk = ig.shape[1]
    ib[:, pl.ds(pl.multiple_of(step * blk, blk), blk)] = jnp.sum(ig[...].astype(F32), axis=0, keepdims=True)

    @pl.when(step == 0)
    def _():
        acc[...] = jnp.zeros_like(acc)

    acc[...] += dot_nt(ig[...], w_in[...])

    @pl.when(step == pl.num_programs(0) - 1)
    def _():
        gain1 = table[GAIN1 : GAIN1 + 1, :]
        gain_sum = jnp.zeros((1, width), F32)
        shift_sum = jnp.zeros((1, width), F32)
        bias_sum = jnp.zeros((1, width), F32)
        blk = 64
        for at in range(0, seq, blk):
            rows = slice(at, at + blk)
            fg = sg[rows, :] + acc[rows, :]
            n = n1[rows, :]
            g = fg * gain1
            gm = jnp.mean(g, axis=-1, keepdims=True)
            gn = jnp.mean(g * n, axis=-1, keepdims=True)
            res = r1[rows, :] * (g - gm - n * gn)
            low = res.astype(LOW)
            res_o[rows, :] = res
            ag_o[rows, :] = low
            gain_sum += jnp.sum(fg * n, axis=0, keepdims=True)
            shift_sum += jnp.sum(fg, axis=0, keepdims=True)
            bias_sum += jnp.sum(low.astype(F32), axis=0, keepdims=True)
        sums_o[...] = jnp.zeros_like(sums_o)
        sums_o[0:1, :] = gain_sum
        sums_o[1:2, :] = shift_sum
        sums_o[2:3, :] = bias_sum
        for at in range(ib.shape[1] // width):
            sums_o[3 + at : 4 + at, :] = ib[:, at * width : (at + 1) * width]


def inner_back(ig, w_in, sg, n1, r1, table):
    seq, width = n1.shape
    ff = ig.shape[1]
    blk = 1536
    whole = full((seq, width))
    return call(
        inner_back_kernel,
        (shape(seq, width, dtype=F32), shape(seq, width), shape(8, width, dtype=F32)),
        [
            pl.BlockSpec((seq, blk), lambda i: (0, i)),
            pl.BlockSpec((width, blk), lambda i: (0, i)),
            whole,
            whole,
            full((seq, 1)),
            full((TABLE, width)),
        ],
        (whole, whole, full((8, width))),
        (ig, w_in, sg, n1, r1, table),
        grid=(ff // blk,),
        scratch=[pltpu.VMEM((seq, width), F32), pltpu.VMEM((1, ff), F32)],
        flops=2 * seq * width * ff,
        moved=2 * width * ff + 2 * seq * ff + 16 * seq * width,
        name="inner_back",
    )


def attention_back_kernel(q, k, v, lse, ag, wo, seg_row, seg_col, dq_o, dk_o, dv_o, sums_o, bias):
    seq = ag.shape[0]

    @pl.when(pl.program_id(0) == 0)
    def _():
        bias[...] = jnp.where(seg_col[...] == seg_row[...], 0.0, NEG)

    grad = dot_nt(ag[...], wo[...]).astype(LOW)
    first = lane_masks(seq)
    zero = jnp.zeros((seq, 128), LOW)
    sums_o[...] = jnp.zeros_like(sums_o)
    for pair in range(q.shape[1] // 128):
        cols = slice(pair * 128, pair * 128 + 128)
        q2, k2, v2, g2 = q[:, cols], k[:, cols], v[:, cols], grad[:, cols]
        k2t = k2.T
        dqs, dks, dvs = [], [], []
        for half in range(2):
            def own(a):
                return jnp.where(first, a, zero) if half == 0 else jnp.where(first, zero, a)

            row = pair * 2 + half
            s = dot_nt(k2, own(q2)) * SCALE + bias[...]
            p = jnp.exp(s - lse[0, row : row + 1, :])
            dp = dot_nt(v2, own(g2))
            weighted = p * dp
            level = jnp.sum(weighted, axis=0, keepdims=True)
            ds = (weighted - p * level).astype(LOW)
            dvs.append(dot(p.astype(LOW), g2))
            dks.append(dot(ds, q2))
            dqs.append(dot(k2t[half * HEAD_DIM : (half + 1) * HEAD_DIM], ds))
        dq = (jnp.concatenate(dqs, axis=0) * SCALE).astype(LOW).T
        dk = (jnp.where(first, dks[0], dks[1]) * SCALE).astype(LOW)
        dv = jnp.where(first, dvs[0], dvs[1]).astype(LOW)
        dq_o[:, cols] = dq
        dk_o[:, cols] = dk
        dv_o[:, cols] = dv
        sums_o[0:1, cols] = jnp.sum(dq.astype(F32), axis=0, keepdims=True)
        sums_o[1:2, cols] = jnp.sum(dv.astype(F32), axis=0, keepdims=True)


def attention_back(q, k, v, lse, ag, wo, segments, begin, count):
    seq, width = ag.shape
    blk = 256
    begin, steps = begin // blk, count // blk
    cols = pl.BlockSpec((seq, blk), lambda i: (0, i + begin))
    out = pl.BlockSpec((seq, blk), lambda i: (0, i))
    return call(
        attention_back_kernel,
        (shape(seq, count),) * 3 + (shape(8, count, dtype=F32),),
        [
            cols,
            cols,
            cols,
            pl.BlockSpec((1, 8, seq), lambda i: (i + begin, 0, 0)),
            full((seq, width)),
            pl.BlockSpec((blk, width), lambda i: (i + begin, 0)),
            full((1, seq)),
            full((seq, 1)),
        ],
        (out,) * 3 + (pl.BlockSpec((8, blk), lambda i: (0, i)),),
        (q, k, v, lse, ag, wo, segments.reshape(1, seq), segments.reshape(seq, 1)),
        grid=(steps,),
        scratch=[pltpu.VMEM((seq, seq), F32)],
        flops=2 * seq * count * (width + 5 * seq),
        moved=16 * seq * count + 2 * width * count,
        trans=seq * seq * count // HEAD_DIM,
        name="attention_back",
    )


def tokens_back_kernel(res, dq, dk, dv, wq, wk, wv, out):
    out[...] = res[...] + dot_nt(dq[...], wq[...]) + dot_nt(dk[...], wk[...]) + dot_nt(dv[...], wv[...])


def tokens_back(res, dq, dk, dv, wq, wk, wv):
    seq, width = res.shape
    blk = 128
    rows = pl.BlockSpec((blk, width), lambda i: (i, 0))
    weight = full((width, width))
    return call(
        tokens_back_kernel,
        shape(seq, width, dtype=F32),
        [rows] * 4 + [weight] * 3,
        rows,
        (res, dq, dk, dv, wq, wk, wv),
        grid=(seq // blk,),
        flops=6 * seq * width * width,
        moved=14 * seq * width + 6 * width * width,
        name="tokens_back",
    )


def grads(name, where, lefts, which, rights, add=None):
    seq = lefts[0].shape[0]
    parts = lefts[0].shape[1] // 16
    widths = tuple((w, r.shape[1] // 2) for w, r in zip(which, rights))
    total = sum(w for _, w in widths)
    half = (lambda i, where: (0, 1 - where[3])) if add is None else (lambda i, where: (0, where[3]))
    specs = [full(a.shape) for a in lefts]
    specs += [pl.BlockSpec((seq, w), half, pipeline_mode=pl.Buffered(1)) for _, w in widths]
    args = [where, *lefts, *rights]
    piece = (4, parts * total // COLUMNS, COLUMNS)
    outs = ((4, *piece),) if add is None else (piece,) * 4
    if add is not None:
        specs.append(full(add.shape))
        args.append(add)

    def kernel(where, *refs):
        left_refs, refs = refs[: len(lefts)], refs[len(lefts) :]
        right_refs, refs = refs[: len(rights)], refs[len(rights) :]
        add_ref = None if add is None else refs[0]
        out_refs, turned = refs[: len(outs)] if add is None else refs[1 : 1 + len(outs)], refs[-len(lefts) :]
        x, y, z0 = where[0], where[1], where[2]
        for left, store in zip(left_refs, turned):
            for start in range(0, left.shape[1], 256):
                store[start : start + 256, :] = left[:, start : start + 256].T
        for place in range(4):
            hh = jnp.bitwise_xor(x, place // 2)
            yy = jnp.bitwise_xor(y, place % 2)
            top = 0
            for (at, width), right in zip(widths, right_refs):
                rows = []
                for dz in range(4):
                    shard = jnp.bitwise_xor(z0, dz) * 2 + yy
                    rows.append(turned[at][pl.ds(pl.multiple_of((shard * 2 + hh) * parts, 16), parts), :])
                got = dot(jnp.concatenate(rows, axis=0), right[...]).reshape(4, parts, width)
                for column in range(0, width, COLUMNS):
                    one = got[:, :, column : column + COLUMNS]
                    if add is None:
                        out_refs[0][place, :, top : top + parts, :] = one.astype(LOW)
                    else:
                        one = one + add_ref[place, :, top : top + parts, :].astype(F32)
                        out_refs[place][:, top : top + parts, :] = one.astype(LOW)
                    top += parts

    got = call(
        kernel,
        tuple(shape(*o) for o in outs),
        specs,
        tuple(full(o) for o in outs),
        args,
        scratch=[pltpu.VMEM((a.shape[1], seq), LOW) for a in lefts],
        prefetch=1,
        flops=2 * seq * 16 * parts * total,
        moved=2 * 16 * parts * total + 2 * seq * 16 * parts,
        name=name,
    )
    return got[0] if add is None else got


def pack_kernel(where, wq, wk, wv, wo, wi, wf, wp, small, own_a, own_b, own_c):
    for out, weights in ((own_a, (wq, wk, wv)), (own_b, (wo, wi))):
        left = 0
        for ref in weights:
            out[: ref.shape[0], left : left + ref.shape[1]] = ref[...]
            left += ref.shape[1]
    at = wq.shape[0]
    own_a[at:, :] = jnp.zeros((8, own_a.shape[1]), LOW)
    for top in range(0, small.shape[0], 8):
        own_a[at:, top * 16 : top * 16 + small.shape[1]] = small[top : top + 8, :]
    rows = wf.shape[0]
    own_c[:rows, :] = wf[...]
    own_c[rows:, :] = wp[...]


def pack(where, wq, wk, wv, wo, wi, wf, wp, small):
    rows, width = wq.shape
    deep = wf.shape[0] // 2
    ff = wi.shape[1]
    outs = (shape(rows // 2 + 8, 3 * width // 2), shape(rows // 2, (width + ff) // 2), shape(deep + rows // 2, width // 2))
    weights = (wq, wk, wv, wo, wi, wf, wp)
    quarters = [
        pl.BlockSpec((w.shape[0] // 2, w.shape[1] // 2), lambda i, where: (where[0], where[3])) for w in weights
    ]
    return call(
        pack_kernel,
        outs,
        quarters + [full(small.shape)],
        tuple(full(o.shape) for o in outs),
        (where, *(pltpu.with_memory_space_constraint(w, pltpu.HBM) for w in weights), small),
        prefetch=1,
        moved=4 * sum(math.prod(o.shape) for o in outs),
        vmem=8,
        name="pack",
    )


def weights_kernel(spans, places, where, *refs):
    pieces, outs, sem = refs[: len(places)], refs[-1 - len(spans) : -1], refs[-1]
    copies = []
    for place, piece in zip(places, pieces):
        hh = jnp.bitwise_xor(where[0], place // 4)
        yy = jnp.bitwise_xor(where[1], place // 2 % 2)
        cc = jnp.bitwise_xor(where[3], place % 2)
        for dz in range(4):
            zz = jnp.bitwise_xor(where[2], dz)
            for (top, rows, left, width), out in zip(spans, outs):
                to = out.at[zz, yy, hh, :, pl.ds(pl.multiple_of(cc * width, 128), width)]
                come = piece.at[dz, top : top + rows, left : left + width]
                copies.append(pltpu.make_async_copy(come, to, sem.at[len(copies)]))
    for one in copies:
        one.start()
    for one in copies:
        one.wait()


def place_some(where, pieces, spans, places, begun=()):
    anywhere = pl.BlockSpec(memory_space=pl.ANY)
    count = 1 + len(pieces)
    return pl.pallas_call(
        functools.partial(weights_kernel, tuple(spans), tuple(places)),
        name="place_weights",
        out_shape=tuple(shape(4, 2, 2, rows, 2 * width) for _, rows, _, width in spans),
        grid_spec=pltpu.PrefetchScalarGridSpec(
            num_scalar_prefetch=1,
            grid=(1,),
            in_specs=[anywhere] * (len(pieces) + len(begun)),
            out_specs=(anywhere,) * len(spans),
            scratch_shapes=[pltpu.SemaphoreType.DMA((4 * len(places) * len(spans),))],
        ),
        input_output_aliases={count + at: at for at in range(len(begun))},
        compiler_params=pltpu.CompilerParams(vmem_limit_bytes=4 * MIB),
        cost_estimate=pl.CostEstimate(flops=0, bytes_accessed=pieces[0].size, transcendentals=0),
    )(where, *pieces, *begun)


def place_weights(where, pieces, spans):
    begun = place_some(where, pieces[:6], spans, range(6))
    return finish_weights(where, begun, pieces[6:], spans)


def finish_weights(where, begun, pieces, spans):
    outs = place_some(where, pieces, spans, (6, 7), begun)
    return [o.reshape(16 * rows, 2 * width) for o, (_, rows, _, width) in zip(outs, spans)]


def shards_kernel(spans, where, *refs):
    pieces, outs = refs[:4], refs[4:]
    for place in range(4):
        hh = jnp.bitwise_xor(where[0], place // 2)
        for core in range(2):

            @pl.when(jnp.bitwise_xor(where[3], place % 2) == core)
            def _():
                for (top, rows, blocks), out in zip(spans, outs):
                    for block in range(blocks):
                        left = (core * blocks + block) * COLUMNS
                        out[hh, :, left : left + COLUMNS] = pieces[place][
                            top + block * rows : top + (block + 1) * rows, :
                        ].astype(F32)


def place_shards(where, pieces, spans):
    sizes = [(2, rows, 2 * blocks * COLUMNS) for _, rows, blocks in spans]
    outs = call(
        functools.partial(shards_kernel, tuple(spans)),
        tuple(shape(*size, dtype=F32) for size in sizes),
        [full(pieces[0].shape)] * 4,
        tuple(full(size) for size in sizes),
        (where, *pieces),
        prefetch=1,
        moved=24 * pieces[0].size,
        vmem=12,
        name="place_shards",
    )
    return [o.reshape(2 * size[1], size[2]) for o, size in zip(outs, sizes)]


def device(x, core, z, y):
    return (x * 2 + core) * 8 + z * 2 + y


ALL = [(x, core, z, y) for x in range(2) for core in range(2) for z in range(4) for y in range(2)]
CORE_SWAP = [(device(*a), device(a[0], 1 - a[1], a[2], a[3])) for a in ALL]
X_SWAP = [(device(*a), device(1 - a[0], a[1], a[2], a[3])) for a in ALL]
Y_SWAP = [(device(*a), device(a[0], a[1], a[2], 1 - a[3])) for a in ALL]
Z_SWAPS = [[(device(*a), device(a[0], a[1], a[2] ^ d, a[3])) for a in ALL] for d in range(4)]
X_CORE_SWAP = [(device(*a), device(1 - a[0], 1 - a[1], a[2], a[3])) for a in ALL]
XY_SWAP = [(device(*a), device(1 - a[0], a[1], a[2], 1 - a[3])) for a in ALL]


def swap(a, pairs):
    return lax.ppermute(a, MESH_AXES, pairs)


def wide(*arrays):
    return functools.reduce(jnp.add, [a.astype(F32) for a in arrays])


def along_z(own):
    return [swap(own, Z_SWAPS[d]) for d in (1, 2, 3)]


def to_core(arrays):
    return [swap(a, CORE_SWAP) for a in arrays]


def together(*groups):
    leaves, tree = jax.tree.flatten(groups)
    return jax.tree.unflatten(tree, lax.optimization_barrier(tuple(leaves)))


def low(a):
    return a.astype(LOW)


def sums_by_z(parts):
    return [wide(*(p[d] for p in parts)) for d in range(4)]


def on_device(
    by_links,
    tokens,
    out_grad,
    segment_ids,
    labels,
    query_weight,
    query_bias,
    key_weight,
    value_weight,
    value_bias,
    output_weight,
    output_bias,
    first_norm_gain,
    first_norm_shift,
    inner_weight,
    inner_bias,
    outer_weight,
    outer_bias,
    second_norm_gain,
    second_norm_shift,
    pooler_weight,
    pooler_bias,
    class_weight,
    class_bias,
):
    _, seq, width = tokens.shape
    tokens = tokens.reshape(seq, width)
    out_grad = out_grad.reshape(seq, width)
    dp, fsdp = lax.axis_index("dp"), lax.axis_index("fsdp")
    where = jnp.stack([dp // 2, fsdp % 2, fsdp // 2, dp % 2]).astype(jnp.int32)
    local = query_bias.shape[0]
    shards = width // local
    ff = inner_weight.shape[1]

    small = jnp.concatenate(
        [
            jnp.stack(
                [
                    query_bias,
                    value_bias,
                    output_bias,
                    first_norm_gain,
                    first_norm_shift,
                    outer_bias,
                    second_norm_gain,
                    second_norm_shift,
                    pooler_bias,
                ]
            ),
            inner_bias.reshape(ff // width, local),
            class_weight.T,
        ]
    )

    def tables(got):
        table = jnp.transpose(got, (1, 0, 2)).reshape(TABLE, width)
        return table, got[:, INNER_B:CLASS_W, :].reshape(1, ff)

    bias3 = class_bias.astype(F32)
    if by_links:
        own_a, own_b, own_c = pack(
            where,
            query_weight,
            key_weight,
            value_weight,
            output_weight,
            inner_weight,
            outer_weight,
            pooler_weight,
            small,
        )
        parts, deep = local // 2, outer_weight.shape[0] // 2
        spans_a = [(0, parts, at * (width // 2), width // 2) for at in range(3)]
        spans_b = [(0, parts, 0, width // 2), (0, parts, width // 2, ff // 2)]
        spans_c = [(0, deep, 0, width // 2), (deep, parts, 0, width // 2)]

        def mixed(near, other):
            return [a for pair in zip(near, other) for a in pair]

        z_a = along_z(own_a)
        (z_a, own_a, own_b, own_c) = together(z_a, own_a, own_b, own_c)
        z_b = along_z(own_b)
        far_a = jnp.stack([own_a, *z_a])
        x_a, y_a = swap(far_a, X_SWAP), swap(far_a, Y_SWAP)
        (far_a, x_a, y_a, z_b, own_b, own_c) = together(far_a, x_a, y_a, z_b, own_b, own_c)
        z_c = along_z(own_c)
        far_b = jnp.stack([own_b, *z_b])
        xy_a = swap(x_a, Y_SWAP)
        x_b = swap(far_b, X_SWAP)
        (core_a,) = to_core([jnp.concatenate([far_a, y_a, x_a])])
        order = [((where[2] ^ d) * 2 + (where[1] ^ e)) for e in range(2) for d in range(4)]
        spread = (jnp.stack(order)[None, :] == jnp.arange(shards)[:, None]).astype(LOW)
        small = jnp.concatenate([far_a[:, parts:, :256], y_a[:, parts:, :256]])
        small = jnp.concatenate([small[:, :, :local], small[:, :, 128 : 128 + local]], axis=1)
        table, inner_row = tables(jnp.einsum("sp,pji->sji", spread, small, preferred_element_type=F32))
        (far_a, y_a, x_a, xy_a, far_b, x_b, z_c, core_a, own_c, table, inner_row) = together(
            far_a, y_a, x_a, xy_a, far_b, x_b, z_c, core_a, own_c, table, inner_row
        )
        y_b = swap(far_b, Y_SWAP)
        far_c = jnp.stack([own_c, *z_c])
        x_c = swap(far_c, X_SWAP)
        core_a = [core_a[:4], core_a[4:8], core_a[8:]] + to_core([xy_a])
        wq, wk, wv = place_weights(where, mixed((far_a, y_a, x_a, xy_a), core_a), spans_a)
        q, k, v, context, lse = attention(tokens, wq, wk, wv, table, segment_ids)
        (q, k, v, context, lse, far_b, x_b, y_b, far_c, x_c) = together(
            q, k, v, context, lse, far_b, x_b, y_b, far_c, x_c
        )
        xy_b = swap(y_b, X_SWAP)
        y_c = swap(far_c, Y_SWAP)
        core_b = to_core([far_b, y_b, x_b])
        begun_b = place_some(where, mixed((far_b, y_b, x_b), core_b), spans_b, range(6))
        (xy_b, begun_b, far_c, x_c, y_c) = together(xy_b, begun_b, far_c, x_c, y_c)
        xy_c = swap(x_c, Y_SWAP)
        (core_xy_b,) = to_core([xy_b])
        core_c = to_core([far_c, y_c, x_c])
        wo, wi = finish_weights(where, begun_b, [xy_b, core_xy_b], spans_b)
        n1, r1, first_low = attended(context, wo, tokens, table)
        activated, slope = inner(first_low, wi, inner_row)
        begun_c = place_some(where, mixed((far_c, y_c, x_c), core_c), spans_c, range(6))
        (xy_c, begun_c, activated, slope) = together(xy_c, begun_c, activated, slope)
        wf, wp = finish_weights(where, begun_c, [xy_c, *to_core([xy_c])], spans_c)
    else:
        wq, wk, wv, wo, wp, wi, wf = (
            lax.all_gather(w, "fsdp", axis=0, tiled=True)
            for w in (
                query_weight,
                key_weight,
                value_weight,
                output_weight,
                pooler_weight,
                inner_weight,
                outer_weight,
            )
        )
        table, inner_row = tables(lax.all_gather(small, "fsdp").astype(F32))
        q, k, v, context, lse = attention(tokens, wq, wk, wv, table, segment_ids)
        n1, r1, first_low = attended(context, wo, tokens, table)
        activated, slope = inner(first_low, wi, inner_row)

    hidden, second_grad, branch_grad, sums2, head, loss = outer(
        activated, wf, n1, table, out_grad, wp, labels, bias3
    )
    def attention_step(attended_grad, begin, count):
        return attention_back(q, k, v, lse, attended_grad, wo, segment_ids, begin, count)

    cut = 512
    if by_links:

        def gathered(heads, pairs):
            return jnp.concatenate([heads, swap(heads, pairs)])

        heads = low(head)[None]

        def plane(parts):
            same, y, x, xy = parts
            return [same, swap(x, X_SWAP), swap(y, Y_SWAP), swap(xy, XY_SWAP)]

        other = grads("outer_grad_a", where, [activated], [0], [branch_grad])
        (other, branch_grad) = together(other, branch_grad)
        other, heads = swap(other, CORE_SWAP), gathered(heads, Z_SWAPS[1])
        inner_grad = inner_grads(branch_grad, wf, slope)
        (other, inner_grad, heads) = together(other, inner_grad, heads)
        mine = grads("outer_grad_b", where, [activated], [0], [branch_grad], other)
        (mine, inner_grad, heads) = together(mine, inner_grad, heads)
        same_f, y_f, x_f, xy_f = mine
        from_x, from_y = swap(x_f[:3], X_SWAP), swap(y_f[:3], Y_SWAP)
        heads = gathered(gathered(heads, Z_SWAPS[2]), Y_SWAP)
        residual_grad, attended_grad, sums1 = inner_back(inner_grad, wi, second_grad, n1, r1, table)
        (attended_grad, inner_grad) = together(attended_grad, inner_grad)
        lefts, rights = [context, first_low], [attended_grad, inner_grad]
        other = grads("inner_grad_a", where, lefts, [0, 1], rights)
        (other, attended_grad, from_x, from_y, x_f, y_f, xy_f, heads) = together(
            other, attended_grad, from_x, from_y, x_f[3], y_f[3], xy_f, heads
        )
        other = swap(other, CORE_SWAP)
        x_f, y_f, xy_f = swap(x_f, X_SWAP), swap(y_f, Y_SWAP), swap(xy_f, XY_SWAP)
        heads = gathered(heads, X_SWAP)
        back_a = attention_step(attended_grad, 0, cut)
        (other, back_a, attended_grad, heads) = together(other, back_a, attended_grad, heads)
        mine = grads("inner_grad_b", where, lefts, [0, 1], rights, other)
        (mine, attended_grad, heads) = together(mine, attended_grad, heads)
        heads = gathered(heads, CORE_SWAP)
        back_b = attention_step(attended_grad, cut, width - cut)
        dq, dk, dv, sums0 = (jnp.concatenate([a, b], axis=1) for a, b in zip(back_a, back_b))
        rights = [dq, dk, dv]
        other = grads("query_grad_a", where, [tokens], [0, 0, 0], rights)
        sums = jnp.stack([sums2, sums1, sums0])
        (other, dq, dk, dv, sums, x_f, y_f, xy_f, mine, heads) = together(
            other, dq, dk, dv, sums, x_f, y_f, xy_f, mine, heads
        )
        rights = [dq, dk, dv]
        parts_i = plane(mine)
        other = swap(other, CORE_SWAP)
        totals_f = [wide(same_f[d], xy_f[d], from_x[d], from_y[d]) for d in range(3)]
        totals_f.append(wide(same_f[3], xy_f[3], x_f, y_f))
        odd_f = swap(low(jnp.stack([totals_f[1], totals_f[3]])), Z_SWAPS[1])
        mine = grads("query_grad_b", where, [tokens], [0, 0, 0], rights, other)
        (mine, odd_f, even_f, dq, dk, dv, sums, heads) = together(
            mine, odd_f, [totals_f[0], totals_f[2]], dq, dk, dv, sums, heads
        )
        go_f = swap(low(wide(even_f[1], odd_f[1])), Z_SWAPS[2])
        sums = sums + swap(sums, Z_SWAPS[1])
        tokens_grad = tokens_back(residual_grad, dq, dk, dv, wq, wk, wv)
        (parts_i, mine, go_f, stay_f, tokens_grad, heads, sums) = together(
            parts_i, mine, go_f, wide(even_f[0], odd_f[0]), tokens_grad, heads, sums
        )
        parts_q = plane(mine)
        totals_i = sums_by_z(parts_i)
        odd_i = swap(low(jnp.stack([totals_i[1], totals_i[3]])), Z_SWAPS[1])
        own_f = low(wide(stay_f, go_f))
        sums = sums + swap(sums, Z_SWAPS[2])
        (odd_i, even_i, own_f, sums, heads) = together(odd_i, [totals_i[0], totals_i[2]], own_f, sums, heads)
        go_i = swap(low(wide(even_i[1], odd_i[1])), Z_SWAPS[2])
        sums = sums + swap(sums, X_SWAP)
        (parts_q, go_i, stay_i, own_f, sums, heads) = together(
            parts_q, go_i, wide(even_i[0], odd_i[0]), own_f, sums, heads
        )
        totals_q = sums_by_z(parts_q)
        z_q = [swap(low(totals_q[d]), Z_SWAPS[d]) for d in (1, 2, 3)]
        own = jnp.concatenate([own_f, low(wide(stay_i, go_i))])
        across = swap(own, X_SWAP)
        sums = sums + swap(sums, Y_SWAP)
        (z_q, own_q, own, across, sums, heads) = together(z_q, totals_q[0], own, across, sums, heads)
        sums = sums + swap(sums, CORE_SWAP)
        core = swap(jnp.stack([own, across]), CORE_SWAP)
        own_q = low(wide(own_q, *z_q))
        all_q = [own_q, swap(own_q, CORE_SWAP), swap(own_q, X_SWAP), swap(own_q, X_CORE_SWAP)]
        outer_grad, output_grad, inner_weight_grad = place_shards(
            where,
            [own, core[0], across, core[1]],
            [(0, deep, 1), (deep, parts, 1), (deep + parts, parts, ff // width)],
        )
        query_grad, key_grad, value_grad = place_shards(where, all_q, [(at * parts, parts, 1) for at in range(3)])
    else:

        def reduced(left, right):
            local_grad = lax.dot_general(left, right, (((0,), (0,)), ((), ())), preferred_element_type=F32)
            shard = lax.psum_scatter(local_grad, "fsdp", scatter_dimension=0, tiled=True)
            return lax.psum(low(shard), "dp").astype(F32)

        inner_grad = inner_grads(branch_grad, wf, slope)
        residual_grad, attended_grad, sums1 = inner_back(inner_grad, wi, second_grad, n1, r1, table)
        dq, dk, dv, sums0 = attention_step(attended_grad, 0, width)
        outer_grad = reduced(activated, branch_grad)
        inner_weight_grad = reduced(first_low, inner_grad)
        output_grad = reduced(context, attended_grad)
        query_grad, key_grad, value_grad = (reduced(tokens, d) for d in (dq, dk, dv))
        tokens_grad = tokens_back(residual_grad, dq, dk, dv, wq, wk, wv)
        sums = lax.psum(jnp.stack([sums2, sums1, sums0]), MESH_AXES)
        heads = lax.all_gather(head, MESH_AXES)

    vectors = lax.dynamic_slice(sums, (0, 0, fsdp * local), (3, 8, local))
    inner_bias_grad = lax.dynamic_slice(
        sums[1, 3 : 3 + ff // width].reshape(ff), (fsdp * (ff // shards),), (ff // shards,)
    )
    class_rows, pre_grads, pooled = heads[:, 0], heads[:, 1], heads[:, 2]
    logit_grads = heads[:, 3, :CLASSES]

    def own_columns(a):
        return lax.dynamic_slice(a, (0, fsdp * local), (a.shape[0], local))

    def over_rows(a, b):
        return lax.dot_general(a, b, (((0,), (0,)), ((), ())), preferred_element_type=F32)

    pooler_grad = over_rows(own_columns(class_rows), pre_grads)
    pooler_bias_grad = jnp.sum(own_columns(pre_grads).astype(F32), axis=0)
    class_grad = over_rows(own_columns(pooled), logit_grads)
    class_bias_grad = jnp.sum(logit_grads.astype(F32), axis=0)

    return (
        hidden[None],
        tokens_grad[None],
        loss[0, :1],
        query_grad,
        vectors[2, 0],
        key_grad,
        value_grad,
        vectors[2, 1],
        output_grad,
        vectors[1, 2],
        vectors[1, 0],
        vectors[1, 1],
        inner_weight_grad,
        inner_bias_grad,
        outer_grad,
        vectors[0, 2],
        vectors[0, 0],
        vectors[0, 1],
        pooler_grad,
        pooler_bias_grad,
        class_grad,
        class_bias_grad,
    )


def solution(mesh):
    sizes = dict(mesh.shape)
    by_links = sizes == {"dp": 4, "fsdp": 8}
    rows = P(MESH_AXES, None, None)
    ids = P(MESH_AXES, None)
    row = P(MESH_AXES)
    matrix = P("fsdp", None)
    vector = P("fsdp")
    return jax.shard_map(
        functools.partial(on_device, by_links),
        mesh=mesh,
        in_specs=(
            rows, rows, ids, row,
            matrix, vector, matrix, matrix, vector, matrix, vector, vector, vector,
            matrix, vector, matrix, vector, vector, vector, matrix, vector, matrix, P(),
        ),
        out_specs=(
            rows, rows, row,
            matrix, vector, matrix, matrix, vector, matrix, vector, vector, vector,
            matrix, vector, matrix, vector, vector, vector, matrix, vector, matrix, P(),
        ),
        check_vma=False,
    )
```

```python
import functools
import math

import jax
import jax.numpy as jnp
from jax import lax
from jax.experimental import pallas as pl
from jax.experimental.pallas import tpu as pltpu
from jax.sharding import PartitionSpec as P

HEAD_DIM = 64
CLASSES = 3
EPS = 1e-06
NEG = -1000000000.0
SCALE = HEAD_DIM**-0.5
LOW = jnp.bfloat16
F32 = jnp.float32
MESH_AXES = ("dp", "fsdp")
MIB = 1 << 20

QUERY_B, VALUE_B, OUTPUT_B, GAIN1, SHIFT1, OUTER_B, GAIN2, SHIFT2, POOLER_B, INNER_B, CLASS_W = (
    0, 1, 2, 3, 4, 5, 6, 7, 8, 9, 13,
)
TABLE = 16
COLUMNS = 384


def dot(a, b, dims=((1,), (0,))):
    return lax.dot_general(a, b, (dims, ((), ())), preferred_element_type=F32)


def dot_nt(a, b):
    return dot(a, b, ((1,), (1,)))


def full(shape):
    zeros = (0,) * len(shape)
    return pl.BlockSpec(shape, lambda *_: zeros, pipeline_mode=pl.Buffered(1))


def after(a, *others):
    return lax.optimization_barrier((a, *others))[0]


def call(kernel, outs, in_specs, out_specs, args, *, grid=(1,), scratch=(), prefetch=0, flops=0, moved=0, trans=0, vmem=20, name=None):
    return pl.pallas_call(
        kernel,
        name=name,
        out_shape=outs,
        grid_spec=pltpu.PrefetchScalarGridSpec(
            num_scalar_prefetch=prefetch,
            grid=grid,
            in_specs=in_specs,
            out_specs=out_specs,
            scratch_shapes=scratch,
        ),
        compiler_params=pltpu.CompilerParams(
            dimension_semantics=("arbitrary",) * len(grid), vmem_limit_bytes=vmem * MIB
        ),
        cost_estimate=pl.CostEstimate(flops=flops // 16, bytes_accessed=moved // 16, transcendentals=trans // 16),
    )(*args)


def shape(*dims, dtype=LOW):
    return jax.ShapeDtypeStruct(dims, dtype)


def lane_masks(rows):
    lanes = lax.broadcasted_iota(jnp.int32, (rows, 128), 1)
    return lanes < HEAD_DIM


def attention_kernel(tok, wq, wk, wv, table, seg_row, seg_col, q_o, k_o, v_o, ctx_o, lse_o, bias):
    step = pl.program_id(0)
    seq = tok.shape[0]

    @pl.when(step == 0)
    def _():
        bias[...] = jnp.where(seg_col[...] == seg_row[...], 0.0, NEG)

    x = tok[...]
    q = (dot(x, wq[...]) + table[QUERY_B : QUERY_B + 1, :]).astype(LOW)
    k = dot(x, wk[...]).astype(LOW)
    v = (dot(x, wv[...]) + table[VALUE_B : VALUE_B + 1, :]).astype(LOW)
    q_o[...] = q
    k_o[...] = k
    v_o[...] = v
    first = lane_masks(seq)
    zero = jnp.zeros((seq, 128), LOW)
    for pair in range(q.shape[1] // 128):
        cols = slice(pair * 128, pair * 128 + 128)
        q2, k2, v2t = q[:, cols], k[:, cols], v[:, cols].T
        parts = []
        for half in range(2):
            qm = jnp.where(first, q2, zero) if half == 0 else jnp.where(first, zero, q2)
            s = dot_nt(k2, qm) * SCALE + bias[...]
            top = jnp.max(s, axis=0, keepdims=True)
            e = jnp.exp(s - top)
            total = jnp.sum(e, axis=0, keepdims=True)
            out = dot(v2t[half * HEAD_DIM : (half + 1) * HEAD_DIM], e.astype(LOW)) / total
            parts.append(out)
            row = pair * 2 + half
            lse_o[0, row : row + 1, :] = top + jnp.log(total)
        ctx_o[:, cols] = jnp.concatenate(parts, axis=0).astype(LOW).T


def attention(tokens, wq, wk, wv, table, segments):
    seq, width = tokens.shape
    blk = 256
    steps = width // blk
    cols = pl.BlockSpec((seq, blk), lambda i: (0, i))
    wcols = pl.BlockSpec((width, blk), lambda i: (0, i))
    return call(
        attention_kernel,
        (shape(seq, width),) * 4 + (shape(steps, 8, seq, dtype=F32),),
        [full((seq, width)), wcols, wcols, wcols, pl.BlockSpec((TABLE, blk), lambda i: (0, i)), full((1, seq)), full((seq, 1))],
        (cols,) * 4 + (pl.BlockSpec((1, 8, seq), lambda i: (i, 0, 0)),),
        (tokens, wq, wk, wv, table, segments.reshape(1, seq), segments.reshape(seq, 1)),
        grid=(steps,),
        scratch=[pltpu.VMEM((seq, seq), F32)],
        flops=2 * seq * width * (3 * width + 2 * seq),
        moved=8 * seq * width + 6 * width * width,
        trans=seq * seq * width // HEAD_DIM,
        name="attention",
    )


def rows_norm(v):
    mean = jnp.mean(v, axis=-1, keepdims=True)
    centered = v - mean
    variance = jnp.mean(centered * centered, axis=-1, keepdims=True)
    scale = lax.rsqrt(variance + EPS)
    return centered * scale, scale


def attended_kernel(ctx, wo, tok, table, n1_o, r1_o, low_o):
    v = dot(ctx[...], wo[...]) + table[OUTPUT_B : OUTPUT_B + 1, :] + tok[...].astype(F32)
    n, r = rows_norm(v)
    n1_o[...] = n
    r1_o[...] = r
    low_o[...] = (n * table[GAIN1 : GAIN1 + 1, :] + table[SHIFT1 : SHIFT1 + 1, :]).astype(LOW)


def attended(ctx, wo, tokens, table):
    seq, width = tokens.shape
    blk = 128
    rows = pl.BlockSpec((blk, width), lambda i: (i, 0))
    return call(
        attended_kernel,
        (shape(seq, width, dtype=F32), shape(seq, 1, dtype=F32), shape(seq, width)),
        [rows, full((width, width)), rows, full((TABLE, width))],
        (rows, pl.BlockSpec((blk, 1), lambda i: (i, 0)), rows),
        (ctx, wo, tokens, table),
        grid=(seq // blk,),
        flops=2 * seq * width * width,
        moved=2 * width * width + 10 * seq * width,
        name="attended",
    )


ERFC_POLY = (
    0.14103029668331146,
    0.14146891236305237,
    0.1189674362540245,
    0.11450903862714767,
    -0.05439696088433266,
    0.22074179351329803,
    -0.34752535820007324,
    0.22408711910247803,
    -0.06580830365419388,
    0.006926023866981268,
)


def gelu_parts(v):
    t = 1.0 / (1.0 + (0.5 * 0.5**0.5) * jnp.abs(v))
    poly = ERFC_POLY[-1] * t + ERFC_POLY[-2]
    for coefficient in ERFC_POLY[-3::-1]:
        poly = poly * t + coefficient
    bell = jnp.exp2(v * v * (-0.5 * math.log2(math.e)))
    tail = t * poly * bell
    below = jnp.where(v < 0, tail, 1.0 - tail)
    return v * below, below + v * (bell * (2 * math.pi) ** -0.5)


def inner_kernel(low, wi, bi, act_o, slope_o):
    blk = 128
    for at in range(0, low.shape[0], blk):
        rows = slice(at, at + blk)
        act, slope = gelu_parts(dot(low[rows, :], wi[...]) + bi[...])
        act_o[rows, :] = act.astype(LOW)
        slope_o[rows, :] = slope.astype(LOW)


def inner(low, wi, bi):
    seq, width = low.shape
    ff = wi.shape[1]
    blk = 512
    cols = pl.BlockSpec((seq, blk), lambda i: (0, i))
    return call(
        inner_kernel,
        (shape(seq, ff), shape(seq, ff)),
        [full((seq, width)), pl.BlockSpec((width, blk), lambda i: (0, i)), pl.BlockSpec((1, blk), lambda i: (0, i))],
        (cols, cols),
        (low, wi, bi),
        grid=(ff // blk,),
        flops=2 * seq * width * ff,
        moved=2 * width * ff + 4 * seq * ff,
        trans=2 * seq * ff,
        name="inner",
    )


def outer_kernel(labels, bias3, act, w, n1, table, out_grad, wp, hid_o, sg_o, bg_o, sums_o, head_o, loss_o, acc, n2_s, r2_s):
    step = pl.program_id(0)
    seq, width = n1.shape

    @pl.when(step == 0)
    def _():
        acc[...] = jnp.zeros_like(acc)

    acc[...] += dot(act[...], w[...])

    @pl.when(step == pl.num_programs(0) - 1)
    def _():
        def row(at):
            return table[at : at + 1, :]

        gain2, shift2 = row(GAIN2), row(SHIFT2)
        blk = 64
        for at in range(0, seq, blk):
            rows = slice(at, at + blk)
            v = acc[rows, :] + row(OUTER_B) + (n1[rows, :] * row(GAIN1) + row(SHIFT1))
            n, r = rows_norm(v)
            n2_s[rows, :] = n
            r2_s[rows, :] = r
            hid_o[rows, :] = (n * gain2 + shift2).astype(LOW)
        class_rows = hid_o[0:8, :]
        pooled_pre = dot(class_rows, wp[...])[0:1, :] + row(POOLER_B)
        bent = jnp.tanh(pooled_pre)
        pooled = bent.astype(LOW).astype(F32)
        logits = [
            jnp.sum(pooled * row(CLASS_W + j), axis=-1, keepdims=True) + bias3[j] for j in range(CLASSES)
        ]
        top = functools.reduce(jnp.maximum, logits)
        exps = [jnp.exp(v - top) for v in logits]
        total = functools.reduce(jnp.add, exps)
        label = labels[0]
        hot = [jnp.where(label == j, 1.0, 0.0) for j in range(CLASSES)]
        picked = functools.reduce(jnp.add, [a * b for a, b in zip(logits, hot)])
        loss_o[...] = jnp.broadcast_to(top + jnp.log(total) - picked, loss_o.shape)
        slopes = [(e / total - o).astype(LOW).astype(F32) for e, o in zip(exps, hot)]
        pooled_grad = functools.reduce(
            jnp.add, [g * row(CLASS_W + j) for j, g in enumerate(slopes)]
        )
        pre_grad = (pooled_grad * (1.0 - bent * bent)).astype(LOW)
        row_grad = dot_nt(jnp.broadcast_to(pre_grad, (8, width)), wp[...])[0:1, :]
        head_o[...] = jnp.zeros_like(head_o)
        lanes = lax.broadcasted_iota(jnp.int32, (1, width), 1)
        head_o[0:1, :] = class_rows[0:1, :].astype(F32)
        head_o[1:2, :] = pre_grad.astype(F32)
        head_o[2:3, :] = pooled
        head_o[3:4, :] = functools.reduce(
            jnp.add, [jnp.where(lanes == j, g, 0.0) for j, g in enumerate(slopes)]
        )
        gain_sum = jnp.zeros((1, width), F32)
        shift_sum = jnp.zeros((1, width), F32)
        bias_sum = jnp.zeros((1, width), F32)
        for at in range(0, seq, blk):
            rows = slice(at, at + blk)
            fg = out_grad[rows, :].astype(F32)
            if at == 0:
                lead = lax.broadcasted_iota(jnp.int32, (blk, width), 0) == 0
                fg = fg + jnp.where(lead, jnp.broadcast_to(row_grad, (blk, width)), 0.0)
            n = n2_s[rows, :]
            g = fg * gain2
            gm = jnp.mean(g, axis=-1, keepdims=True)
            gn = jnp.mean(g * n, axis=-1, keepdims=True)
            sg = r2_s[rows, :] * (g - gm - n * gn)
            low = sg.astype(LOW)
            sg_o[rows, :] = sg
            bg_o[rows, :] = low
            gain_sum += jnp.sum(fg * n, axis=0, keepdims=True)
            shift_sum += jnp.sum(fg, axis=0, keepdims=True)
            bias_sum += jnp.sum(low.astype(F32), axis=0, keepdims=True)
        sums_o[...] = jnp.zeros_like(sums_o)
        sums_o[0:1, :] = gain_sum
        sums_o[1:2, :] = shift_sum
        sums_o[2:3, :] = bias_sum


def outer(act, w, n1, table, out_grad, wp, labels, bias3):
    seq, width = n1.shape
    ff = act.shape[1]
    blk = 1536
    whole = full((seq, width))
    return call(
        outer_kernel,
        (
            shape(seq, width),
            shape(seq, width, dtype=F32),
            shape(seq, width),
            shape(8, width, dtype=F32),
            shape(8, width, dtype=F32),
            shape(8, 128, dtype=F32),
        ),
        [
            pl.BlockSpec((seq, blk), lambda i, *_: (0, i)),
            pl.BlockSpec((blk, width), lambda i, *_: (i, 0)),
            whole,
            full((TABLE, width)),
            whole,
            full((width, width)),
        ],
        (whole, whole, whole, full((8, width)), full((8, width)), full((8, 128))),
        (labels, bias3, act, w, n1, table, out_grad, wp),
        grid=(ff // blk,),
        scratch=[pltpu.VMEM((seq, width), F32), pltpu.VMEM((seq, width), F32), pltpu.VMEM((seq, 1), F32)],
        prefetch=2,
        flops=2 * seq * width * ff,
        moved=2 * width * ff + 2 * seq * ff + 14 * seq * width,
        name="outer",
    )


def inner_grad_kernel(bg, w_out, slope, ig_o):
    ig_o[...] = (dot_nt(bg[...], w_out[...]) * slope[...].astype(F32)).astype(LOW)


def inner_grads(bg, w_out, slope):
    seq, width = bg.shape
    ff = slope.shape[1]
    blk = 1024
    cols = pl.BlockSpec((seq, blk), lambda i: (0, i))
    return call(
        inner_grad_kernel,
        shape(seq, ff),
        [full((seq, width)), pl.BlockSpec((blk, width), lambda i: (i, 0)), cols],
        cols,
        (bg, w_out, slope),
        grid=(ff // blk,),
        flops=2 * seq * width * ff,
        moved=2 * width * ff + 4 * seq * ff,
        name="inner_grads",
    )


def inner_back_kernel(ig, w_in, sg, n1, r1, table, res_o, ag_o, sums_o, acc, ib):
    step = pl.program_id(0)
    seq, width = n1.shape
    blk = ig.shape[1]
    ib[:, pl.ds(pl.multiple_of(step * blk, blk), blk)] = jnp.sum(ig[...].astype(F32), axis=0, keepdims=True)

    @pl.when(step == 0)
    def _():
        acc[...] = jnp.zeros_like(acc)

    acc[...] += dot_nt(ig[...], w_in[...])

    @pl.when(step == pl.num_programs(0) - 1)
    def _():
        gain1 = table[GAIN1 : GAIN1 + 1, :]
        gain_sum = jnp.zeros((1, width), F32)
        shift_sum = jnp.zeros((1, width), F32)
        bias_sum = jnp.zeros((1, width), F32)
        blk = 64
        for at in range(0, seq, blk):
            rows = slice(at, at + blk)
            fg = sg[rows, :] + acc[rows, :]
            n = n1[rows, :]
            g = fg * gain1
            gm = jnp.mean(g, axis=-1, keepdims=True)
            gn = jnp.mean(g * n, axis=-1, keepdims=True)
            res = r1[rows, :] * (g - gm - n * gn)
            low = res.astype(LOW)
            res_o[rows, :] = res
            ag_o[rows, :] = low
            gain_sum += jnp.sum(fg * n, axis=0, keepdims=True)
            shift_sum += jnp.sum(fg, axis=0, keepdims=True)
            bias_sum += jnp.sum(low.astype(F32), axis=0, keepdims=True)
        sums_o[...] = jnp.zeros_like(sums_o)
        sums_o[0:1, :] = gain_sum
        sums_o[1:2, :] = shift_sum
        sums_o[2:3, :] = bias_sum
        for at in range(ib.shape[1] // width):
            sums_o[3 + at : 4 + at, :] = ib[:, at * width : (at + 1) * width]


def inner_back(ig, w_in, sg, n1, r1, table):
    seq, width = n1.shape
    ff = ig.shape[1]
    blk = 1536
    whole = full((seq, width))
    return call(
        inner_back_kernel,
        (shape(seq, width, dtype=F32), shape(seq, width), shape(8, width, dtype=F32)),
        [
            pl.BlockSpec((seq, blk), lambda i: (0, i)),
            pl.BlockSpec((width, blk), lambda i: (0, i)),
            whole,
            whole,
            full((seq, 1)),
            full((TABLE, width)),
        ],
        (whole, whole, full((8, width))),
        (ig, w_in, sg, n1, r1, table),
        grid=(ff // blk,),
        scratch=[pltpu.VMEM((seq, width), F32), pltpu.VMEM((1, ff), F32)],
        flops=2 * seq * width * ff,
        moved=2 * width * ff + 2 * seq * ff + 16 * seq * width,
        name="inner_back",
    )


def attention_back_kernel(q, k, v, lse, ag, wo, seg_row, seg_col, dq_o, dk_o, dv_o, sums_o, bias):
    seq = ag.shape[0]

    @pl.when(pl.program_id(0) == 0)
    def _():
        bias[...] = jnp.where(seg_col[...] == seg_row[...], 0.0, NEG)

    grad = dot_nt(ag[...], wo[...]).astype(LOW)
    first = lane_masks(seq)
    zero = jnp.zeros((seq, 128), LOW)
    sums_o[...] = jnp.zeros_like(sums_o)
    for pair in range(q.shape[1] // 128):
        cols = slice(pair * 128, pair * 128 + 128)
        q2, k2, v2, g2 = q[:, cols], k[:, cols], v[:, cols], grad[:, cols]
        k2t = k2.T
        dqs, dks, dvs = [], [], []
        for half in range(2):
            def own(a):
                return jnp.where(first, a, zero) if half == 0 else jnp.where(first, zero, a)

            row = pair * 2 + half
            s = dot_nt(k2, own(q2)) * SCALE + bias[...]
            p = jnp.exp(s - lse[0, row : row + 1, :])
            dp = dot_nt(v2, own(g2))
            weighted = p * dp
            level = jnp.sum(weighted, axis=0, keepdims=True)
            ds = (weighted - p * level).astype(LOW)
            dvs.append(dot(p.astype(LOW), g2))
            dks.append(dot(ds, q2))
            dqs.append(dot(k2t[half * HEAD_DIM : (half + 1) * HEAD_DIM], ds))
        dq = (jnp.concatenate(dqs, axis=0) * SCALE).astype(LOW).T
        dk = (jnp.where(first, dks[0], dks[1]) * SCALE).astype(LOW)
        dv = jnp.where(first, dvs[0], dvs[1]).astype(LOW)
        dq_o[:, cols] = dq
        dk_o[:, cols] = dk
        dv_o[:, cols] = dv
        sums_o[0:1, cols] = jnp.sum(dq.astype(F32), axis=0, keepdims=True)
        sums_o[1:2, cols] = jnp.sum(dv.astype(F32), axis=0, keepdims=True)


def attention_back(q, k, v, lse, ag, wo, segments, begin, count):
    seq, width = ag.shape
    blk = 256
    begin, steps = begin // blk, count // blk
    cols = pl.BlockSpec((seq, blk), lambda i: (0, i + begin))
    out = pl.BlockSpec((seq, blk), lambda i: (0, i))
    return call(
        attention_back_kernel,
        (shape(seq, count),) * 3 + (shape(8, count, dtype=F32),),
        [
            cols,
            cols,
            cols,
            pl.BlockSpec((1, 8, seq), lambda i: (i + begin, 0, 0)),
            full((seq, width)),
            pl.BlockSpec((blk, width), lambda i: (i + begin, 0)),
            full((1, seq)),
            full((seq, 1)),
        ],
        (out,) * 3 + (pl.BlockSpec((8, blk), lambda i: (0, i)),),
        (q, k, v, lse, ag, wo, segments.reshape(1, seq), segments.reshape(seq, 1)),
        grid=(steps,),
        scratch=[pltpu.VMEM((seq, seq), F32)],
        flops=2 * seq * count * (width + 5 * seq),
        moved=16 * seq * count + 2 * width * count,
        trans=seq * seq * count // HEAD_DIM,
        name="attention_back",
    )


def tokens_back_kernel(res, dq, dk, dv, wq, wk, wv, out):
    out[...] = res[...] + dot_nt(dq[...], wq[...]) + dot_nt(dk[...], wk[...]) + dot_nt(dv[...], wv[...])


def tokens_back(res, dq, dk, dv, wq, wk, wv):
    seq, width = res.shape
    blk = 128
    rows = pl.BlockSpec((blk, width), lambda i: (i, 0))
    weight = full((width, width))
    return call(
        tokens_back_kernel,
        shape(seq, width, dtype=F32),
        [rows] * 4 + [weight] * 3,
        rows,
        (res, dq, dk, dv, wq, wk, wv),
        grid=(seq // blk,),
        flops=6 * seq * width * width,
        moved=14 * seq * width + 6 * width * width,
        name="tokens_back",
    )


def grads(name, where, lefts, which, rights, add=None):
    features, seq = lefts[0].shape if add is not None else lefts[0].shape[::-1]
    parts = features // 16
    widths = tuple((w, r.shape[1] // 2) for w, r in zip(which, rights))
    total = sum(w for _, w in widths)
    half = (lambda i, where: (0, 1 - where[3])) if add is None else (lambda i, where: (0, where[3]))
    specs = [full(a.shape) for a in lefts]
    specs += [pl.BlockSpec((seq, w), half, pipeline_mode=pl.Buffered(1)) for _, w in widths]
    args = [where, *lefts, *rights]
    piece = (4, parts * total // COLUMNS, COLUMNS)
    outs = ((4, *piece),) + ((features, seq),) * len(lefts) if add is None else (piece,) * 4
    if add is not None:
        specs.append(full(add.shape))
        args.append(add)

    def kernel(where, *refs):
        left_refs, refs = refs[: len(lefts)], refs[len(lefts) :]
        right_refs, refs = refs[: len(rights)], refs[len(rights) :]
        x, y, z0 = where[0], where[1], where[2]
        if add is None:
            out_refs, turned = refs[:1], refs[1:]
            for left, store in zip(left_refs, turned):
                for start in range(0, features, 256):
                    store[start : start + 256, :] = left[:, start : start + 256].T
        else:
            add_ref, out_refs, turned = refs[0], refs[1:], left_refs
        for place in range(4):
            hh = jnp.bitwise_xor(x, place // 2)
            yy = jnp.bitwise_xor(y, place % 2)
            top = 0
            for (at, width), right in zip(widths, right_refs):
                rows = []
                for dz in range(4):
                    shard = jnp.bitwise_xor(z0, dz) * 2 + yy
                    rows.append(turned[at][pl.ds(pl.multiple_of((shard * 2 + hh) * parts, 16), parts), :])
                got = dot(jnp.concatenate(rows, axis=0), right[...]).reshape(4, parts, width)
                for column in range(0, width, COLUMNS):
                    one = got[:, :, column : column + COLUMNS]
                    if add is None:
                        out_refs[0][place, :, top : top + parts, :] = one.astype(LOW)
                    else:
                        one = one + add_ref[place, :, top : top + parts, :].astype(F32)
                        out_refs[place][:, top : top + parts, :] = one.astype(LOW)
                    top += parts

    got = call(
        kernel,
        tuple(shape(*o) for o in outs),
        specs,
        tuple(full(o) for o in outs),
        args,
        prefetch=1,
        flops=2 * seq * 16 * parts * total,
        moved=2 * 16 * parts * total + 2 * seq * 16 * parts,
        name=name,
    )
    return (got[0], list(got[1:])) if add is None else got


def pack_kernel(where, wq, wk, wv, wo, wi, wf, wp, small, own_a, own_b, own_c):
    for out, weights in ((own_a, (wq, wk, wv)), (own_b, (wo, wi))):
        left = 0
        for ref in weights:
            out[: ref.shape[0], left : left + ref.shape[1]] = ref[...]
            left += ref.shape[1]
    at = wq.shape[0]
    own_a[at:, :] = jnp.zeros((8, own_a.shape[1]), LOW)
    for top in range(0, small.shape[0], 8):
        own_a[at:, top * 16 : top * 16 + small.shape[1]] = small[top : top + 8, :]
    rows = wf.shape[0]
    own_c[:rows, :] = wf[...]
    own_c[rows:, :] = wp[...]


def pack(where, wq, wk, wv, wo, wi, wf, wp, small):
    rows, width = wq.shape
    deep = wf.shape[0] // 2
    ff = wi.shape[1]
    outs = (shape(rows // 2 + 8, 3 * width // 2), shape(rows // 2, (width + ff) // 2), shape(deep + rows // 2, width // 2))
    weights = (wq, wk, wv, wo, wi, wf, wp)
    quarters = [
        pl.BlockSpec((w.shape[0] // 2, w.shape[1] // 2), lambda i, where: (where[0], where[3])) for w in weights
    ]
    return call(
        pack_kernel,
        outs,
        quarters + [full(small.shape)],
        tuple(full(o.shape) for o in outs),
        (where, *(pltpu.with_memory_space_constraint(w, pltpu.HBM) for w in weights), small),
        prefetch=1,
        moved=4 * sum(math.prod(o.shape) for o in outs),
        vmem=8,
        name="pack",
    )


def weights_kernel(spans, places, where, *refs):
    pieces, outs, sem = refs[: len(places)], refs[-1 - len(spans) : -1], refs[-1]
    copies = []
    for place, piece in zip(places, pieces):
        hh = jnp.bitwise_xor(where[0], place // 4)
        yy = jnp.bitwise_xor(where[1], place // 2 % 2)
        cc = jnp.bitwise_xor(where[3], place % 2)
        for dz in range(4):
            zz = jnp.bitwise_xor(where[2], dz)
            for (top, rows, left, width), out in zip(spans, outs):
                to = out.at[zz, yy, hh, :, pl.ds(pl.multiple_of(cc * width, 128), width)]
                come = piece.at[dz, top : top + rows, left : left + width]
                copies.append(pltpu.make_async_copy(come, to, sem.at[len(copies)]))
    for one in copies:
        one.start()
    for one in copies:
        one.wait()


def place_some(where, pieces, spans, places, begun=()):
    anywhere = pl.BlockSpec(memory_space=pl.ANY)
    count = 1 + len(pieces)
    return pl.pallas_call(
        functools.partial(weights_kernel, tuple(spans), tuple(places)),
        name="place_weights",
        out_shape=tuple(shape(4, 2, 2, rows, 2 * width) for _, rows, _, width in spans),
        grid_spec=pltpu.PrefetchScalarGridSpec(
            num_scalar_prefetch=1,
            grid=(1,),
            in_specs=[anywhere] * (len(pieces) + len(begun)),
            out_specs=(anywhere,) * len(spans),
            scratch_shapes=[pltpu.SemaphoreType.DMA((4 * len(places) * len(spans),))],
        ),
        input_output_aliases={count + at: at for at in range(len(begun))},
        compiler_params=pltpu.CompilerParams(vmem_limit_bytes=4 * MIB),
        cost_estimate=pl.CostEstimate(flops=0, bytes_accessed=pieces[0].size, transcendentals=0),
    )(where, *pieces, *begun)


def place_weights(where, pieces, spans):
    begun = place_some(where, pieces[:6], spans, range(6))
    return finish_weights(where, begun, pieces[6:], spans)


def finish_weights(where, begun, pieces, spans):
    outs = place_some(where, pieces, spans, (6, 7), begun)
    return [o.reshape(16 * rows, 2 * width) for o, (_, rows, _, width) in zip(outs, spans)]


def shards_kernel(spans, where, *refs):
    pieces, outs = refs[:4], refs[4:]
    for place in range(4):
        hh = jnp.bitwise_xor(where[0], place // 2)
        for core in range(2):

            @pl.when(jnp.bitwise_xor(where[3], place % 2) == core)
            def _():
                for (top, rows, blocks), out in zip(spans, outs):
                    for block in range(blocks):
                        left = (core * blocks + block) * COLUMNS
                        out[hh, :, left : left + COLUMNS] = pieces[place][
                            top + block * rows : top + (block + 1) * rows, :
                        ].astype(F32)


def place_shards(where, pieces, spans):
    sizes = [(2, rows, 2 * blocks * COLUMNS) for _, rows, blocks in spans]
    outs = call(
        functools.partial(shards_kernel, tuple(spans)),
        tuple(shape(*size, dtype=F32) for size in sizes),
        [full(pieces[0].shape)] * 4,
        tuple(full(size) for size in sizes),
        (where, *pieces),
        prefetch=1,
        moved=24 * pieces[0].size,
        vmem=12,
        name="place_shards",
    )
    return [o.reshape(2 * size[1], size[2]) for o, size in zip(outs, sizes)]


def device(x, core, z, y):
    return (x * 2 + core) * 8 + z * 2 + y


ALL = [(x, core, z, y) for x in range(2) for core in range(2) for z in range(4) for y in range(2)]
CORE_SWAP = [(device(*a), device(a[0], 1 - a[1], a[2], a[3])) for a in ALL]
X_SWAP = [(device(*a), device(1 - a[0], a[1], a[2], a[3])) for a in ALL]
Y_SWAP = [(device(*a), device(a[0], a[1], a[2], 1 - a[3])) for a in ALL]
Z_SWAPS = [[(device(*a), device(a[0], a[1], a[2] ^ d, a[3])) for a in ALL] for d in range(4)]
X_CORE_SWAP = [(device(*a), device(1 - a[0], 1 - a[1], a[2], a[3])) for a in ALL]
XY_SWAP = [(device(*a), device(1 - a[0], a[1], a[2], 1 - a[3])) for a in ALL]


def swap(a, pairs):
    return lax.ppermute(a, MESH_AXES, pairs)


def wide(*arrays):
    return functools.reduce(jnp.add, [a.astype(F32) for a in arrays])


def along_z(own):
    return [swap(own, Z_SWAPS[d]) for d in (1, 2, 3)]


def to_core(arrays):
    return [swap(a, CORE_SWAP) for a in arrays]


def together(*groups):
    leaves, tree = jax.tree.flatten(groups)
    return jax.tree.unflatten(tree, lax.optimization_barrier(tuple(leaves)))


def low(a):
    return a.astype(LOW)


def sums_by_z(parts):
    return [wide(*(p[d] for p in parts)) for d in range(4)]


def on_device(
    by_links,
    tokens,
    out_grad,
    segment_ids,
    labels,
    query_weight,
    query_bias,
    key_weight,
    value_weight,
    value_bias,
    output_weight,
    output_bias,
    first_norm_gain,
    first_norm_shift,
    inner_weight,
    inner_bias,
    outer_weight,
    outer_bias,
    second_norm_gain,
    second_norm_shift,
    pooler_weight,
    pooler_bias,
    class_weight,
    class_bias,
):
    _, seq, width = tokens.shape
    tokens = tokens.reshape(seq, width)
    out_grad = out_grad.reshape(seq, width)
    dp, fsdp = lax.axis_index("dp"), lax.axis_index("fsdp")
    where = jnp.stack([dp // 2, fsdp % 2, fsdp // 2, dp % 2]).astype(jnp.int32)
    local = query_bias.shape[0]
    shards = width // local
    ff = inner_weight.shape[1]

    small = jnp.concatenate(
        [
            jnp.stack(
                [
                    query_bias,
                    value_bias,
                    output_bias,
                    first_norm_gain,
                    first_norm_shift,
                    outer_bias,
                    second_norm_gain,
                    second_norm_shift,
                    pooler_bias,
                ]
            ),
            inner_bias.reshape(ff // width, local),
            class_weight.T,
        ]
    )

    def tables(got):
        table = jnp.transpose(got, (1, 0, 2)).reshape(TABLE, width)
        return table, got[:, INNER_B:CLASS_W, :].reshape(1, ff)

    bias3 = class_bias.astype(F32)
    if by_links:
        own_a, own_b, own_c = pack(
            where,
            query_weight,
            key_weight,
            value_weight,
            output_weight,
            inner_weight,
            outer_weight,
            pooler_weight,
            small,
        )
        parts, deep = local // 2, outer_weight.shape[0] // 2
        spans_a = [(0, parts, at * (width // 2), width // 2) for at in range(3)]
        spans_b = [(0, parts, 0, width // 2), (0, parts, width // 2, ff // 2)]
        spans_c = [(0, deep, 0, width // 2), (deep, parts, 0, width // 2)]

        def mixed(near, other):
            return [a for pair in zip(near, other) for a in pair]

        z_a = along_z(own_a)
        (z_a, own_a, own_b, own_c) = together(z_a, own_a, own_b, own_c)
        z_b = along_z(own_b)
        far_a = jnp.stack([own_a, *z_a])
        x_a, y_a = swap(far_a, X_SWAP), swap(far_a, Y_SWAP)
        (far_a, x_a, y_a, z_b, own_b, own_c) = together(far_a, x_a, y_a, z_b, own_b, own_c)
        z_c = along_z(own_c)
        far_b = jnp.stack([own_b, *z_b])
        xy_a = swap(x_a, Y_SWAP)
        x_b = swap(far_b, X_SWAP)
        (core_a,) = to_core([jnp.concatenate([far_a, y_a, x_a])])
        order = [((where[2] ^ d) * 2 + (where[1] ^ e)) for e in range(2) for d in range(4)]
        spread = (jnp.stack(order)[None, :] == jnp.arange(shards)[:, None]).astype(LOW)
        small = jnp.concatenate([far_a[:, parts:, :256], y_a[:, parts:, :256]])
        small = jnp.concatenate([small[:, :, :local], small[:, :, 128 : 128 + local]], axis=1)
        table, inner_row = tables(jnp.einsum("sp,pji->sji", spread, small, preferred_element_type=F32))
        (far_a, y_a, x_a, xy_a, far_b, x_b, z_c, core_a, own_c, table, inner_row) = together(
            far_a, y_a, x_a, xy_a, far_b, x_b, z_c, core_a, own_c, table, inner_row
        )
        y_b = swap(far_b, Y_SWAP)
        far_c = jnp.stack([own_c, *z_c])
        x_c = swap(far_c, X_SWAP)
        core_a = [core_a[:4], core_a[4:8], core_a[8:]] + to_core([xy_a])
        wq, wk, wv = place_weights(where, mixed((far_a, y_a, x_a, xy_a), core_a), spans_a)
        q, k, v, context, lse = attention(tokens, wq, wk, wv, table, segment_ids)
        (q, k, v, context, lse, far_b, x_b, y_b, far_c, x_c) = together(
            q, k, v, context, lse, far_b, x_b, y_b, far_c, x_c
        )
        xy_b = swap(y_b, X_SWAP)
        y_c = swap(far_c, Y_SWAP)
        core_b = to_core([far_b, y_b, x_b])
        begun_b = place_some(where, mixed((far_b, y_b, x_b), core_b), spans_b, range(6))
        (xy_b, begun_b, far_c, x_c, y_c) = together(xy_b, begun_b, far_c, x_c, y_c)
        xy_c = swap(x_c, Y_SWAP)
        (core_xy_b,) = to_core([xy_b])
        core_c = to_core([far_c, y_c, x_c])
        wo, wi = finish_weights(where, begun_b, [xy_b, core_xy_b], spans_b)
        n1, r1, first_low = attended(context, wo, tokens, table)
        activated, slope = inner(first_low, wi, inner_row)
        (core_c, activated, slope) = together(core_c, activated, slope)
        begun_c = place_some(where, mixed((far_c, y_c, x_c), core_c), spans_c, range(6))
        (xy_c, begun_c, activated, slope) = together(xy_c, begun_c, activated, slope)
        wf, wp = finish_weights(where, begun_c, [xy_c, *to_core([xy_c])], spans_c)
    else:
        wq, wk, wv, wo, wp, wi, wf = (
            lax.all_gather(w, "fsdp", axis=0, tiled=True)
            for w in (
                query_weight,
                key_weight,
                value_weight,
                output_weight,
                pooler_weight,
                inner_weight,
                outer_weight,
            )
        )
        table, inner_row = tables(lax.all_gather(small, "fsdp").astype(F32))
        q, k, v, context, lse = attention(tokens, wq, wk, wv, table, segment_ids)
        n1, r1, first_low = attended(context, wo, tokens, table)
        activated, slope = inner(first_low, wi, inner_row)

    hidden, second_grad, branch_grad, sums2, head, loss = outer(
        activated, wf, n1, table, out_grad, wp, labels, bias3
    )
    def attention_step(attended_grad, begin, count):
        return attention_back(q, k, v, lse, attended_grad, wo, segment_ids, begin, count)

    cut = 512
    if by_links:

        def gathered(heads, pairs):
            return jnp.concatenate([heads, swap(heads, pairs)])

        heads = low(head)[None]

        def plane(parts):
            same, y, x, xy = parts
            return [same, swap(x, X_SWAP), swap(y, Y_SWAP), swap(xy, XY_SWAP)]

        other, lefts = grads("outer_grad_a", where, [activated], [0], [branch_grad])
        (other, branch_grad) = together(other, branch_grad)
        other, heads = swap(other, CORE_SWAP), gathered(heads, Z_SWAPS[1])
        inner_grad = inner_grads(branch_grad, wf, slope)
        (other, inner_grad, heads) = together(other, inner_grad, heads)
        mine = grads("outer_grad_b", where, lefts, [0], [branch_grad], other)
        (mine, inner_grad, heads) = together(mine, inner_grad, heads)
        same_f, y_f, x_f, xy_f = mine
        from_x, from_y = swap(x_f[:3], X_SWAP), swap(y_f[:3], Y_SWAP)
        heads = gathered(gathered(heads, Z_SWAPS[2]), Y_SWAP)
        residual_grad, attended_grad, sums1 = inner_back(inner_grad, wi, second_grad, n1, r1, table)
        (attended_grad, inner_grad) = together(attended_grad, inner_grad)
        lefts, rights = [context, first_low], [attended_grad, inner_grad]
        other, lefts = grads("inner_grad_a", where, lefts, [0, 1], rights)
        (other, attended_grad, from_x, from_y, x_f, y_f, xy_f, heads) = together(
            other, attended_grad, from_x, from_y, x_f[3], y_f[3], xy_f, heads
        )
        other = swap(other, CORE_SWAP)
        x_f, y_f, xy_f = swap(x_f, X_SWAP), swap(y_f, Y_SWAP), swap(xy_f, XY_SWAP)
        heads = gathered(heads, X_SWAP)
        back_a = attention_step(attended_grad, 0, cut)
        (other, back_a, attended_grad, heads) = together(other, back_a, attended_grad, heads)
        mine = grads("inner_grad_b", where, lefts, [0, 1], rights, other)
        (mine, attended_grad, heads) = together(mine, attended_grad, heads)
        heads = gathered(heads, CORE_SWAP)
        back_b = attention_step(attended_grad, cut, width - cut)
        dq, dk, dv, sums0 = (jnp.concatenate([a, b], axis=1) for a, b in zip(back_a, back_b))
        rights = [dq, dk, dv]
        other, lefts = grads("query_grad_a", where, [tokens], [0, 0, 0], rights)
        sums = jnp.stack([sums2, sums1, sums0])
        (other, dq, dk, dv, sums, x_f, y_f, xy_f, mine, heads) = together(
            other, dq, dk, dv, sums, x_f, y_f, xy_f, mine, heads
        )
        rights = [dq, dk, dv]
        parts_i = plane(mine)
        other = swap(other, CORE_SWAP)
        totals_f = [wide(same_f[d], xy_f[d], from_x[d], from_y[d]) for d in range(3)]
        totals_f.append(wide(same_f[3], xy_f[3], x_f, y_f))
        odd_f = swap(low(jnp.stack([totals_f[1], totals_f[3]])), Z_SWAPS[1])
        mine = grads("query_grad_b", where, lefts, [0, 0, 0], rights, other)
        (mine, odd_f, even_f, dq, dk, dv, sums, heads) = together(
            mine, odd_f, [totals_f[0], totals_f[2]], dq, dk, dv, sums, heads
        )
        go_f = swap(low(wide(even_f[1], odd_f[1])), Z_SWAPS[2])
        sums = sums + swap(sums, Z_SWAPS[1])
        tokens_grad = tokens_back(residual_grad, dq, dk, dv, wq, wk, wv)
        (parts_i, mine, go_f, stay_f, tokens_grad, heads, sums) = together(
            parts_i, mine, go_f, wide(even_f[0], odd_f[0]), tokens_grad, heads, sums
        )
        parts_q = plane(mine)
        totals_i = sums_by_z(parts_i)
        odd_i = swap(low(jnp.stack([totals_i[1], totals_i[3]])), Z_SWAPS[1])
        own_f = low(wide(stay_f, go_f))
        sums = sums + swap(sums, Z_SWAPS[2])
        (odd_i, even_i, own_f, sums, heads) = together(odd_i, [totals_i[0], totals_i[2]], own_f, sums, heads)
        go_i = swap(low(wide(even_i[1], odd_i[1])), Z_SWAPS[2])
        sums = sums + swap(sums, X_SWAP)
        (parts_q, go_i, stay_i, own_f, sums, heads) = together(
            parts_q, go_i, wide(even_i[0], odd_i[0]), own_f, sums, heads
        )
        totals_q = sums_by_z(parts_q)
        z_q = [swap(low(totals_q[d]), Z_SWAPS[d]) for d in (1, 2, 3)]
        own = jnp.concatenate([own_f, low(wide(stay_i, go_i))])
        across = swap(own, X_SWAP)
        sums = sums + swap(sums, Y_SWAP)
        (z_q, own_q, own, across, sums, heads) = together(z_q, totals_q[0], own, across, sums, heads)
        sums = sums + swap(sums, CORE_SWAP)
        core = swap(jnp.stack([own, across]), CORE_SWAP)
        own_q = low(wide(own_q, *z_q))
        all_q = [own_q, swap(own_q, CORE_SWAP), swap(own_q, X_SWAP), swap(own_q, X_CORE_SWAP)]
        outer_grad, output_grad, inner_weight_grad = place_shards(
            where,
            [own, core[0], across, core[1]],
            [(0, deep, 1), (deep, parts, 1), (deep + parts, parts, ff // width)],
        )
        query_grad, key_grad, value_grad = place_shards(where, all_q, [(at * parts, parts, 1) for at in range(3)])
    else:

        def reduced(left, right):
            local_grad = lax.dot_general(left, right, (((0,), (0,)), ((), ())), preferred_element_type=F32)
            shard = lax.psum_scatter(local_grad, "fsdp", scatter_dimension=0, tiled=True)
            return lax.psum(low(shard), "dp").astype(F32)

        inner_grad = inner_grads(branch_grad, wf, slope)
        residual_grad, attended_grad, sums1 = inner_back(inner_grad, wi, second_grad, n1, r1, table)
        dq, dk, dv, sums0 = attention_step(attended_grad, 0, width)
        outer_grad = reduced(activated, branch_grad)
        inner_weight_grad = reduced(first_low, inner_grad)
        output_grad = reduced(context, attended_grad)
        query_grad, key_grad, value_grad = (reduced(tokens, d) for d in (dq, dk, dv))
        tokens_grad = tokens_back(residual_grad, dq, dk, dv, wq, wk, wv)
        sums = lax.psum(jnp.stack([sums2, sums1, sums0]), MESH_AXES)
        heads = lax.all_gather(head, MESH_AXES)

    vectors = lax.dynamic_slice(sums, (0, 0, fsdp * local), (3, 8, local))
    inner_bias_grad = lax.dynamic_slice(
        sums[1, 3 : 3 + ff // width].reshape(ff), (fsdp * (ff // shards),), (ff // shards,)
    )
    class_rows, pre_grads, pooled = heads[:, 0], heads[:, 1], heads[:, 2]
    logit_grads = heads[:, 3, :CLASSES]

    def own_columns(a):
        return lax.dynamic_slice(a, (0, fsdp * local), (a.shape[0], local))

    def over_rows(a, b):
        return lax.dot_general(a, b, (((0,), (0,)), ((), ())), preferred_element_type=F32)

    pooler_grad = over_rows(own_columns(class_rows), pre_grads)
    pooler_bias_grad = jnp.sum(own_columns(pre_grads).astype(F32), axis=0)
    class_grad = over_rows(own_columns(pooled), logit_grads)
    class_bias_grad = jnp.sum(logit_grads.astype(F32), axis=0)

    return (
        hidden[None],
        tokens_grad[None],
        loss[0, :1],
        query_grad,
        vectors[2, 0],
        key_grad,
        value_grad,
        vectors[2, 1],
        output_grad,
        vectors[1, 2],
        vectors[1, 0],
        vectors[1, 1],
        inner_weight_grad,
        inner_bias_grad,
        outer_grad,
        vectors[0, 2],
        vectors[0, 0],
        vectors[0, 1],
        pooler_grad,
        pooler_bias_grad,
        class_grad,
        class_bias_grad,
    )


def solution(mesh):
    sizes = dict(mesh.shape)
    by_links = sizes == {"dp": 4, "fsdp": 8}
    rows = P(MESH_AXES, None, None)
    ids = P(MESH_AXES, None)
    row = P(MESH_AXES)
    matrix = P("fsdp", None)
    vector = P("fsdp")
    return jax.shard_map(
        functools.partial(on_device, by_links),
        mesh=mesh,
        in_specs=(
            rows, rows, ids, row,
            matrix, vector, matrix, matrix, vector, matrix, vector, vector, vector,
            matrix, vector, matrix, vector, vector, vector, matrix, vector, matrix, P(),
        ),
        out_specs=(
            rows, rows, row,
            matrix, vector, matrix, matrix, vector, matrix, vector, vector, vector,
            matrix, vector, matrix, vector, vector, vector, matrix, vector, matrix, P(),
        ),
        check_vma=False,
    )
```

```python
import functools
import math

import jax
import jax.numpy as jnp
from jax import lax
from jax.experimental import pallas as pl
from jax.experimental.pallas import tpu as pltpu
from jax.sharding import PartitionSpec as P

HEAD_DIM = 64
CLASSES = 3
EPS = 1e-06
NEG = -1000000000.0
SCALE = HEAD_DIM**-0.5
LOW = jnp.bfloat16
F32 = jnp.float32
MESH_AXES = ("dp", "fsdp")
MIB = 1 << 20

QUERY_B, VALUE_B, OUTPUT_B, GAIN1, SHIFT1, OUTER_B, GAIN2, SHIFT2, POOLER_B, INNER_B, CLASS_W = (
    0, 1, 2, 3, 4, 5, 6, 7, 8, 9, 13,
)
TABLE = 16
COLUMNS = 384


def dot(a, b, dims=((1,), (0,))):
    return lax.dot_general(a, b, (dims, ((), ())), preferred_element_type=F32)


def dot_nt(a, b):
    return dot(a, b, ((1,), (1,)))


def full(shape):
    zeros = (0,) * len(shape)
    return pl.BlockSpec(shape, lambda *_: zeros, pipeline_mode=pl.Buffered(1))


def after(a, *others):
    return lax.optimization_barrier((a, *others))[0]


def call(kernel, outs, in_specs, out_specs, args, *, grid=(1,), scratch=(), prefetch=0, flops=0, moved=0, trans=0, vmem=20, name=None):
    return pl.pallas_call(
        kernel,
        name=name,
        out_shape=outs,
        grid_spec=pltpu.PrefetchScalarGridSpec(
            num_scalar_prefetch=prefetch,
            grid=grid,
            in_specs=in_specs,
            out_specs=out_specs,
            scratch_shapes=scratch,
        ),
        compiler_params=pltpu.CompilerParams(
            dimension_semantics=("arbitrary",) * len(grid), vmem_limit_bytes=vmem * MIB
        ),
        cost_estimate=pl.CostEstimate(flops=flops // 16, bytes_accessed=moved // 16, transcendentals=trans // 16),
    )(*args)


def shape(*dims, dtype=LOW):
    return jax.ShapeDtypeStruct(dims, dtype)


def lane_masks(rows):
    lanes = lax.broadcasted_iota(jnp.int32, (rows, 128), 1)
    return lanes < HEAD_DIM


def attention_kernel(tok, wq, wk, wv, table, seg_row, seg_col, q_o, k_o, v_o, ctx_o, lse_o, bias):
    step = pl.program_id(0)
    seq = tok.shape[0]

    @pl.when(step == 0)
    def _():
        bias[...] = jnp.where(seg_col[...] == seg_row[...], 0.0, NEG)

    x = tok[...]
    q = (dot(x, wq[...]) + table[QUERY_B : QUERY_B + 1, :]).astype(LOW)
    k = dot(x, wk[...]).astype(LOW)
    v = (dot(x, wv[...]) + table[VALUE_B : VALUE_B + 1, :]).astype(LOW)
    q_o[...] = q
    k_o[...] = k
    v_o[...] = v
    first = lane_masks(seq)
    zero = jnp.zeros((seq, 128), LOW)
    for pair in range(q.shape[1] // 128):
        cols = slice(pair * 128, pair * 128 + 128)
        q2, k2, v2t = q[:, cols], k[:, cols], v[:, cols].T
        parts = []
        for half in range(2):
            qm = jnp.where(first, q2, zero) if half == 0 else jnp.where(first, zero, q2)
            s = dot_nt(k2, qm) * SCALE + bias[...]
            top = jnp.max(s, axis=0, keepdims=True)
            e = jnp.exp(s - top)
            total = jnp.sum(e, axis=0, keepdims=True)
            out = dot(v2t[half * HEAD_DIM : (half + 1) * HEAD_DIM], e.astype(LOW)) / total
            parts.append(out)
            row = pair * 2 + half
            lse_o[0, row : row + 1, :] = top + jnp.log(total)
        ctx_o[:, cols] = jnp.concatenate(parts, axis=0).astype(LOW).T


def attention(tokens, wq, wk, wv, table, segments):
    seq, width = tokens.shape
    blk = 256
    steps = width // blk
    cols = pl.BlockSpec((seq, blk), lambda i: (0, i))
    wcols = pl.BlockSpec((width, blk), lambda i: (0, i))
    return call(
        attention_kernel,
        (shape(seq, width),) * 4 + (shape(steps, 8, seq, dtype=F32),),
        [full((seq, width)), wcols, wcols, wcols, pl.BlockSpec((TABLE, blk), lambda i: (0, i)), full((1, seq)), full((seq, 1))],
        (cols,) * 4 + (pl.BlockSpec((1, 8, seq), lambda i: (i, 0, 0)),),
        (tokens, wq, wk, wv, table, segments.reshape(1, seq), segments.reshape(seq, 1)),
        grid=(steps,),
        scratch=[pltpu.VMEM((seq, seq), F32)],
        flops=2 * seq * width * (3 * width + 2 * seq),
        moved=8 * seq * width + 6 * width * width,
        trans=seq * seq * width // HEAD_DIM,
        name="attention",
    )


def rows_norm(v):
    mean = jnp.mean(v, axis=-1, keepdims=True)
    centered = v - mean
    variance = jnp.mean(centered * centered, axis=-1, keepdims=True)
    scale = lax.rsqrt(variance + EPS)
    return centered * scale, scale


def attended_kernel(ctx, wo, tok, table, n1_o, r1_o, low_o):
    v = dot(ctx[...], wo[...]) + table[OUTPUT_B : OUTPUT_B + 1, :] + tok[...].astype(F32)
    n, r = rows_norm(v)
    n1_o[...] = n
    r1_o[...] = r
    low_o[...] = (n * table[GAIN1 : GAIN1 + 1, :] + table[SHIFT1 : SHIFT1 + 1, :]).astype(LOW)


def attended(ctx, wo, tokens, table):
    seq, width = tokens.shape
    blk = 256
    rows = pl.BlockSpec((blk, width), lambda i: (i, 0))
    return call(
        attended_kernel,
        (shape(seq, width, dtype=F32), shape(seq, 1, dtype=F32), shape(seq, width)),
        [rows, full((width, width)), rows, full((TABLE, width))],
        (rows, pl.BlockSpec((blk, 1), lambda i: (i, 0)), rows),
        (ctx, wo, tokens, table),
        grid=(seq // blk,),
        flops=2 * seq * width * width,
        moved=2 * width * width + 10 * seq * width,
        name="attended",
    )


ERFC_POLY = (
    0.14103029668331146,
    0.14146891236305237,
    0.1189674362540245,
    0.11450903862714767,
    -0.05439696088433266,
    0.22074179351329803,
    -0.34752535820007324,
    0.22408711910247803,
    -0.06580830365419388,
    0.006926023866981268,
)


def gelu_parts(v):
    t = 1.0 / (1.0 + (0.5 * 0.5**0.5) * jnp.abs(v))
    poly = ERFC_POLY[-1] * t + ERFC_POLY[-2]
    for coefficient in ERFC_POLY[-3::-1]:
        poly = poly * t + coefficient
    bell = jnp.exp2(v * v * (-0.5 * math.log2(math.e)))
    tail = t * poly * bell
    below = jnp.where(v < 0, tail, 1.0 - tail)
    return v * below, below + v * (bell * (2 * math.pi) ** -0.5)


def inner_kernel(low, wi, bi, act_o, slope_o):
    blk = 128
    for at in range(0, low.shape[0], blk):
        rows = slice(at, at + blk)
        act, slope = gelu_parts(dot(low[rows, :], wi[...]) + bi[...])
        act_o[rows, :] = act.astype(LOW)
        slope_o[rows, :] = slope.astype(LOW)


def inner(low, wi, bi):
    seq, width = low.shape
    ff = wi.shape[1]
    blk = 1024
    cols = pl.BlockSpec((seq, blk), lambda i: (0, i))
    return call(
        inner_kernel,
        (shape(seq, ff), shape(seq, ff)),
        [full((seq, width)), pl.BlockSpec((width, blk), lambda i: (0, i)), pl.BlockSpec((1, blk), lambda i: (0, i))],
        (cols, cols),
        (low, wi, bi),
        grid=(ff // blk,),
        flops=2 * seq * width * ff,
        moved=2 * width * ff + 4 * seq * ff,
        trans=2 * seq * ff,
        name="inner",
    )


def outer_kernel(labels, bias3, act, w, n1, table, out_grad, wp, hid_o, sg_o, bg_o, sums_o, head_o, loss_o, acc, n2_s, r2_s):
    step = pl.program_id(0)
    seq, width = n1.shape

    @pl.when(step == 0)
    def _():
        acc[...] = jnp.zeros_like(acc)

    acc[...] += dot(act[...], w[...])

    @pl.when(step == pl.num_programs(0) - 1)
    def _():
        def row(at):
            return table[at : at + 1, :]

        gain2, shift2 = row(GAIN2), row(SHIFT2)
        blk = 64
        for at in range(0, seq, blk):
            rows = slice(at, at + blk)
            v = acc[rows, :] + row(OUTER_B) + (n1[rows, :] * row(GAIN1) + row(SHIFT1))
            n, r = rows_norm(v)
            n2_s[rows, :] = n
            r2_s[rows, :] = r
            hid_o[rows, :] = (n * gain2 + shift2).astype(LOW)
        class_rows = hid_o[0:8, :]
        pooled_pre = dot(class_rows, wp[...])[0:1, :] + row(POOLER_B)
        bent = jnp.tanh(pooled_pre)
        pooled = bent.astype(LOW).astype(F32)
        logits = [
            jnp.sum(pooled * row(CLASS_W + j), axis=-1, keepdims=True) + bias3[j] for j in range(CLASSES)
        ]
        top = functools.reduce(jnp.maximum, logits)
        exps = [jnp.exp(v - top) for v in logits]
        total = functools.reduce(jnp.add, exps)
        label = labels[0]
        hot = [jnp.where(label == j, 1.0, 0.0) for j in range(CLASSES)]
        picked = functools.reduce(jnp.add, [a * b for a, b in zip(logits, hot)])
        loss_o[...] = jnp.broadcast_to(top + jnp.log(total) - picked, loss_o.shape)
        slopes = [(e / total - o).astype(LOW).astype(F32) for e, o in zip(exps, hot)]
        pooled_grad = functools.reduce(
            jnp.add, [g * row(CLASS_W + j) for j, g in enumerate(slopes)]
        )
        pre_grad = (pooled_grad * (1.0 - bent * bent)).astype(LOW)
        row_grad = dot_nt(jnp.broadcast_to(pre_grad, (8, width)), wp[...])[0:1, :]
        head_o[...] = jnp.zeros_like(head_o)
        lanes = lax.broadcasted_iota(jnp.int32, (1, width), 1)
        head_o[0:1, :] = class_rows[0:1, :].astype(F32)
        head_o[1:2, :] = pre_grad.astype(F32)
        head_o[2:3, :] = pooled
        head_o[3:4, :] = functools.reduce(
            jnp.add, [jnp.where(lanes == j, g, 0.0) for j, g in enumerate(slopes)]
        )
        gain_sum = jnp.zeros((1, width), F32)
        shift_sum = jnp.zeros((1, width), F32)
        bias_sum = jnp.zeros((1, width), F32)
        for at in range(0, seq, blk):
            rows = slice(at, at + blk)
            fg = out_grad[rows, :].astype(F32)
            if at == 0:
                lead = lax.broadcasted_iota(jnp.int32, (blk, width), 0) == 0
                fg = fg + jnp.where(lead, jnp.broadcast_to(row_grad, (blk, width)), 0.0)
            n = n2_s[rows, :]
            g = fg * gain2
            gm = jnp.mean(g, axis=-1, keepdims=True)
            gn = jnp.mean(g * n, axis=-1, keepdims=True)
            sg = r2_s[rows, :] * (g - gm - n * gn)
            low = sg.astype(LOW)
            sg_o[rows, :] = sg
            bg_o[rows, :] = low
            gain_sum += jnp.sum(fg * n, axis=0, keepdims=True)
            shift_sum += jnp.sum(fg, axis=0, keepdims=True)
            bias_sum += jnp.sum(low.astype(F32), axis=0, keepdims=True)
        sums_o[...] = jnp.zeros_like(sums_o)
        sums_o[0:1, :] = gain_sum
        sums_o[1:2, :] = shift_sum
        sums_o[2:3, :] = bias_sum


def outer(act, w, n1, table, out_grad, wp, labels, bias3):
    seq, width = n1.shape
    ff = act.shape[1]
    blk = 1536
    whole = full((seq, width))
    return call(
        outer_kernel,
        (
            shape(seq, width),
            shape(seq, width, dtype=F32),
            shape(seq, width),
            shape(8, width, dtype=F32),
            shape(8, width, dtype=F32),
            shape(8, 128, dtype=F32),
        ),
        [
            pl.BlockSpec((seq, blk), lambda i, *_: (0, i)),
            pl.BlockSpec((blk, width), lambda i, *_: (i, 0)),
            whole,
            full((TABLE, width)),
            whole,
            full((width, width)),
        ],
        (whole, whole, whole, full((8, width)), full((8, width)), full((8, 128))),
        (labels, bias3, act, w, n1, table, out_grad, wp),
        grid=(ff // blk,),
        scratch=[pltpu.VMEM((seq, width), F32), pltpu.VMEM((seq, width), F32), pltpu.VMEM((seq, 1), F32)],
        prefetch=2,
        flops=2 * seq * width * ff,
        moved=2 * width * ff + 2 * seq * ff + 14 * seq * width,
        name="outer",
    )


def inner_grad_kernel(bg, w_out, slope, ig_o):
    ig_o[...] = (dot_nt(bg[...], w_out[...]) * slope[...].astype(F32)).astype(LOW)


def inner_grads(bg, w_out, slope):
    seq, width = bg.shape
    ff = slope.shape[1]
    blk = 1024
    cols = pl.BlockSpec((seq, blk), lambda i: (0, i))
    return call(
        inner_grad_kernel,
        shape(seq, ff),
        [full((seq, width)), pl.BlockSpec((blk, width), lambda i: (i, 0)), cols],
        cols,
        (bg, w_out, slope),
        grid=(ff // blk,),
        flops=2 * seq * width * ff,
        moved=2 * width * ff + 4 * seq * ff,
        name="inner_grads",
    )


def inner_back_kernel(ig, w_in, sg, n1, r1, table, res_o, ag_o, sums_o, acc, ib):
    step = pl.program_id(0)
    seq, width = n1.shape
    blk = ig.shape[1]
    ib[:, pl.ds(pl.multiple_of(step * blk, blk), blk)] = jnp.sum(ig[...].astype(F32), axis=0, keepdims=True)

    @pl.when(step == 0)
    def _():
        acc[...] = jnp.zeros_like(acc)

    acc[...] += dot_nt(ig[...], w_in[...])

    @pl.when(step == pl.num_programs(0) - 1)
    def _():
        gain1 = table[GAIN1 : GAIN1 + 1, :]
        gain_sum = jnp.zeros((1, width), F32)
        shift_sum = jnp.zeros((1, width), F32)
        bias_sum = jnp.zeros((1, width), F32)
        blk = 64
        for at in range(0, seq, blk):
            rows = slice(at, at + blk)
            fg = sg[rows, :] + acc[rows, :]
            n = n1[rows, :]
            g = fg * gain1
            gm = jnp.mean(g, axis=-1, keepdims=True)
            gn = jnp.mean(g * n, axis=-1, keepdims=True)
            res = r1[rows, :] * (g - gm - n * gn)
            low = res.astype(LOW)
            res_o[rows, :] = res
            ag_o[rows, :] = low
            gain_sum += jnp.sum(fg * n, axis=0, keepdims=True)
            shift_sum += jnp.sum(fg, axis=0, keepdims=True)
            bias_sum += jnp.sum(low.astype(F32), axis=0, keepdims=True)
        sums_o[...] = jnp.zeros_like(sums_o)
        sums_o[0:1, :] = gain_sum
        sums_o[1:2, :] = shift_sum
        sums_o[2:3, :] = bias_sum
        for at in range(ib.shape[1] // width):
            sums_o[3 + at : 4 + at, :] = ib[:, at * width : (at + 1) * width]


def inner_back(ig, w_in, sg, n1, r1, table):
    seq, width = n1.shape
    ff = ig.shape[1]
    blk = 1536
    whole = full((seq, width))
    return call(
        inner_back_kernel,
        (shape(seq, width, dtype=F32), shape(seq, width), shape(8, width, dtype=F32)),
        [
            pl.BlockSpec((seq, blk), lambda i: (0, i)),
            pl.BlockSpec((width, blk), lambda i: (0, i)),
            whole,
            whole,
            full((seq, 1)),
            full((TABLE, width)),
        ],
        (whole, whole, full((8, width))),
        (ig, w_in, sg, n1, r1, table),
        grid=(ff // blk,),
        scratch=[pltpu.VMEM((seq, width), F32), pltpu.VMEM((1, ff), F32)],
        flops=2 * seq * width * ff,
        moved=2 * width * ff + 2 * seq * ff + 16 * seq * width,
        name="inner_back",
    )


def attention_back_kernel(q, k, v, lse, ag, wo, seg_row, seg_col, dq_o, dk_o, dv_o, sums_o, bias):
    seq = ag.shape[0]

    @pl.when(pl.program_id(0) == 0)
    def _():
        bias[...] = jnp.where(seg_col[...] == seg_row[...], 0.0, NEG)

    grad = dot_nt(ag[...], wo[...]).astype(LOW)
    first = lane_masks(seq)
    zero = jnp.zeros((seq, 128), LOW)
    sums_o[...] = jnp.zeros_like(sums_o)
    for pair in range(q.shape[1] // 128):
        cols = slice(pair * 128, pair * 128 + 128)
        q2, k2, v2, g2 = q[:, cols], k[:, cols], v[:, cols], grad[:, cols]
        k2t = k2.T
        dqs, dks, dvs = [], [], []
        for half in range(2):
            def own(a):
                return jnp.where(first, a, zero) if half == 0 else jnp.where(first, zero, a)

            row = pair * 2 + half
            s = dot_nt(k2, own(q2)) * SCALE + bias[...]
            p = jnp.exp(s - lse[0, row : row + 1, :])
            dp = dot_nt(v2, own(g2))
            weighted = p * dp
            level = jnp.sum(weighted, axis=0, keepdims=True)
            ds = (weighted - p * level).astype(LOW)
            dvs.append(dot(p.astype(LOW), g2))
            dks.append(dot(ds, q2))
            dqs.append(dot(k2t[half * HEAD_DIM : (half + 1) * HEAD_DIM], ds))
        dq = (jnp.concatenate(dqs, axis=0) * SCALE).astype(LOW).T
        dk = (jnp.where(first, dks[0], dks[1]) * SCALE).astype(LOW)
        dv = jnp.where(first, dvs[0], dvs[1]).astype(LOW)
        dq_o[:, cols] = dq
        dk_o[:, cols] = dk
        dv_o[:, cols] = dv
        sums_o[0:1, cols] = jnp.sum(dq.astype(F32), axis=0, keepdims=True)
        sums_o[1:2, cols] = jnp.sum(dv.astype(F32), axis=0, keepdims=True)


def attention_back(q, k, v, lse, ag, wo, segments, begin, count):
    seq, width = ag.shape
    blk = 256
    begin, steps = begin // blk, count // blk
    cols = pl.BlockSpec((seq, blk), lambda i: (0, i + begin))
    out = pl.BlockSpec((seq, blk), lambda i: (0, i))
    return call(
        attention_back_kernel,
        (shape(seq, count),) * 3 + (shape(8, count, dtype=F32),),
        [
            cols,
            cols,
            cols,
            pl.BlockSpec((1, 8, seq), lambda i: (i + begin, 0, 0)),
            full((seq, width)),
            pl.BlockSpec((blk, width), lambda i: (i + begin, 0)),
            full((1, seq)),
            full((seq, 1)),
        ],
        (out,) * 3 + (pl.BlockSpec((8, blk), lambda i: (0, i)),),
        (q, k, v, lse, ag, wo, segments.reshape(1, seq), segments.reshape(seq, 1)),
        grid=(steps,),
        scratch=[pltpu.VMEM((seq, seq), F32)],
        flops=2 * seq * count * (width + 5 * seq),
        moved=16 * seq * count + 2 * width * count,
        trans=seq * seq * count // HEAD_DIM,
        name="attention_back",
    )


def tokens_back_kernel(res, dq, dk, dv, wq, wk, wv, out):
    out[...] = res[...] + dot_nt(dq[...], wq[...]) + dot_nt(dk[...], wk[...]) + dot_nt(dv[...], wv[...])


def tokens_back(res, dq, dk, dv, wq, wk, wv):
    seq, width = res.shape
    blk = 128
    rows = pl.BlockSpec((blk, width), lambda i: (i, 0))
    weight = full((width, width))
    return call(
        tokens_back_kernel,
        shape(seq, width, dtype=F32),
        [rows] * 4 + [weight] * 3,
        rows,
        (res, dq, dk, dv, wq, wk, wv),
        grid=(seq // blk,),
        flops=6 * seq * width * width,
        moved=14 * seq * width + 6 * width * width,
        name="tokens_back",
    )


def grads(name, where, lefts, which, rights, add=None):
    features, seq = lefts[0].shape if add is not None else lefts[0].shape[::-1]
    parts = features // 16
    widths = tuple((w, r.shape[1] // 2) for w, r in zip(which, rights))
    total = sum(w for _, w in widths)
    half = (lambda i, where: (0, 1 - where[3])) if add is None else (lambda i, where: (0, where[3]))
    specs = [full(a.shape) for a in lefts]
    specs += [pl.BlockSpec((seq, w), half, pipeline_mode=pl.Buffered(1)) for _, w in widths]
    args = [where, *lefts, *rights]
    piece = (4, parts * total // COLUMNS, COLUMNS)
    outs = ((4, *piece),) + ((features, seq),) * len(lefts) if add is None else (piece,) * 4
    if add is not None:
        specs.append(full(add.shape))
        args.append(add)

    def kernel(where, *refs):
        left_refs, refs = refs[: len(lefts)], refs[len(lefts) :]
        right_refs, refs = refs[: len(rights)], refs[len(rights) :]
        x, y, z0 = where[0], where[1], where[2]
        if add is None:
            out_refs, turned = refs[:1], refs[1:]
            for left, store in zip(left_refs, turned):
                for start in range(0, features, 256):
                    store[start : start + 256, :] = left[:, start : start + 256].T
        else:
            add_ref, out_refs, turned = refs[0], refs[1:], left_refs
        for place in range(4):
            hh = jnp.bitwise_xor(x, place // 2)
            yy = jnp.bitwise_xor(y, place % 2)
            top = 0
            for (at, width), right in zip(widths, right_refs):
                rows = []
                for dz in range(4):
                    shard = jnp.bitwise_xor(z0, dz) * 2 + yy
                    rows.append(turned[at][pl.ds(pl.multiple_of((shard * 2 + hh) * parts, 16), parts), :])
                got = dot(jnp.concatenate(rows, axis=0), right[...]).reshape(4, parts, width)
                for column in range(0, width, COLUMNS):
                    one = got[:, :, column : column + COLUMNS]
                    if add is None:
                        out_refs[0][place, :, top : top + parts, :] = one.astype(LOW)
                    else:
                        one = one + add_ref[place, :, top : top + parts, :].astype(F32)
                        out_refs[place][:, top : top + parts, :] = one.astype(LOW)
                    top += parts

    got = call(
        kernel,
        tuple(shape(*o) for o in outs),
        specs,
        tuple(full(o) for o in outs),
        args,
        prefetch=1,
        flops=2 * seq * 16 * parts * total,
        moved=2 * 16 * parts * total + 2 * seq * 16 * parts,
        name=name,
    )
    return (got[0], list(got[1:])) if add is None else got


def pack_kernel(where, wq, wk, wv, wo, wi, wf, wp, small, own_a, own_b, own_c):
    for out, weights in ((own_a, (wq, wk, wv)), (own_b, (wo, wi))):
        left = 0
        for ref in weights:
            out[: ref.shape[0], left : left + ref.shape[1]] = ref[...]
            left += ref.shape[1]
    at = wq.shape[0]
    own_a[at:, :] = jnp.zeros((8, own_a.shape[1]), LOW)
    for top in range(0, small.shape[0], 8):
        own_a[at:, top * 16 : top * 16 + small.shape[1]] = small[top : top + 8, :]
    rows = wf.shape[0]
    own_c[:rows, :] = wf[...]
    own_c[rows:, :] = wp[...]


def pack(where, wq, wk, wv, wo, wi, wf, wp, small):
    rows, width = wq.shape
    deep = wf.shape[0] // 2
    ff = wi.shape[1]
    outs = (shape(rows // 2 + 8, 3 * width // 2), shape(rows // 2, (width + ff) // 2), shape(deep + rows // 2, width // 2))
    weights = (wq, wk, wv, wo, wi, wf, wp)
    quarters = [
        pl.BlockSpec((w.shape[0] // 2, w.shape[1] // 2), lambda i, where: (where[0], where[3])) for w in weights
    ]
    return call(
        pack_kernel,
        outs,
        quarters + [full(small.shape)],
        tuple(full(o.shape) for o in outs),
        (where, *(pltpu.with_memory_space_constraint(w, pltpu.HBM) for w in weights), small),
        prefetch=1,
        moved=4 * sum(math.prod(o.shape) for o in outs),
        vmem=8,
        name="pack",
    )


def weights_kernel(spans, places, where, *refs):
    pieces, outs, sem = refs[: len(places)], refs[-1 - len(spans) : -1], refs[-1]
    copies = []
    for place, piece in zip(places, pieces):
        hh = jnp.bitwise_xor(where[0], place // 4)
        yy = jnp.bitwise_xor(where[1], place // 2 % 2)
        cc = jnp.bitwise_xor(where[3], place % 2)
        for dz in range(4):
            zz = jnp.bitwise_xor(where[2], dz)
            for (top, rows, left, width), out in zip(spans, outs):
                to = out.at[zz, yy, hh, :, pl.ds(pl.multiple_of(cc * width, 128), width)]
                come = piece.at[dz, top : top + rows, left : left + width]
                copies.append(pltpu.make_async_copy(come, to, sem.at[len(copies)]))
    for one in copies:
        one.start()
    for one in copies:
        one.wait()


def place_some(where, pieces, spans, places, begun=()):
    anywhere = pl.BlockSpec(memory_space=pl.ANY)
    count = 1 + len(pieces)
    return pl.pallas_call(
        functools.partial(weights_kernel, tuple(spans), tuple(places)),
        name="place_weights",
        out_shape=tuple(shape(4, 2, 2, rows, 2 * width) for _, rows, _, width in spans),
        grid_spec=pltpu.PrefetchScalarGridSpec(
            num_scalar_prefetch=1,
            grid=(1,),
            in_specs=[anywhere] * (len(pieces) + len(begun)),
            out_specs=(anywhere,) * len(spans),
            scratch_shapes=[pltpu.SemaphoreType.DMA((4 * len(places) * len(spans),))],
        ),
        input_output_aliases={count + at: at for at in range(len(begun))},
        compiler_params=pltpu.CompilerParams(vmem_limit_bytes=4 * MIB),
        cost_estimate=pl.CostEstimate(flops=0, bytes_accessed=pieces[0].size, transcendentals=0),
    )(where, *pieces, *begun)


def place_weights(where, pieces, spans):
    begun = place_some(where, pieces[:6], spans, range(6))
    return finish_weights(where, begun, pieces[6:], spans)


def finish_weights(where, begun, pieces, spans):
    outs = place_some(where, pieces, spans, (6, 7), begun)
    return [o.reshape(16 * rows, 2 * width) for o, (_, rows, _, width) in zip(outs, spans)]


def shards_kernel(spans, where, *refs):
    pieces, outs = refs[:4], refs[4:]
    for place in range(4):
        hh = jnp.bitwise_xor(where[0], place // 2)
        for core in range(2):

            @pl.when(jnp.bitwise_xor(where[3], place % 2) == core)
            def _():
                for (top, rows, blocks), out in zip(spans, outs):
                    for block in range(blocks):
                        left = (core * blocks + block) * COLUMNS
                        out[hh, :, left : left + COLUMNS] = pieces[place][
                            top + block * rows : top + (block + 1) * rows, :
                        ].astype(F32)


def place_shards(where, pieces, spans):
    sizes = [(2, rows, 2 * blocks * COLUMNS) for _, rows, blocks in spans]
    outs = call(
        functools.partial(shards_kernel, tuple(spans)),
        tuple(shape(*size, dtype=F32) for size in sizes),
        [full(pieces[0].shape)] * 4,
        tuple(full(size) for size in sizes),
        (where, *pieces),
        prefetch=1,
        moved=24 * pieces[0].size,
        vmem=12,
        name="place_shards",
    )
    return [o.reshape(2 * size[1], size[2]) for o, size in zip(outs, sizes)]


def device(x, core, z, y):
    return (x * 2 + core) * 8 + z * 2 + y


ALL = [(x, core, z, y) for x in range(2) for core in range(2) for z in range(4) for y in range(2)]
CORE_SWAP = [(device(*a), device(a[0], 1 - a[1], a[2], a[3])) for a in ALL]
X_SWAP = [(device(*a), device(1 - a[0], a[1], a[2], a[3])) for a in ALL]
Y_SWAP = [(device(*a), device(a[0], a[1], a[2], 1 - a[3])) for a in ALL]
Z_SWAPS = [[(device(*a), device(a[0], a[1], a[2] ^ d, a[3])) for a in ALL] for d in range(4)]
X_CORE_SWAP = [(device(*a), device(1 - a[0], 1 - a[1], a[2], a[3])) for a in ALL]
XY_SWAP = [(device(*a), device(1 - a[0], a[1], a[2], 1 - a[3])) for a in ALL]


def swap(a, pairs):
    return lax.ppermute(a, MESH_AXES, pairs)


def wide(*arrays):
    return functools.reduce(jnp.add, [a.astype(F32) for a in arrays])


def along_z(own):
    return [swap(own, Z_SWAPS[d]) for d in (1, 2, 3)]


def to_core(arrays):
    return [swap(a, CORE_SWAP) for a in arrays]


def together(*groups):
    leaves, tree = jax.tree.flatten(groups)
    return jax.tree.unflatten(tree, lax.optimization_barrier(tuple(leaves)))


def low(a):
    return a.astype(LOW)


def sums_by_z(parts):
    return [wide(*(p[d] for p in parts)) for d in range(4)]


def on_device(
    by_links,
    tokens,
    out_grad,
    segment_ids,
    labels,
    query_weight,
    query_bias,
    key_weight,
    value_weight,
    value_bias,
    output_weight,
    output_bias,
    first_norm_gain,
    first_norm_shift,
    inner_weight,
    inner_bias,
    outer_weight,
    outer_bias,
    second_norm_gain,
    second_norm_shift,
    pooler_weight,
    pooler_bias,
    class_weight,
    class_bias,
):
    _, seq, width = tokens.shape
    tokens = tokens.reshape(seq, width)
    out_grad = out_grad.reshape(seq, width)
    dp, fsdp = lax.axis_index("dp"), lax.axis_index("fsdp")
    where = jnp.stack([dp // 2, fsdp % 2, fsdp // 2, dp % 2]).astype(jnp.int32)
    local = query_bias.shape[0]
    shards = width // local
    ff = inner_weight.shape[1]

    small = jnp.concatenate(
        [
            jnp.stack(
                [
                    query_bias,
                    value_bias,
                    output_bias,
                    first_norm_gain,
                    first_norm_shift,
                    outer_bias,
                    second_norm_gain,
                    second_norm_shift,
                    pooler_bias,
                ]
            ),
            inner_bias.reshape(ff // width, local),
            class_weight.T,
        ]
    )

    def tables(got):
        table = jnp.transpose(got, (1, 0, 2)).reshape(TABLE, width)
        return table, got[:, INNER_B:CLASS_W, :].reshape(1, ff)

    bias3 = class_bias.astype(F32)
    if by_links:
        own_a, own_b, own_c = pack(
            where,
            query_weight,
            key_weight,
            value_weight,
            output_weight,
            inner_weight,
            outer_weight,
            pooler_weight,
            small,
        )
        parts, deep = local // 2, outer_weight.shape[0] // 2
        spans_a = [(0, parts, at * (width // 2), width // 2) for at in range(3)]
        spans_b = [(0, parts, 0, width // 2), (0, parts, width // 2, ff // 2)]
        spans_c = [(0, deep, 0, width // 2), (deep, parts, 0, width // 2)]

        def mixed(near, other):
            return [a for pair in zip(near, other) for a in pair]

        z_a = along_z(own_a)
        (z_a, own_a, own_b, own_c) = together(z_a, own_a, own_b, own_c)
        z_b = along_z(own_b)
        far_a = jnp.stack([own_a, *z_a])
        x_a, y_a = swap(far_a, X_SWAP), swap(far_a, Y_SWAP)
        (far_a, x_a, y_a, z_b, own_b, own_c) = together(far_a, x_a, y_a, z_b, own_b, own_c)
        z_c = along_z(own_c)
        far_b = jnp.stack([own_b, *z_b])
        xy_a = swap(x_a, Y_SWAP)
        x_b = swap(far_b, X_SWAP)
        (core_a,) = to_core([jnp.concatenate([far_a, y_a, x_a])])
        order = [((where[2] ^ d) * 2 + (where[1] ^ e)) for e in range(2) for d in range(4)]
        spread = (jnp.stack(order)[None, :] == jnp.arange(shards)[:, None]).astype(LOW)
        small = jnp.concatenate([far_a[:, parts:, :256], y_a[:, parts:, :256]])
        small = jnp.concatenate([small[:, :, :local], small[:, :, 128 : 128 + local]], axis=1)
        table, inner_row = tables(jnp.einsum("sp,pji->sji", spread, small, preferred_element_type=F32))
        (far_a, y_a, x_a, xy_a, far_b, x_b, z_c, core_a, own_c, table, inner_row) = together(
            far_a, y_a, x_a, xy_a, far_b, x_b, z_c, core_a, own_c, table, inner_row
        )
        y_b = swap(far_b, Y_SWAP)
        far_c = jnp.stack([own_c, *z_c])
        x_c = swap(far_c, X_SWAP)
        core_a = [core_a[:4], core_a[4:8], core_a[8:]] + to_core([xy_a])
        wq, wk, wv = place_weights(where, mixed((far_a, y_a, x_a, xy_a), core_a), spans_a)
        q, k, v, context, lse = attention(tokens, wq, wk, wv, table, segment_ids)
        (q, k, v, context, lse, far_b, x_b, y_b, far_c, x_c) = together(
            q, k, v, context, lse, far_b, x_b, y_b, far_c, x_c
        )
        xy_b = swap(y_b, X_SWAP)
        y_c = swap(far_c, Y_SWAP)
        core_b = to_core([far_b, y_b, x_b])
        begun_b = place_some(where, mixed((far_b, y_b, x_b), core_b), spans_b, range(6))
        (xy_b, begun_b, far_c, x_c, y_c) = together(xy_b, begun_b, far_c, x_c, y_c)
        xy_c = swap(x_c, Y_SWAP)
        (core_xy_b,) = to_core([xy_b])
        core_c = to_core([far_c, y_c, x_c])
        wo, wi = finish_weights(where, begun_b, [xy_b, core_xy_b], spans_b)
        n1, r1, first_low = attended(context, wo, tokens, table)
        activated, slope = inner(first_low, wi, inner_row)
        (core_c, activated, slope) = together(core_c, activated, slope)
        begun_c = place_some(where, mixed((far_c, y_c, x_c), core_c), spans_c, range(6))
        (xy_c, begun_c, activated, slope) = together(xy_c, begun_c, activated, slope)
        wf, wp = finish_weights(where, begun_c, [xy_c, *to_core([xy_c])], spans_c)
    else:
        wq, wk, wv, wo, wp, wi, wf = (
            lax.all_gather(w, "fsdp", axis=0, tiled=True)
            for w in (
                query_weight,
                key_weight,
                value_weight,
                output_weight,
                pooler_weight,
                inner_weight,
                outer_weight,
            )
        )
        table, inner_row = tables(lax.all_gather(small, "fsdp").astype(F32))
        q, k, v, context, lse = attention(tokens, wq, wk, wv, table, segment_ids)
        n1, r1, first_low = attended(context, wo, tokens, table)
        activated, slope = inner(first_low, wi, inner_row)

    hidden, second_grad, branch_grad, sums2, head, loss = outer(
        activated, wf, n1, table, out_grad, wp, labels, bias3
    )
    def attention_step(attended_grad, begin, count):
        return attention_back(q, k, v, lse, attended_grad, wo, segment_ids, begin, count)

    cut = 512
    if by_links:

        def gathered(heads, pairs):
            return jnp.concatenate([heads, swap(heads, pairs)])

        heads = low(head)[None]

        def plane(parts):
            same, y, x, xy = parts
            return [same, swap(x, X_SWAP), swap(y, Y_SWAP), swap(xy, XY_SWAP)]

        other, lefts = grads("outer_grad_a", where, [activated], [0], [branch_grad])
        (other, branch_grad) = together(other, branch_grad)
        other, heads = swap(other, CORE_SWAP), gathered(heads, Z_SWAPS[1])
        inner_grad = inner_grads(branch_grad, wf, slope)
        (other, inner_grad, heads) = together(other, inner_grad, heads)
        mine = grads("outer_grad_b", where, lefts, [0], [branch_grad], other)
        (mine, inner_grad, heads) = together(mine, inner_grad, heads)
        same_f, y_f, x_f, xy_f = mine
        from_x, from_y = swap(x_f[:3], X_SWAP), swap(y_f[:3], Y_SWAP)
        heads = gathered(gathered(heads, Z_SWAPS[2]), Y_SWAP)
        residual_grad, attended_grad, sums1 = inner_back(inner_grad, wi, second_grad, n1, r1, table)
        (attended_grad, inner_grad) = together(attended_grad, inner_grad)
        lefts, rights = [context, first_low], [attended_grad, inner_grad]
        other, lefts = grads("inner_grad_a", where, lefts, [0, 1], rights)
        (other, attended_grad, from_x, from_y, x_f, y_f, xy_f, heads) = together(
            other, attended_grad, from_x, from_y, x_f[3], y_f[3], xy_f, heads
        )
        other = swap(other, CORE_SWAP)
        x_f, y_f, xy_f = swap(x_f, X_SWAP), swap(y_f, Y_SWAP), swap(xy_f, XY_SWAP)
        heads = gathered(heads, X_SWAP)
        back_a = attention_step(attended_grad, 0, cut)
        (other, back_a, attended_grad, heads) = together(other, back_a, attended_grad, heads)
        mine = grads("inner_grad_b", where, lefts, [0, 1], rights, other)
        (mine, attended_grad, heads) = together(mine, attended_grad, heads)
        heads = gathered(heads, CORE_SWAP)
        back_b = attention_step(attended_grad, cut, width - cut)
        dq, dk, dv, sums0 = (jnp.concatenate([a, b], axis=1) for a, b in zip(back_a, back_b))
        rights = [dq, dk, dv]
        other, lefts = grads("query_grad_a", where, [tokens], [0, 0, 0], rights)
        sums = jnp.stack([sums2, sums1, sums0])
        (other, dq, dk, dv, sums, x_f, y_f, xy_f, mine, heads) = together(
            other, dq, dk, dv, sums, x_f, y_f, xy_f, mine, heads
        )
        rights = [dq, dk, dv]
        parts_i = plane(mine)
        other = swap(other, CORE_SWAP)
        totals_f = [wide(same_f[d], xy_f[d], from_x[d], from_y[d]) for d in range(3)]
        totals_f.append(wide(same_f[3], xy_f[3], x_f, y_f))
        odd_f = swap(low(jnp.stack([totals_f[1], totals_f[3]])), Z_SWAPS[1])
        mine = grads("query_grad_b", where, lefts, [0, 0, 0], rights, other)
        (mine, odd_f, even_f, dq, dk, dv, sums, heads) = together(
            mine, odd_f, [totals_f[0], totals_f[2]], dq, dk, dv, sums, heads
        )
        go_f = swap(low(wide(even_f[1], odd_f[1])), Z_SWAPS[2])
        sums = sums + swap(sums, Z_SWAPS[1])
        tokens_grad = tokens_back(residual_grad, dq, dk, dv, wq, wk, wv)
        (parts_i, mine, go_f, stay_f, tokens_grad, heads, sums) = together(
            parts_i, mine, go_f, wide(even_f[0], odd_f[0]), tokens_grad, heads, sums
        )
        parts_q = plane(mine)
        totals_i = sums_by_z(parts_i)
        odd_i = swap(low(jnp.stack([totals_i[1], totals_i[3]])), Z_SWAPS[1])
        own_f = low(wide(stay_f, go_f))
        sums = sums + swap(sums, Z_SWAPS[2])
        (odd_i, even_i, own_f, sums, heads) = together(odd_i, [totals_i[0], totals_i[2]], own_f, sums, heads)
        go_i = swap(low(wide(even_i[1], odd_i[1])), Z_SWAPS[2])
        sums = sums + swap(sums, X_SWAP)
        (parts_q, go_i, stay_i, own_f, sums, heads) = together(
            parts_q, go_i, wide(even_i[0], odd_i[0]), own_f, sums, heads
        )
        totals_q = sums_by_z(parts_q)
        z_q = [swap(low(totals_q[d]), Z_SWAPS[d]) for d in (1, 2, 3)]
        own = jnp.concatenate([own_f, low(wide(stay_i, go_i))])
        across = swap(own, X_SWAP)
        sums = sums + swap(sums, Y_SWAP)
        (z_q, own_q, own, across, sums, heads) = together(z_q, totals_q[0], own, across, sums, heads)
        sums = sums + swap(sums, CORE_SWAP)
        core = swap(jnp.stack([own, across]), CORE_SWAP)
        own_q = low(wide(own_q, *z_q))
        all_q = [own_q, swap(own_q, CORE_SWAP), swap(own_q, X_SWAP), swap(own_q, X_CORE_SWAP)]
        outer_grad, output_grad, inner_weight_grad = place_shards(
            where,
            [own, core[0], across, core[1]],
            [(0, deep, 1), (deep, parts, 1), (deep + parts, parts, ff // width)],
        )
        query_grad, key_grad, value_grad = place_shards(where, all_q, [(at * parts, parts, 1) for at in range(3)])
    else:

        def reduced(left, right):
            local_grad = lax.dot_general(left, right, (((0,), (0,)), ((), ())), preferred_element_type=F32)
            shard = lax.psum_scatter(local_grad, "fsdp", scatter_dimension=0, tiled=True)
            return lax.psum(low(shard), "dp").astype(F32)

        inner_grad = inner_grads(branch_grad, wf, slope)
        residual_grad, attended_grad, sums1 = inner_back(inner_grad, wi, second_grad, n1, r1, table)
        dq, dk, dv, sums0 = attention_step(attended_grad, 0, width)
        outer_grad = reduced(activated, branch_grad)
        inner_weight_grad = reduced(first_low, inner_grad)
        output_grad = reduced(context, attended_grad)
        query_grad, key_grad, value_grad = (reduced(tokens, d) for d in (dq, dk, dv))
        tokens_grad = tokens_back(residual_grad, dq, dk, dv, wq, wk, wv)
        sums = lax.psum(jnp.stack([sums2, sums1, sums0]), MESH_AXES)
        heads = lax.all_gather(head, MESH_AXES)

    vectors = lax.dynamic_slice(sums, (0, 0, fsdp * local), (3, 8, local))
    inner_bias_grad = lax.dynamic_slice(
        sums[1, 3 : 3 + ff // width].reshape(ff), (fsdp * (ff // shards),), (ff // shards,)
    )
    class_rows, pre_grads, pooled = heads[:, 0], heads[:, 1], heads[:, 2]
    logit_grads = heads[:, 3, :CLASSES]

    def own_columns(a):
        return lax.dynamic_slice(a, (0, fsdp * local), (a.shape[0], local))

    def over_rows(a, b):
        return lax.dot_general(a, b, (((0,), (0,)), ((), ())), preferred_element_type=F32)

    pooler_grad = over_rows(own_columns(class_rows), pre_grads)
    pooler_bias_grad = jnp.sum(own_columns(pre_grads).astype(F32), axis=0)
    class_grad = over_rows(own_columns(pooled), logit_grads)
    class_bias_grad = jnp.sum(logit_grads.astype(F32), axis=0)

    return (
        hidden[None],
        tokens_grad[None],
        loss[0, :1],
        query_grad,
        vectors[2, 0],
        key_grad,
        value_grad,
        vectors[2, 1],
        output_grad,
        vectors[1, 2],
        vectors[1, 0],
        vectors[1, 1],
        inner_weight_grad,
        inner_bias_grad,
        outer_grad,
        vectors[0, 2],
        vectors[0, 0],
        vectors[0, 1],
        pooler_grad,
        pooler_bias_grad,
        class_grad,
        class_bias_grad,
    )


def solution(mesh):
    sizes = dict(mesh.shape)
    by_links = sizes == {"dp": 4, "fsdp": 8}
    rows = P(MESH_AXES, None, None)
    ids = P(MESH_AXES, None)
    row = P(MESH_AXES)
    matrix = P("fsdp", None)
    vector = P("fsdp")
    return jax.shard_map(
        functools.partial(on_device, by_links),
        mesh=mesh,
        in_specs=(
            rows, rows, ids, row,
            matrix, vector, matrix, matrix, vector, matrix, vector, vector, vector,
            matrix, vector, matrix, vector, vector, vector, matrix, vector, matrix, P(),
        ),
        out_specs=(
            rows, rows, row,
            matrix, vector, matrix, matrix, vector, matrix, vector, vector, vector,
            matrix, vector, matrix, vector, vector, vector, matrix, vector, matrix, P(),
        ),
        check_vma=False,
    )
```
